32 devices in a mesh: win: 2 (over y), vel: 8 (over z, x), sp: 2 (over core).
Axes of the slice: x: 2, y: 2, z: 4, core: 2. Of those that a mesh axis runs over, the one named last changes fastest.
Arguments:
- f_start: float32 [2, 1536, 64, 128], P('win', 'vel', 'sp'), may hold values from 0 to 15, as said below
- relax_rate: float32 [64, 128], P('sp'), may hold values from 0.1 to 10
Outputs:
- corrected: float32 [2, 4, 64, 128], P('win', None, 'sp')
- lifted: float32 [2, 1536, 64, 128], P('win', 'vel', 'sp')
The draws below stay inside these ranges and needn't reach their ends.
Inputs may be any that keep to these rules, and one draw needn't show every extreme that they name: `f_start`: no entry is negative.
All inputs are finite; a program needn't handle non-finite values.
Results may differ from the reference program's by a relative error of at most 0.00021.
Values sent between devices are 32-bit elements; how exact they have to be, the bound alone decides.
A program may use at most 64 MiB of HBM per device.

```python
import math
import jax
import jax.numpy as jnp
from jax import lax

NVX = 48
NVY = 32
NX = 64
NY = 128
NV = 1536
WINDOWS = 2


def draw_f_start(key, part):
    random_seeds = jax.random.split(key, 5)
    grid_volume = (WINDOWS, 1, NX, NY)
    mass_per_volume = jnp.exp(jax.random.uniform(random_seeds[0], grid_volume, jnp.float32, math.log(0.2), math.log(2.0)))
    pointwise_thermal_level = jnp.exp(jax.random.uniform(random_seeds[1], grid_volume, jnp.float32, math.log(0.2), math.log(1.5)))
    horizontal_flow = jax.random.uniform(random_seeds[2], grid_volume, jnp.float32, -0.5, 0.5)
    upward_flow = jax.random.uniform(random_seeds[3], grid_volume, jnp.float32, -0.5, 0.5)
    full = (WINDOWS, NV, NX, NY)
    noise = jnp.clip(0.15 * jax.random.normal(random_seeds[4], full, jnp.float32), -0.45, 0.45)
    index = jnp.arange(NV, dtype=jnp.int32)
    vel_x = -6.0 + ((index // NVY).astype(jnp.float32) + 0.5) * (12.0 / NVX)
    vel_y = -6.0 + ((index % NVY).astype(jnp.float32) + 0.5) * (12.0 / NVY)
    horizontal_gradient = vel_x[None, :, None, None] - horizontal_flow
    upward_gradient = vel_y[None, :, None, None] - upward_flow
    gaussian_profile = mass_per_volume / pointwise_thermal_level * jnp.exp(-(horizontal_gradient * horizontal_gradient + upward_gradient * upward_gradient) / (2.0 * pointwise_thermal_level))
    return (gaussian_profile * (1.0 + noise)).astype(jnp.float32)


def block_levels(key, extent, cuts, low, top_value):
    loudness, own = 1.0, jax.random.fold_in(key, 6)
    for axis_at, shards_of in cuts:
        heights = jnp.exp(jax.random.uniform(jax.random.fold_in(own, axis_at), (shards_of,), jnp.float32, low / len(cuts), top_value / len(cuts)))
        loudness = loudness * jnp.repeat(heights, extent[axis_at] // shards_of).reshape([-1 if axis == axis_at else 1 for axis in range(len(extent))])
    return loudness


def setup_inputs(seed: int = 0) -> dict:
    keys = jax.random.split(jax.random.key(seed), 3)
    f_start = draw_f_start(jax.random.fold_in(keys[2], 71), 0)
    relax_rate = jnp.clip(jnp.exp(math.log(10.0) - 4.6051702 * jax.random.uniform(keys[1], (NX, NY), jnp.float32) ** block_levels(keys[1], (NX, NY), ((0, 2),), -0.2, 0.2)), 0.1, 10.0)
    return dict(f_start=f_start, relax_rate=relax_rate)


vel_max = 6.0
fine_ratio = 0.075
coarse_ratio = 0.15
density_floor = 0.3
thermal_lower_bound = 0.3

def velocity_table(first, count):
    index = first + jnp.arange(count, dtype=jnp.int32)
    vel_x = -vel_max + ((index // NVY).astype(jnp.float32) + 0.5) * (2.0 * vel_max / NVX)
    vel_y = -vel_max + ((index % NVY).astype(jnp.float32) + 0.5) * (2.0 * vel_max / NVY)
    return (vel_x, vel_y)

def moment_table(vel_x, vel_y):
    weight_unit = 2.0 * vel_max / NVX * (2.0 * vel_max / NVY) / (2.0 * math.pi)
    return jnp.stack([jnp.ones_like(vel_x), vel_x, vel_y, 0.5 * (vel_x * vel_x + vel_y * vel_y)]) * weight_unit

def moments(field, table):
    flat = field.reshape(field.shape[0], -1)
    out = jnp.dot(table, flat, precision=lax.Precision.HIGHEST, preferred_element_type=jnp.float32)
    return out.reshape(4, field.shape[1], field.shape[2])

def physical_variables(distribution_array):
    mass_per_volume = jnp.maximum(distribution_array[0], density_floor)
    horizontal_flow = distribution_array[1] / mass_per_volume
    upward_flow = distribution_array[2] / mass_per_volume
    inner_volumes = (distribution_array[3] - 0.5 * (distribution_array[1] * horizontal_flow + distribution_array[2] * upward_flow)) / mass_per_volume
    pointwise_thermal_level = jnp.maximum(inner_volumes, thermal_lower_bound)
    return (mass_per_volume, horizontal_flow, upward_flow, pointwise_thermal_level)

def equilibrium_density(distribution_array, vel_x, vel_y):
    mass_per_volume, horizontal_flow, upward_flow, pointwise_thermal_level = physical_variables(distribution_array)
    horizontal_gradient = vel_x[:, None, None] - horizontal_flow[None]
    upward_gradient = vel_y[:, None, None] - upward_flow[None]
    return (mass_per_volume / pointwise_thermal_level)[None] * jnp.exp(-(horizontal_gradient * horizontal_gradient + upward_gradient * upward_gradient) / (2.0 * pointwise_thermal_level[None]))

def transport(field, left, right, vel_x, vel_y):
    coef_x = (vel_x * fine_ratio)[:, None, None]
    coef_y = (vel_y * fine_ratio)[:, None, None]
    below = jnp.roll(field, 1, axis=2)
    above = jnp.roll(field, -1, axis=2)
    out = field - jnp.maximum(coef_x, 0.0) * (field - left) - jnp.minimum(coef_x, 0.0) * (right - field)
    return out - jnp.maximum(coef_y, 0.0) * (field - below) - jnp.minimum(coef_y, 0.0) * (above - field)

def euler_update(padded_array):
    mass_per_volume, horizontal_flow, upward_flow, pointwise_thermal_level = physical_variables(padded_array)
    normal_stress = mass_per_volume * pointwise_thermal_level
    acoustic_wave_rate = jnp.sqrt(2.0 * pointwise_thermal_level)
    flux_x = jnp.stack([padded_array[1], padded_array[1] * horizontal_flow + normal_stress, padded_array[2] * horizontal_flow, (padded_array[3] + normal_stress) * horizontal_flow])
    flux_y = jnp.stack([padded_array[2], padded_array[1] * upward_flow, padded_array[2] * upward_flow + normal_stress, (padded_array[3] + normal_stress) * upward_flow])
    reach_x = jnp.abs(horizontal_flow) + acoustic_wave_rate
    reach_y = jnp.abs(upward_flow) + acoustic_wave_rate
    face_x = 0.5 * (flux_x[:, :-1, 1:-1] + flux_x[:, 1:, 1:-1]) - 0.5 * jnp.maximum(reach_x[:-1, 1:-1], reach_x[1:, 1:-1])[None] * (padded_array[:, 1:, 1:-1] - padded_array[:, :-1, 1:-1])
    face_y = 0.5 * (flux_y[:, 1:-1, :-1] + flux_y[:, 1:-1, 1:]) - 0.5 * jnp.maximum(reach_y[1:-1, :-1], reach_y[1:-1, 1:])[None] * (padded_array[:, 1:-1, 1:] - padded_array[:, 1:-1, :-1])
    return padded_array[:, 1:-1, 1:-1] - coarse_ratio * (face_x[:, 1:] - face_x[:, :-1] + (face_y[:, :, 1:] - face_y[:, :, :-1]))

def coarse(distribution_array):
    return euler_update(jnp.pad(distribution_array, ((0, 0), (1, 1), (1, 1)), mode='wrap'))

def fine(field, rates, vel_x, vel_y, table):
    start = moments(field, table)
    current = field
    for step in range(2):
        star = transport(current, jnp.roll(current, 1, axis=1), jnp.roll(current, -1, axis=1), vel_x, vel_y)
        distribution_array = moments(star, table)
        current = (star + rates[None] * equilibrium_density(distribution_array, vel_x, vel_y)) / (1.0 + rates[None])
    return (start, distribution_array, current)

def reference(f_start, relax_rate):
    vel_x, vel_y = velocity_table(0, NV)
    table = moment_table(vel_x, vel_y)

    def first_pass(field):
        start, ending, unused = fine(field, relax_rate, vel_x, vel_y, table)
        return (start, ending)
    starts, endings = lax.map(first_pass, f_start)
    delta = endings - lax.map(coarse, starts)
    distribution_array = starts[0]
    outs = []
    for time_window in range(WINDOWS):
        distribution_array = coarse(distribution_array) + delta[time_window]
        outs.append(distribution_array)
    corrected = jnp.stack(outs)

    def lift(items):
        field, target, ending = items
        unused_a, unused_b, current = fine(field, relax_rate, vel_x, vel_y, table)
        return current + equilibrium_density(target, vel_x, vel_y) - equilibrium_density(ending, vel_x, vel_y)
    lifted = lax.map(lift, (f_start, corrected, endings))
    return (corrected, lifted)
```

```python
import functools
import math

import jax
import jax.numpy as jnp
from jax import lax
from jax.experimental import pallas as pl
from jax.experimental.pallas import tpu as pltpu
from jax.sharding import PartitionSpec as P

NVX = 48
NVY = 32
HALF = NVY // 2
TILE = 8
vel_max = 6.0
fine_ratio = 0.075
coarse_ratio = 0.15
density_floor = 0.3
thermal_lower_bound = 0.3
DVX = 2.0 * vel_max / NVX
DVY = 2.0 * vel_max / NVY
WEIGHT = DVX * DVY / (2.0 * math.pi)
MESH = pl.DeviceIdType.MESH
f32 = jnp.float32
ORDERS = [(p, q) for p in range(5) for q in range(5 - p)]
PLACE = {order: n for n, order in enumerate(ORDERS)}
MAIN = [(0, 0), (0, 1), (1, 0), (0, 2), (2, 0)]
FIRST, START, SECOND = range(3)


def physical_variables(u):
    rs = jnp.maximum(u[0], density_floor)
    ux = u[1] / rs
    uy = u[2] / rs
    temp = jnp.maximum((u[3] - 0.5 * (u[1] * ux + u[2] * uy)) / rs, thermal_lower_bound)
    return rs, ux, uy, temp


def chunk_of(first, c):
    k = first + c * HALF
    i = k // NVY
    j = k % NVY
    vx = -vel_max + (i.astype(f32) + 0.5) * DVX
    vy = -vel_max + (j.astype(f32) + 0.5) * DVY
    return vx, vy, j // HALF, j


def coarse(u, band):
    rows, ny = u[0].shape
    rs, ux, uy, temp = physical_variables(u)
    p = rs * temp
    wave = jnp.sqrt(2.0 * temp)
    fx = [u[1], u[1] * ux + p, u[2] * ux, (u[3] + p) * ux]
    fy = [u[2], u[1] * uy, u[2] * uy + p, (u[3] + p) * uy]
    sx = jnp.abs(ux) + wave
    sy = jnp.abs(uy) + wave
    mx = jnp.maximum(sx, pltpu.roll(sx, rows - 1, 0))
    my = jnp.maximum(sy, pltpu.roll(sy, ny - 1, 1))
    out = []
    for c in range(4):
        face_x = 0.5 * (fx[c] + pltpu.roll(fx[c], rows - 1, 0)) - 0.5 * mx * (
            pltpu.roll(u[c], rows - 1, 0) - u[c]
        )
        face_y = 0.5 * (fy[c] + pltpu.roll(fy[c], ny - 1, 1)) - 0.5 * my * (
            pltpu.roll(u[c], ny - 1, 1) - u[c]
        )
        g = u[c] - coarse_ratio * (
            face_x - pltpu.roll(face_x, 1, 0) + (face_y - pltpu.roll(face_y, 1, 1))
        )
        out.append(g[:band])
    return out


def advance_kernel(
    nw, nv,
    f, r, star2, ye, e_phys, corr_out,
    fpad, spad, rfull, bsum, hsum, gout, msg, xmsg, red, redx, xs, es, fr, flux, energy, delta, gs,
    pmsg, pin, vmsg, vrow, vin, vrow_in, phys, xpad, yt, yr,
    load_sem, halo_send, halo_recv, rs_send, rs_recv, ag_send, ag_recv, win_send, win_recv,
):
    w, v, s = lax.axis_index("win"), lax.axis_index("vel"), lax.axis_index("sp")
    count, nx, ny = f.shape
    chunks = count // HALF
    first = v * count
    other = 1 - s
    pos = (2 * v) // nv
    band = nx // 2
    frame = band + TILE
    full = 4 * band
    main = pl.ds(2 * TILE, nx)
    end = 2 * TILE + nx
    up = pl.ds(2 * TILE + 1 - 2 * pos, nx)
    hb = pl.multiple_of(end - (end - TILE) * pos, TILE)
    edge = pl.ds(hb, TILE)
    edge_up = pl.ds(hb + 1 - 2 * pos, TILE)
    ho = pl.multiple_of(TILE + (end - TILE) * pos, TILE)
    away = pl.ds(ho, TILE)
    away_up = pl.ds(ho + 1 - 2 * pos, TILE)
    tiles = nx // TILE

    base = nv // 2 - 2
    off = v - base
    is_owner = (s == 1) & (off >= 0) & (off < 4)
    b = off // 2
    h = (off + b) % 2
    g = 2 * h + b

    def owner_at(half, k):
        return base + (half if k == 0 else 3 - half)

    def load_f(t):
        rows = pl.ds(pl.multiple_of(t * TILE, TILE), TILE)
        padded = pl.ds(pl.multiple_of((t + 2) * TILE, TILE), TILE)
        return pltpu.make_async_copy(f.at[:, rows], fpad.at[:, padded], load_sem.at[t])

    for t in range(tiles):
        load_f(t).start()
    mine = pl.ds(pl.multiple_of(s * nx, TILE), nx)
    load_r = pltpu.make_async_copy(r, rfull.at[mine], load_sem.at[tiles])
    load_r.start()

    def signal(device):
        pl.semaphore_signal(barrier, inc=1, device_id=device, device_id_type=MESH)

    barrier = pltpu.get_barrier_semaphore()
    signal((w, v, other))
    for o in range(4):

        @pl.when(jnp.logical_not((v == base + o) & (s == 1)))
        def _():
            signal((w, base + o, 1))

    @pl.when(is_owner)
    def _():
        signal((w, v, 0))
        for d in range(1, nv):
            for half in range(2):
                signal((w, lax.rem(v + d, nv), half))

        @pl.when(w + 1 < nw)
        def _():
            for o in range(4):
                signal((w + 1, base + o, 1))

        @pl.when(w > 0)
        def _():
            for o in range(4):
                signal((w - 1, base + o, 1))

    def remote(src, dst, send, recv, device):
        return pltpu.make_async_remote_copy(
            src_ref=src, dst_ref=dst, send_sem=send, recv_sem=recv,
            device_id=device, device_id_type=MESH,
        )

    def settle(ref, sem):
        pltpu.make_async_copy(ref, ref, sem).wait()

    empty = jnp.zeros((TILE, ny), f32)
    for side in range(2):
        for n in range(len(ORDERS)):
            for at in (TILE, end):
                bsum[side, n, pl.ds(at, TILE)] = empty
                hsum[side, n, pl.ds(at, TILE)] = empty

    parity = (first // HALF) % 2
    rounds = (chunks + 1) // 2

    @pl.loop(0, tiles)
    def _(t):
        load_f(t).wait()
        rows = pl.ds(pl.multiple_of(2 * TILE + t * TILE, TILE), TILE)
        for side in range(2):
            acc = {order: jnp.zeros((TILE, ny), f32) for order in ORDERS}
            for n in range(rounds):
                c = (side + parity) % 2 + 2 * n
                weight = 1.0
                if chunks % 2:
                    weight = jnp.where(c < chunks, 1.0, 0.0).astype(f32)
                    c = jnp.minimum(c, chunks - 1)
                vx = chunk_of(first, c)[0]
                sums = [jnp.zeros((TILE, ny), f32)] * 5
                for jj in range(HALF // 2, HALF):
                    tt = (jj + 0.5) * DVY - 0.5 * vel_max
                    high = fpad[c * HALF + jj, rows]
                    low = fpad[c * HALF + HALF - 1 - jj, rows]
                    even, odd = high + low, high - low
                    sums = [
                        sums[0] + even, sums[1] + tt * odd, sums[2] + tt**2 * even,
                        sums[3] + tt**3 * odd, sums[4] + tt**4 * even,
                    ]
                power = weight
                for q in range(5):
                    for m in range(5 - q):
                        term = sums[m] if q == 0 and chunks % 2 == 0 else sums[m] * power
                        acc[m, q] = acc[m, q] + term
                    power = power * vx
            centre = (side - 0.5) * vel_max
            for p, q in ORDERS:
                total = acc[p, q]
                for m in range(p):
                    total = total + (math.comb(p, m) * centre ** (p - m)) * acc[m, q]
                bsum[side, PLACE[p, q], rows] = total

    def components(get):
        return [
            WEIGHT * get(0, 0), WEIGHT * get(0, 1), WEIGHT * get(1, 0),
            (0.5 * WEIGHT) * (get(0, 2) + get(2, 0)),
        ]

    def fill(field, values):
        for c in range(4):
            for k in range(2):
                msg[field, k, pl.ds(c * band, band)] = values[c][k * band : (k + 1) * band]

    def fill_edges(field):
        for c in range(4):
            for k in range(2):
                if field == FIRST:
                    outer = gout[0, c, pl.ds(TILE - 1 if k == 0 else 0, 1)]
                else:
                    outer = jnp.zeros((1, ny), f32)
                msg[field, k, pl.ds(full + c, 1)] = outer
                inner = c * band if k == 0 else (c + 1) * band - 1
                msg[field, k, pl.ds(full + 4 + c, 1)] = msg[field, 1 - k, pl.ds(inner, 1)]

    def to_owner(half, k):
        target = owner_at(half, k)
        return target, (v == target) & (s == 1)

    sizes = {FIRST: full + TILE, START: full + TILE, SECOND: full}

    def scatter(field):
        size = pl.ds(0, sizes[field])
        for k in range(2):
            target, own = to_owner(s, k)

            @pl.when(own)
            def _():
                red[field, v, size] = msg[field, k, size]

            @pl.when(jnp.logical_not(own))
            def _():
                remote(
                    msg.at[field, k, size], red.at[field, v, size],
                    rs_send.at[field], rs_recv.at[field], (w, target, 1),
                ).start()

    def scatter_across():
        for k in range(2):
            target, own = to_owner(other, k)

            @pl.when(own)
            def _():
                redx[v] = xmsg[k]

            @pl.when(jnp.logical_not(own))
            def _():
                remote(xmsg.at[k], redx.at[v], rs_send.at[3], rs_recv.at[3], (w, target, 1)).start()

    fill(START, components(lambda p, q: bsum[0, PLACE[p, q], main] + bsum[1, PLACE[p, q], main]))
    fill_edges(START)

    neighbours = jnp.where(w > 0, 4, 0) + jnp.where(w + 1 < nw, 4, 0)
    pl.semaphore_wait(barrier, jnp.where(is_owner, 2 * nv + 3 + neighbours, 5))
    load_r.wait()
    source = pl.ds(pl.multiple_of((nx - TILE) * pos, TILE), TILE)
    halo_r = remote(r, rfull.at[mine], halo_send.at[0], halo_recv.at[0], (w, v, other))
    halo_f = remote(f.at[:, source], fpad.at[:, edge], halo_send.at[1], halo_recv.at[1], (w, v, other))
    halo_r.start()
    halo_f.start()

    inv_main = 1.0 / (1.0 + rfull[mine])
    along = fine_ratio * (2 * pos - 1).astype(f32)
    ACROSS = ((-fine_ratio, ny - 1), (fine_ratio, 1))

    def moved(table, side, p, q, rows, rows_up):
        across, shift = ACROSS[side]
        bx = table[side, PLACE[p, q + 1], rows]
        by = table[side, PLACE[p + 1, q], rows]
        return (
            table[side, PLACE[p, q], rows]
            + along * (table[side, PLACE[p, q + 1], rows_up] - bx)
            + across * (pltpu.roll(by, shift, 1) - by)
        )

    star_main, star_away = {}, {}
    for side in range(2):
        for p, q in ORDERS:
            if p + q < 4:
                star = moved(bsum, side, p, q, main, up)
                beyond = moved(bsum, side, p, q, away, away_up)
                if (p, q) in MAIN:
                    star_main[p, q] = star + star_main[p, q] if side else star
                    star_away[p, q] = beyond + star_away[p, q] if side else beyond
                hsum[side, PLACE[p, q], main] = star * inv_main
                hsum[side, PLACE[p, q], away] = beyond
    fill(FIRST, components(lambda p, q: star_main[p, q]))
    for c, value in enumerate(components(lambda p, q: star_away[p, q])):
        gout[0, c] = value
    fill_edges(FIRST)
    scatter(FIRST)
    again = {o: moved(hsum, 0, *o, main, up) + moved(hsum, 1, *o, main, up) for o in MAIN}
    fill(SECOND, components(lambda p, q: again[p, q]))
    scatter(SECOND)

    halo_r.wait()
    theirs = other * nx
    inv_away = 1.0 / (1.0 + rfull[pl.ds(theirs + (nx - 1) * (1 - pos), 1)])
    inv_edge = 1.0 / (1.0 + rfull[pl.ds(pl.multiple_of(theirs + (nx - TILE) * pos, TILE), TILE)])
    for side in range(2):
        for p, q in ORDERS:
            if p + q < 4:
                hsum[side, PLACE[p, q], away] = hsum[side, PLACE[p, q], away] * inv_away
    again = {o: moved(hsum, 0, *o, away, away_up) + moved(hsum, 1, *o, away, away_up) for o in MAIN}
    for c, value in enumerate(components(lambda p, q: again[p, q])):
        gout[1, c] = value
    for k in range(2):
        last = band - 1 if k == 0 else 0
        near, far = (0, 1) if k == 0 else (TILE - 1, TILE - 2)
        for c in range(4):
            row = pl.ds(c * band + last, 1)
            xmsg[k, pl.ds(c, 1)] = msg[FIRST, 1 - k, row]
            xmsg[k, pl.ds(4 + c, 1)] = gout[0, c, pl.ds(near, 1)]
            xmsg[k, pl.ds(8 + c, 1)] = gout[1, c, pl.ds(near, 1)]
            xmsg[k, pl.ds(12 + c, 1)] = gout[1, c, pl.ds(far, 1)]
            xmsg[k, pl.ds(16 + c, 1)] = msg[START, 1 - k, row]
            xmsg[k, pl.ds(20 + c, 1)] = jnp.zeros((1, ny), f32)
    scatter_across()
    scatter(START)
    halo_f.wait()

    @pl.loop(0, chunks)
    def _(c):
        vx, vy0, half, _j = chunk_of(first, c)
        shift = ny - 1 - (ny - 2) * half
        ca = fine_ratio * jnp.abs(vx)
        for jj in range(HALF):
            k = c * HALF + jj
            cb = fine_ratio * jnp.abs(vy0 + jj * DVY)
            cc = 1.0 - ca - cb
            x = fpad[k, main]
            spad[k, main] = (cc * x + ca * fpad[k, up] + cb * pltpu.roll(x, shift, 1)) * inv_main
            x = fpad[k, edge]
            spad[k, edge] = (cc * x + ca * fpad[k, edge_up] + cb * pltpu.roll(x, shift, 1)) * inv_edge

    row8 = lax.broadcasted_iota(jnp.int32, (TILE, ny), 0)
    row_band = lax.broadcasted_iota(jnp.int32, (band, ny), 0)
    brow = (band - 1) * b
    brow2 = 1 + (band - 3) * b

    def received(field):
        size = pl.ds(0, sizes[field])

        @pl.when(h == 1)
        def _():
            settle(red.at[field, pl.ds(0, nv - 1), size], rs_recv.at[field])

        @pl.when(h == 0)
        def _():
            settle(red.at[field, :, size], rs_recv.at[field])

    def summed(field, rows):
        total = red[field, 0, rows]
        for n in range(1, nv):
            total = total + red[field, n, rows]
        return total

    def comp(c):
        return pl.ds(c * band, band)

    def framed(value, outer, inner):
        above = jnp.where(b == 0, outer, inner)
        below = jnp.where(b == 0, inner, outer)
        return jnp.concatenate([value, jnp.where(row8 == TILE - 1, above, below)], axis=0)

    def placed(row, at):
        return jnp.where(row_band == at, row, 0.0)

    def share(n, size):
        rows = pl.ds(0, size)

        @pl.when(h == 1)
        def _():
            pin[n, b, rows] = pmsg[n, rows]

        @pl.when(h == 0)
        def _():
            remote(
                pmsg.at[n, rows], pin.at[n, b, rows], ag_send.at[n], ag_recv.at[n], (w, v, 0)
            ).start()

        for d in range(1, nv):
            remote(
                pmsg.at[n, rows], pin.at[n, b, rows], ag_send.at[n], ag_recv.at[n],
                (w, lax.rem(v + d, nv), h),
            ).start()

    def pass_on():
        after, before = lax.rem(g + 1, 4), lax.rem(g + 3, 4)

        def place(n):
            half, k = n // 2, n % 2
            return base + half + k * (3 - 2 * half)

        return [
            remote(vmsg, vin, win_send.at[0], win_recv.at[0], (w + 1, v, 1)),
            remote(vrow.at[0], vrow_in.at[1], win_send.at[1], win_recv.at[1], (w + 1, place(before), 1)),
            remote(vrow.at[1], vrow_in.at[0], win_send.at[2], win_recv.at[2], (w + 1, place(after), 1)),
        ]

    def finish(values):
        for c in range(4):
            pmsg[2, comp(c)] = values[c]
        if nw > 1:

            @pl.when(w + 1 < nw)
            def _():
                for c in range(4):
                    vmsg[comp(c)] = values[c]
                    vrow[0, pl.ds(c, 1)] = values[c][:1]
                    vrow[0, pl.ds(4 + c, 1)] = values[c][:1]
                    vrow[1, pl.ds(c, 1)] = values[c][-1:]
                    vrow[1, pl.ds(4 + c, 1)] = values[c][-1:]
                for copy in pass_on():
                    copy.start()

        share(2, full)

    @pl.when(is_owner)
    def _():
        received(FIRST)

        @pl.when(h == 1)
        def _():
            settle(redx, rs_recv.at[3])

        @pl.when(h == 0)
        def _():
            settle(redx.at[pl.ds(0, nv - 1)], rs_recv.at[3])

        across = redx[0]
        for n in range(1, nv):
            across = across + redx[n]
        xs[...] = across

        def x_row(n):
            return xs[pl.ds(n, 1)]

        def assembled(field, at):
            es[...] = summed(field, pl.ds(full, TILE))
            out = []
            for c in range(4):
                value = summed(field, comp(c))
                if field == FIRST:
                    value = value + placed(x_row(4 + c), brow)
                out.append(framed(value, es[pl.ds(c, 1)] + x_row(at + c), es[pl.ds(4 + c, 1)]))
            return out

        rs, ux, uy, temp = physical_variables(assembled(FIRST, 0))
        rows_all = 2 * nx
        mid = pl.ds(pl.multiple_of(g * band, TILE), band)
        above = rfull[pl.ds(lax.rem(g * band + rows_all - 1, rows_all), 1)]
        below = rfull[pl.ds(lax.rem(g * band + band, rows_all), 1)]
        rate = jnp.concatenate([rfull[mid], jnp.where(row8 == TILE - 1, above, below)], axis=0)
        fr[0] = ux
        fr[1] = uy
        fr[2] = -0.5 / temp
        fr[3] = rs / temp * (rate / (1.0 + rate))
        for n in range(4):
            pmsg[0, comp(n)] = fr[n, pl.ds(0, band)]
            outer = fr[n, pl.ds(band + (TILE - 1) * (1 - b), 1)]
            pmsg[0, pl.ds(full + n, 1)] = outer
            pmsg[0, pl.ds(full + 4 + n, 1)] = outer
        share(0, full + TILE)

        @pl.loop(0, frame // TILE)
        def _(t):
            rows = pl.ds(pl.multiple_of(t * TILE, TILE), TILE)
            ux, uy, scale, amp = [fr[n, rows] for n in range(4)]

            def half_sums(speeds, drift):
                weights = []
                for speed in speeds:
                    d = speed - drift
                    weights.append(jnp.exp(d * d * scale))
                sides = []
                half = len(speeds) // 2
                for at, c in ((half, 0.5 * vel_max), (0, -0.5 * vel_max)):
                    m = [empty] * 4
                    for n in range(half // 2, half):
                        t = speeds[at + n] - c
                        high, low = weights[at + n], weights[at + half - 1 - n]
                        even, odd = high + low, high - low
                        m = [m[0] + even, m[1] + t * odd, m[2] + t**2 * even, m[3] + t**3 * odd]
                    sides.append([
                        m[0],
                        m[1] + c * m[0],
                        m[2] + (2 * c) * m[1] + c**2 * m[0],
                        m[3] + (3 * c) * m[2] + (3 * c**2) * m[1] + c**3 * m[0],
                    ])
                return sides

            xp, xm = half_sums([-vel_max + (i + 0.5) * DVX for i in range(NVX)], ux)
            yp, ym = half_sums([-vel_max + (j + 0.5) * DVY for j in range(NVY)], uy)
            xs_ = [x + y for x, y in zip(xp, xm)]
            ys_ = [x + y for x, y in zip(yp, ym)]
            amp = WEIGHT * amp

            def store(n, coef, x, y):
                x = [coef * amp * t for t in x]
                flux[n, rows] = x[0] * y[0]
                flux[n + 1, rows] = x[1] * y[0]
                flux[n + 2, rows] = x[0] * y[1]
                flux[n + 3, rows] = 0.5 * (x[2] * y[0] + x[0] * y[2])

            store(0, 1.0, xs_, ys_)
            store(4, fine_ratio, xp[1:], ys_)
            store(8, -fine_ratio, xm[1:], ys_)
            store(12, fine_ratio, xs_, yp[1:])
            store(16, -fine_ratio, xs_, ym[1:])

        received(SECOND)
        inner = pl.ds(0, band)
        for c in range(4):
            to_y, from_y = flux[12 + c, inner], flux[16 + c, inner]
            energy[c] = (
                summed(SECOND, comp(c)) + placed(x_row(8 + c), brow) + placed(x_row(12 + c), brow2)
            ) + (
                flux[c, inner] - flux[4 + c, inner] - flux[8 + c, inner] - to_y - from_y
                + pltpu.roll(flux[4 + c], 1, 0)[:band] + pltpu.roll(flux[8 + c], frame - 1, 0)[:band]
                + pltpu.roll(to_y, 1, 1) + pltpu.roll(from_y, ny - 1, 1)
            )
        rs, ux, uy, temp = physical_variables(energy)
        pmsg[1, comp(0)] = ux
        pmsg[1, comp(1)] = uy
        pmsg[1, comp(2)] = -0.5 / temp
        pmsg[1, comp(3)] = rs / temp * (1.0 / (1.0 + rfull[mid]))
        share(1, full)

        received(START)
        stepped = coarse(assembled(START, 16), band)
        for c in range(4):
            gs[c] = stepped[c]
            delta[c] = energy[c] - stepped[c]

        @pl.when(w == 0)
        def _():
            finish([gs[c] + delta[c] for c in range(4)])

    @pl.loop(0, chunks)
    def _(c):
        vx, vy0, half, _j = chunk_of(first, c)
        shift = ny - 1 - (ny - 2) * half
        ca = fine_ratio * jnp.abs(vx)
        for jj in range(HALF):
            k = c * HALF + jj
            cb = fine_ratio * jnp.abs(vy0 + jj * DVY)
            x = spad[k, main]
            star = (1.0 - ca - cb) * x + ca * spad[k, up] + cb * pltpu.roll(x, shift, 1)
            star2[k] = star * inv_main

    if nw > 1:

        @pl.when(is_owner & (w > 0))
        def _():
            settle(vin, win_recv.at[0])
            settle(vrow_in.at[1], win_recv.at[1])
            settle(vrow_in.at[0], win_recv.at[2])
            u = [
                jnp.concatenate(
                    [
                        vin[comp(c)],
                        jnp.where(row8 == TILE - 1, vrow_in[0, pl.ds(c, 1)], vrow_in[1, pl.ds(c, 1)]),
                    ],
                    axis=0,
                )
                for c in range(4)
            ]
            stepped = coarse(u, band)
            finish([stepped[c] + delta[c] for c in range(4)])

    def shared(n, size):
        rows = pl.ds(0, size)

        @pl.when(is_owner & (h == 1))
        def _():
            settle(pin.at[n, 0, rows], ag_recv.at[n])

        @pl.when(jnp.logical_not(is_owner & (h == 1)))
        def _():
            settle(pin.at[n, :, rows], ag_recv.at[n])

    shared(0, full + TILE)
    for n in range(4):
        for k in range(2):
            phys[n, pl.ds(2 * TILE + k * band, band)] = pin[0, k, comp(n)]
        phys[n, edge] = jnp.broadcast_to(pin[0, 1 - pos, pl.ds(full + n, 1)], (TILE, ny))
    for rows in (main, edge):
        drift, scale = phys[1, rows], phys[2, rows]
        for j in range(NVY):
            d = (-vel_max + (j + 0.5) * DVY) - drift
            e = jnp.exp(d * d * scale)
            yt[j, rows] = e
            if rows is main:
                yr[j] = pltpu.roll(e, ny - 1 if j < HALF else 1, 1)

    @pl.loop(0, chunks)
    def _(c):
        vx, vy0, half, j0 = chunk_of(first, c)
        shift = ny - 1 - (ny - 2) * half
        ca = fine_ratio * jnp.abs(vx)
        for rows in (main, edge):
            d = vx - phys[0, rows]
            xpad[rows] = phys[3, rows] * jnp.exp(d * d * phys[2, rows])
        x = xpad[main]
        here = inv_main * x
        behind = (ca * inv_main) * xpad[up]
        beside = inv_main * pltpu.roll(x, shift, 1)
        for jj in range(HALF):
            k = c * HALF + jj
            cb = fine_ratio * jnp.abs(vy0 + jj * DVY)
            star2[k] = (
                star2[k] + ((1.0 - ca - cb) * here) * yt[j0 + jj, main] + behind * yt[j0 + jj, up]
                + (cb * beside) * yr[j0 + jj]
            )

    shared(1, full)
    for k in range(2):
        rows = pl.ds(k * band, band)
        for n in range(4):
            e_phys[n, rows] = pin[1, k, comp(n)]
    drift, scale = e_phys[1], e_phys[2]
    for j in range(NVY):
        d = (-vel_max + (j + 0.5) * DVY) - drift
        ye[j] = jnp.exp(d * d * scale)
    shared(2, full)
    for k in range(2):
        for n in range(4):
            corr_out[n, pl.ds(k * band, band)] = pin[2, k, comp(n)]

    for field in range(3):
        size = pl.ds(0, sizes[field])
        for k in range(2):
            own = to_owner(s, k)[1]

            @pl.when(jnp.logical_not(own))
            def _():
                settle(msg.at[field, k, size], rs_send.at[field])

    for k in range(2):
        own = to_owner(other, k)[1]

        @pl.when(jnp.logical_not(own))
        def _():
            settle(xmsg.at[k], rs_send.at[3])

    @pl.when(is_owner)
    def _():
        for n, size in ((0, full + TILE), (1, full), (2, full)):
            rows = pl.ds(0, size)
            for _ in range(nv - 1):
                settle(pmsg.at[n, rows], ag_send.at[n])

            @pl.when(h == 0)
            def _():
                settle(pmsg.at[n, rows], ag_send.at[n])

        if nw > 1:

            @pl.when(w + 1 < nw)
            def _():
                settle(vmsg, win_send.at[0])
                settle(vrow.at[0], win_send.at[1])
                settle(vrow.at[1], win_send.at[2])


def lift_kernel(parts, star2, ye, e_phys, corr, lifted, corrected, yc, out, save_sem):
    count = star2.shape[0]
    first = lax.axis_index("vel") * count
    corrected[...] = corr[...]
    rs, uc, uy, temp = physical_variables(corr)
    sc = -0.5 / temp
    mc = rs / temp
    for j in range(NVY):
        d = (-vel_max + (j + 0.5) * DVY) - uy
        yc[j] = jnp.exp(d * d * sc)
    chunks = count // HALF
    per = chunks // parts

    def save(n):
        rows = pl.ds(n * per * HALF, per * HALF)
        return pltpu.make_async_copy(out.at[rows], lifted.at[rows], save_sem.at[n])

    for n in range(parts):

        @pl.loop(n * per, (n + 1) * per)
        def _(c):
            vx, _vy, _half, j0 = chunk_of(first, c)
            dc = vx - uc
            xc = mc * jnp.exp(dc * dc * sc)
            de = vx - e_phys[0]
            xe = e_phys[3] * jnp.exp(de * de * e_phys[2])
            for jj in range(HALF):
                k = c * HALF + jj
                out[k] = star2[k] + (xc * yc[j0 + jj] - xe * ye[j0 + jj])

        save(n).start()
    for n in range(parts):
        save(n).wait()


def per_device(nw, nv, f_start, relax_rate):
    field = f_start[0]
    count, nx, ny = field.shape
    band = nx // 2
    frame = band + TILE
    full = 4 * band
    pad = nx + 4 * TILE
    vmem = pltpu.VMEM
    dma = pltpu.SemaphoreType.DMA
    small = jax.ShapeDtypeStruct((4, nx, ny), f32)
    speeds = jax.ShapeDtypeStruct((NVY, nx, ny), f32)
    in_vmem = pl.BlockSpec(memory_space=pltpu.VMEM)
    in_hbm = pl.BlockSpec(memory_space=pltpu.HBM)
    field = pltpu.with_memory_space_constraint(field, pltpu.HBM)
    star2, ye, e_phys, corr = pl.pallas_call(
        functools.partial(advance_kernel, nw, nv),
        out_shape=(jax.ShapeDtypeStruct((count, nx, ny), f32), speeds, small, small),
        in_specs=[in_hbm, in_hbm],
        out_specs=(in_vmem,) * 4,
        scratch_shapes=[
            vmem((count, pad, ny), f32),
            vmem((count, pad, ny), f32),
            vmem((2 * nx, ny), f32),
            vmem((2, len(ORDERS), pad, ny), f32),
            vmem((2, len(ORDERS), pad, ny), f32),
            vmem((2, 4, TILE, ny), f32),
            vmem((3, 2, full + TILE, ny), f32),
            vmem((2, 3 * TILE, ny), f32),
            vmem((3, nv, full + TILE, ny), f32),
            vmem((nv, 3 * TILE, ny), f32),
            vmem((3 * TILE, ny), f32),
            vmem((TILE, ny), f32),
            vmem((4, frame, ny), f32),
            vmem((20, frame, ny), f32),
            vmem((4, band, ny), f32),
            vmem((4, band, ny), f32),
            vmem((4, band, ny), f32),
            vmem((3, full + TILE, ny), f32),
            vmem((3, 2, full + TILE, ny), f32),
            vmem((full, ny), f32),
            vmem((2, TILE, ny), f32),
            vmem((full, ny), f32),
            vmem((2, TILE, ny), f32),
            vmem((4, pad, ny), f32),
            vmem((pad, ny), f32),
            vmem((NVY, pad, ny), f32),
            vmem((NVY, nx, ny), f32),
            dma((1 + nx // TILE,)), dma((2,)), dma((2,)), dma((4,)), dma((4,)), dma((3,)), dma((3,)),
            dma((3,)), dma((3,)),
        ],
        compiler_params=pltpu.CompilerParams(
            collective_id=0, has_side_effects=True, vmem_limit_bytes=40 << 20
        ),
        name="advance",
    )(field, pltpu.with_memory_space_constraint(relax_rate, pltpu.HBM))

    chunks = count // HALF
    parts = next(n for n in (6, 4, 3, 2, 1) if chunks % n == 0)
    lifted, corrected = pl.pallas_call(
        functools.partial(lift_kernel, parts),
        out_shape=(jax.ShapeDtypeStruct((count, nx, ny), f32), small),
        in_specs=[in_vmem] * 4,
        out_specs=(in_hbm, in_vmem),
        scratch_shapes=[
            vmem((NVY, nx, ny), f32), vmem((count, nx, ny), f32), dma((parts,)),
        ],
        compiler_params=pltpu.CompilerParams(vmem_limit_bytes=16 << 20),
        name="lift",
    )(star2, ye, e_phys, corr)
    return corrected[None], lifted[None]


def solution(mesh):
    return jax.shard_map(
        functools.partial(per_device, mesh.shape["win"], mesh.shape["vel"]),
        mesh=mesh,
        in_specs=(P("win", "vel", "sp", None), P("sp", None)),
        out_specs=(P("win", None, "sp", None), P("win", "vel", "sp", None)),
        check_vma=False,
    )
```

```python
import functools
import math

import jax
import jax.numpy as jnp
from jax import lax
from jax.experimental import pallas as pl
from jax.experimental.pallas import tpu as pltpu
from jax.sharding import PartitionSpec as P

NVX = 48
NVY = 32
HALF = NVY // 2
TILE = 8
vel_max = 6.0
fine_ratio = 0.075
coarse_ratio = 0.15
density_floor = 0.3
thermal_lower_bound = 0.3
DVX = 2.0 * vel_max / NVX
DVY = 2.0 * vel_max / NVY
WEIGHT = DVX * DVY / (2.0 * math.pi)
MESH = pl.DeviceIdType.MESH
f32 = jnp.float32
ORDERS = [(p, q) for p in range(5) for q in range(5 - p)]
PLACE = {order: n for n, order in enumerate(ORDERS)}
MAIN = [(0, 0), (0, 1), (1, 0), (0, 2), (2, 0)]
FIRST, START, SECOND = range(3)


def physical_variables(u):
    rs = jnp.maximum(u[0], density_floor)
    ux = u[1] / rs
    uy = u[2] / rs
    temp = jnp.maximum((u[3] - 0.5 * (u[1] * ux + u[2] * uy)) / rs, thermal_lower_bound)
    return rs, ux, uy, temp


def chunk_of(first, c):
    k = first + c * HALF
    i = k // NVY
    j = k % NVY
    vx = -vel_max + (i.astype(f32) + 0.5) * DVX
    vy = -vel_max + (j.astype(f32) + 0.5) * DVY
    return vx, vy, j // HALF, j


def coarse(u, band):
    rows, ny = u[0].shape
    rs, ux, uy, temp = physical_variables(u)
    p = rs * temp
    wave = jnp.sqrt(2.0 * temp)
    fx = [u[1], u[1] * ux + p, u[2] * ux, (u[3] + p) * ux]
    fy = [u[2], u[1] * uy, u[2] * uy + p, (u[3] + p) * uy]
    sx = jnp.abs(ux) + wave
    sy = jnp.abs(uy) + wave
    mx = jnp.maximum(sx, pltpu.roll(sx, rows - 1, 0))
    my = jnp.maximum(sy, pltpu.roll(sy, ny - 1, 1))
    out = []
    for c in range(4):
        face_x = 0.5 * (fx[c] + pltpu.roll(fx[c], rows - 1, 0)) - 0.5 * mx * (
            pltpu.roll(u[c], rows - 1, 0) - u[c]
        )
        face_y = 0.5 * (fy[c] + pltpu.roll(fy[c], ny - 1, 1)) - 0.5 * my * (
            pltpu.roll(u[c], ny - 1, 1) - u[c]
        )
        g = u[c] - coarse_ratio * (
            face_x - pltpu.roll(face_x, 1, 0) + (face_y - pltpu.roll(face_y, 1, 1))
        )
        out.append(g[:band])
    return out


def advance_kernel(
    nw, nv,
    f, r, star2, ye, e_phys, corr_out,
    fpad, spad, rfull, bsum, hsum, gout, msg, xmsg, red, redx, xs, es, fr, flux, energy, delta, gs,
    pmsg, pin, vmsg, vrow, vin, vrow_in, phys, xpad, yt, yr,
    load_sem, halo_send, halo_recv, rs_send, rs_recv, ag_send, ag_recv, win_send, win_recv,
):
    w, v, s = lax.axis_index("win"), lax.axis_index("vel"), lax.axis_index("sp")
    count, nx, ny = f.shape
    chunks = count // HALF
    first = v * count
    other = 1 - s
    pos = (2 * v) // nv
    band = nx // 2
    frame = band + TILE
    full = 4 * band
    main = pl.ds(2 * TILE, nx)
    end = 2 * TILE + nx
    up = pl.ds(2 * TILE + 1 - 2 * pos, nx)
    hb = pl.multiple_of(end - (end - TILE) * pos, TILE)
    edge = pl.ds(hb, TILE)
    edge_up = pl.ds(hb + 1 - 2 * pos, TILE)
    ho = pl.multiple_of(TILE + (end - TILE) * pos, TILE)
    away = pl.ds(ho, TILE)
    away_up = pl.ds(ho + 1 - 2 * pos, TILE)
    tiles = nx // TILE

    base = nv // 2 - 2
    off = v - base
    is_owner = (s == 1) & (off >= 0) & (off < 4)
    b = off // 2
    h = (off + b) % 2
    g = 2 * h + b

    def owner_at(half, k):
        return base + (half if k == 0 else 3 - half)

    def load_f(t):
        rows = pl.ds(pl.multiple_of(t * TILE, TILE), TILE)
        padded = pl.ds(pl.multiple_of((t + 2) * TILE, TILE), TILE)
        return pltpu.make_async_copy(f.at[:, rows], fpad.at[:, padded], load_sem.at[t])

    for t in range(tiles):
        load_f(t).start()
    mine = pl.ds(pl.multiple_of(s * nx, TILE), nx)
    load_r = pltpu.make_async_copy(r, rfull.at[mine], load_sem.at[tiles])
    load_r.start()

    def signal(device):
        pl.semaphore_signal(barrier, inc=1, device_id=device, device_id_type=MESH)

    barrier = pltpu.get_barrier_semaphore()
    signal((w, v, other))
    for o in range(4):

        @pl.when(jnp.logical_not((v == base + o) & (s == 1)))
        def _():
            signal((w, base + o, 1))

    @pl.when(is_owner)
    def _():
        signal((w, v, 0))
        for d in range(1, nv):
            for half in range(2):
                signal((w, lax.rem(v + d, nv), half))

        @pl.when(w + 1 < nw)
        def _():
            for o in range(4):
                signal((w + 1, base + o, 1))

        @pl.when(w > 0)
        def _():
            for o in range(4):
                signal((w - 1, base + o, 1))

    def remote(src, dst, send, recv, device):
        return pltpu.make_async_remote_copy(
            src_ref=src, dst_ref=dst, send_sem=send, recv_sem=recv,
            device_id=device, device_id_type=MESH,
        )

    def settle(ref, sem):
        pltpu.make_async_copy(ref, ref, sem).wait()

    empty = jnp.zeros((TILE, ny), f32)
    for side in range(2):
        for n in range(len(ORDERS)):
            for at in (TILE, end):
                bsum[side, n, pl.ds(at, TILE)] = empty
                hsum[side, n, pl.ds(at, TILE)] = empty

    parity = (first // HALF) % 2
    rounds = (chunks + 1) // 2

    @pl.loop(0, tiles)
    def _(t):
        load_f(t).wait()
        rows = pl.ds(pl.multiple_of(2 * TILE + t * TILE, TILE), TILE)
        for side in range(2):
            acc = {order: jnp.zeros((TILE, ny), f32) for order in ORDERS}
            for n in range(rounds):
                c = (side + parity) % 2 + 2 * n
                weight = 1.0
                if chunks % 2:
                    weight = jnp.where(c < chunks, 1.0, 0.0).astype(f32)
                    c = jnp.minimum(c, chunks - 1)
                vx = chunk_of(first, c)[0]
                sums = [jnp.zeros((TILE, ny), f32)] * 5
                for jj in range(HALF // 2, HALF):
                    tt = (jj + 0.5) * DVY - 0.5 * vel_max
                    high = fpad[c * HALF + jj, rows]
                    low = fpad[c * HALF + HALF - 1 - jj, rows]
                    even, odd = high + low, high - low
                    sums = [
                        sums[0] + even, sums[1] + tt * odd, sums[2] + tt**2 * even,
                        sums[3] + tt**3 * odd, sums[4] + tt**4 * even,
                    ]
                power = weight
                for q in range(5):
                    for m in range(5 - q):
                        term = sums[m] if q == 0 and chunks % 2 == 0 else sums[m] * power
                        acc[m, q] = acc[m, q] + term
                    power = power * vx
            centre = (side - 0.5) * vel_max
            for p, q in ORDERS:
                total = acc[p, q]
                for m in range(p):
                    total = total + (math.comb(p, m) * centre ** (p - m)) * acc[m, q]
                bsum[side, PLACE[p, q], rows] = total

    def components(get):
        return [
            WEIGHT * get(0, 0), WEIGHT * get(0, 1), WEIGHT * get(1, 0),
            (0.5 * WEIGHT) * (get(0, 2) + get(2, 0)),
        ]

    def fill(field, values):
        for c in range(4):
            for k in range(2):
                msg[field, k, pl.ds(c * band, band)] = values[c][k * band : (k + 1) * band]

    def fill_edges(field):
        for c in range(4):
            for k in range(2):
                if field == FIRST:
                    outer = gout[0, c, pl.ds(TILE - 1 if k == 0 else 0, 1)]
                else:
                    outer = jnp.zeros((1, ny), f32)
                msg[field, k, pl.ds(full + c, 1)] = outer
                inner = c * band if k == 0 else (c + 1) * band - 1
                msg[field, k, pl.ds(full + 4 + c, 1)] = msg[field, 1 - k, pl.ds(inner, 1)]

    def to_owner(half, k):
        target = owner_at(half, k)
        return target, (v == target) & (s == 1)

    sizes = {FIRST: full + TILE, START: full + TILE, SECOND: full}

    def scatter(field):
        size = pl.ds(0, sizes[field])
        for k in range(2):
            target, own = to_owner(s, k)

            @pl.when(own)
            def _():
                red[field, v, size] = msg[field, k, size]

            @pl.when(jnp.logical_not(own))
            def _():
                remote(
                    msg.at[field, k, size], red.at[field, v, size],
                    rs_send.at[field], rs_recv.at[field], (w, target, 1),
                ).start()

    ACROSS_ROWS = (pl.ds(0, TILE), pl.ds(TILE, 2 * TILE))

    def scatter_across(part):
        rows = ACROSS_ROWS[part]
        for k in range(2):
            target, own = to_owner(other, k)

            @pl.when(own)
            def _():
                redx[v, rows] = xmsg[k, rows]

            @pl.when(jnp.logical_not(own))
            def _():
                remote(
                    xmsg.at[k, rows], redx.at[v, rows],
                    rs_send.at[3 + part], rs_recv.at[3 + part], (w, target, 1),
                ).start()

    fill(START, components(lambda p, q: bsum[0, PLACE[p, q], main] + bsum[1, PLACE[p, q], main]))
    fill_edges(START)

    neighbours = jnp.where(w > 0, 4, 0) + jnp.where(w + 1 < nw, 4, 0)
    pl.semaphore_wait(barrier, jnp.where(is_owner, 2 * nv + 3 + neighbours, 5))
    load_r.wait()
    source = pl.ds(pl.multiple_of((nx - TILE) * pos, TILE), TILE)
    halo_r = remote(r, rfull.at[mine], halo_send.at[0], halo_recv.at[0], (w, v, other))
    halo_f = remote(f.at[:, source], fpad.at[:, edge], halo_send.at[1], halo_recv.at[1], (w, v, other))
    halo_r.start()
    halo_f.start()

    inv_main = 1.0 / (1.0 + rfull[mine])
    along = fine_ratio * (2 * pos - 1).astype(f32)
    ACROSS = ((-fine_ratio, ny - 1), (fine_ratio, 1))

    def moved(table, side, p, q, rows, rows_up):
        across, shift = ACROSS[side]
        bx = table[side, PLACE[p, q + 1], rows]
        by = table[side, PLACE[p + 1, q], rows]
        return (
            table[side, PLACE[p, q], rows]
            + along * (table[side, PLACE[p, q + 1], rows_up] - bx)
            + across * (pltpu.roll(by, shift, 1) - by)
        )

    star_main, star_away = {}, {}

    def one_step(side, p, q):
        star = moved(bsum, side, p, q, main, up)
        beyond = moved(bsum, side, p, q, away, away_up)
        hsum[side, PLACE[p, q], main] = star * inv_main
        hsum[side, PLACE[p, q], away] = beyond
        return star, beyond

    for order in MAIN:
        parts = [one_step(side, *order) for side in range(2)]
        star_main[order] = parts[0][0] + parts[1][0]
        star_away[order] = parts[0][1] + parts[1][1]
    fill(FIRST, components(lambda p, q: star_main[p, q]))
    for c, value in enumerate(components(lambda p, q: star_away[p, q])):
        gout[0, c] = value
    fill_edges(FIRST)
    for k in range(2):
        last = band - 1 if k == 0 else 0
        for c in range(4):
            xmsg[k, pl.ds(c, 1)] = msg[FIRST, 1 - k, pl.ds(c * band + last, 1)]
            xmsg[k, pl.ds(4 + c, 1)] = gout[0, c, pl.ds(0 if k == 0 else TILE - 1, 1)]
    scatter_across(0)
    scatter(FIRST)
    for p, q in ORDERS:
        if p + q < 4 and (p, q) not in MAIN:
            for side in range(2):
                one_step(side, p, q)
    again = {o: moved(hsum, 0, *o, main, up) + moved(hsum, 1, *o, main, up) for o in MAIN}
    fill(SECOND, components(lambda p, q: again[p, q]))
    scatter(SECOND)

    halo_r.wait()
    theirs = other * nx
    inv_away = 1.0 / (1.0 + rfull[pl.ds(theirs + (nx - 1) * (1 - pos), 1)])
    inv_edge = 1.0 / (1.0 + rfull[pl.ds(pl.multiple_of(theirs + (nx - TILE) * pos, TILE), TILE)])
    for side in range(2):
        for p, q in ORDERS:
            if p + q < 4:
                hsum[side, PLACE[p, q], away] = hsum[side, PLACE[p, q], away] * inv_away
    again = {o: moved(hsum, 0, *o, away, away_up) + moved(hsum, 1, *o, away, away_up) for o in MAIN}
    for c, value in enumerate(components(lambda p, q: again[p, q])):
        gout[1, c] = value
    for k in range(2):
        last = band - 1 if k == 0 else 0
        near, far = (0, 1) if k == 0 else (TILE - 1, TILE - 2)
        for c in range(4):
            xmsg[k, pl.ds(8 + c, 1)] = gout[1, c, pl.ds(near, 1)]
            xmsg[k, pl.ds(12 + c, 1)] = gout[1, c, pl.ds(far, 1)]
            xmsg[k, pl.ds(16 + c, 1)] = msg[START, 1 - k, pl.ds(c * band + last, 1)]
            xmsg[k, pl.ds(20 + c, 1)] = jnp.zeros((1, ny), f32)
    scatter_across(1)
    scatter(START)
    halo_f.wait()

    @pl.loop(0, chunks)
    def _(c):
        vx, vy0, half, _j = chunk_of(first, c)
        shift = ny - 1 - (ny - 2) * half
        ca = fine_ratio * jnp.abs(vx)
        for jj in range(HALF):
            k = c * HALF + jj
            cb = fine_ratio * jnp.abs(vy0 + jj * DVY)
            cc = 1.0 - ca - cb
            x = fpad[k, main]
            spad[k, main] = (cc * x + ca * fpad[k, up] + cb * pltpu.roll(x, shift, 1)) * inv_main
            x = fpad[k, edge]
            spad[k, edge] = (cc * x + ca * fpad[k, edge_up] + cb * pltpu.roll(x, shift, 1)) * inv_edge

    row8 = lax.broadcasted_iota(jnp.int32, (TILE, ny), 0)
    row_band = lax.broadcasted_iota(jnp.int32, (band, ny), 0)
    brow = (band - 1) * b
    brow2 = 1 + (band - 3) * b

    def received(field):
        size = pl.ds(0, sizes[field])

        @pl.when(h == 1)
        def _():
            settle(red.at[field, pl.ds(0, nv - 1), size], rs_recv.at[field])

        @pl.when(h == 0)
        def _():
            settle(red.at[field, :, size], rs_recv.at[field])

    def summed(field, rows):
        total = red[field, 0, rows]
        for n in range(1, nv):
            total = total + red[field, n, rows]
        return total

    def comp(c):
        return pl.ds(c * band, band)

    def framed(value, outer, inner):
        above = jnp.where(b == 0, outer, inner)
        below = jnp.where(b == 0, inner, outer)
        return jnp.concatenate([value, jnp.where(row8 == TILE - 1, above, below)], axis=0)

    def placed(row, at):
        return jnp.where(row_band == at, row, 0.0)

    def share(n, size):
        rows = pl.ds(0, size)

        @pl.when(h == 1)
        def _():
            pin[n, b, rows] = pmsg[n, rows]

        @pl.when(h == 0)
        def _():
            remote(
                pmsg.at[n, rows], pin.at[n, b, rows], ag_send.at[n], ag_recv.at[n], (w, v, 0)
            ).start()

        for d in range(1, nv):
            remote(
                pmsg.at[n, rows], pin.at[n, b, rows], ag_send.at[n], ag_recv.at[n],
                (w, lax.rem(v + d, nv), h),
            ).start()

    def pass_on():
        after, before = lax.rem(g + 1, 4), lax.rem(g + 3, 4)

        def place(n):
            half, k = n // 2, n % 2
            return base + half + k * (3 - 2 * half)

        return [
            remote(vmsg, vin, win_send.at[0], win_recv.at[0], (w + 1, v, 1)),
            remote(vrow.at[0], vrow_in.at[1], win_send.at[1], win_recv.at[1], (w + 1, place(before), 1)),
            remote(vrow.at[1], vrow_in.at[0], win_send.at[2], win_recv.at[2], (w + 1, place(after), 1)),
        ]

    def finish(values):
        for c in range(4):
            pmsg[2, comp(c)] = values[c]
        if nw > 1:

            @pl.when(w + 1 < nw)
            def _():
                for c in range(4):
                    vmsg[comp(c)] = values[c]
                    vrow[0, pl.ds(c, 1)] = values[c][:1]
                    vrow[0, pl.ds(4 + c, 1)] = values[c][:1]
                    vrow[1, pl.ds(c, 1)] = values[c][-1:]
                    vrow[1, pl.ds(4 + c, 1)] = values[c][-1:]
                for copy in pass_on():
                    copy.start()

        share(2, full)

    @pl.when(is_owner)
    def _():
        def received_across(part):
            rows = ACROSS_ROWS[part]

            @pl.when(h == 1)
            def _():
                settle(redx.at[:, rows], rs_recv.at[3 + part])

            @pl.when(h == 0)
            def _():
                settle(redx.at[pl.ds(0, nv - 1), rows], rs_recv.at[3 + part])

            across = redx[0, rows]
            for n in range(1, nv):
                across = across + redx[n, rows]
            xs[rows] = across

        received(FIRST)
        received_across(0)

        def x_row(n):
            return xs[pl.ds(n, 1)]

        def assembled(field, at):
            es[...] = summed(field, pl.ds(full, TILE))
            out = []
            for c in range(4):
                value = summed(field, comp(c))
                if field == FIRST:
                    value = value + placed(x_row(4 + c), brow)
                out.append(framed(value, es[pl.ds(c, 1)] + x_row(at + c), es[pl.ds(4 + c, 1)]))
            return out

        rs, ux, uy, temp = physical_variables(assembled(FIRST, 0))
        rows_all = 2 * nx
        mid = pl.ds(pl.multiple_of(g * band, TILE), band)
        above = rfull[pl.ds(lax.rem(g * band + rows_all - 1, rows_all), 1)]
        below = rfull[pl.ds(lax.rem(g * band + band, rows_all), 1)]
        rate = jnp.concatenate([rfull[mid], jnp.where(row8 == TILE - 1, above, below)], axis=0)
        fr[0] = ux
        fr[1] = uy
        fr[2] = -0.5 / temp
        fr[3] = rs / temp * (rate / (1.0 + rate))
        for n in range(4):
            pmsg[0, comp(n)] = fr[n, pl.ds(0, band)]
            outer = fr[n, pl.ds(band + (TILE - 1) * (1 - b), 1)]
            pmsg[0, pl.ds(full + n, 1)] = outer
            pmsg[0, pl.ds(full + 4 + n, 1)] = outer
        share(0, full + TILE)

        @pl.loop(0, frame // TILE)
        def _(t):
            rows = pl.ds(pl.multiple_of(t * TILE, TILE), TILE)
            ux, uy, scale, amp = [fr[n, rows] for n in range(4)]

            def half_sums(speeds, drift):
                weights = []
                for speed in speeds:
                    d = speed - drift
                    weights.append(jnp.exp(d * d * scale))
                sides = []
                half = len(speeds) // 2
                for at, c in ((half, 0.5 * vel_max), (0, -0.5 * vel_max)):
                    m = [empty] * 4
                    for n in range(half // 2, half):
                        t = speeds[at + n] - c
                        high, low = weights[at + n], weights[at + half - 1 - n]
                        even, odd = high + low, high - low
                        m = [m[0] + even, m[1] + t * odd, m[2] + t**2 * even, m[3] + t**3 * odd]
                    sides.append([
                        m[0],
                        m[1] + c * m[0],
                        m[2] + (2 * c) * m[1] + c**2 * m[0],
                        m[3] + (3 * c) * m[2] + (3 * c**2) * m[1] + c**3 * m[0],
                    ])
                return sides

            xp, xm = half_sums([-vel_max + (i + 0.5) * DVX for i in range(NVX)], ux)
            yp, ym = half_sums([-vel_max + (j + 0.5) * DVY for j in range(NVY)], uy)
            xs_ = [x + y for x, y in zip(xp, xm)]
            ys_ = [x + y for x, y in zip(yp, ym)]
            amp = WEIGHT * amp

            def store(n, coef, x, y):
                x = [coef * amp * t for t in x]
                flux[n, rows] = x[0] * y[0]
                flux[n + 1, rows] = x[1] * y[0]
                flux[n + 2, rows] = x[0] * y[1]
                flux[n + 3, rows] = 0.5 * (x[2] * y[0] + x[0] * y[2])

            store(0, 1.0, xs_, ys_)
            store(4, fine_ratio, xp[1:], ys_)
            store(8, -fine_ratio, xm[1:], ys_)
            store(12, fine_ratio, xs_, yp[1:])
            store(16, -fine_ratio, xs_, ym[1:])

        received(SECOND)
        received_across(1)
        inner = pl.ds(0, band)
        for c in range(4):
            to_y, from_y = flux[12 + c, inner], flux[16 + c, inner]
            energy[c] = (
                summed(SECOND, comp(c)) + placed(x_row(8 + c), brow) + placed(x_row(12 + c), brow2)
            ) + (
                flux[c, inner] - flux[4 + c, inner] - flux[8 + c, inner] - to_y - from_y
                + pltpu.roll(flux[4 + c], 1, 0)[:band] + pltpu.roll(flux[8 + c], frame - 1, 0)[:band]
                + pltpu.roll(to_y, 1, 1) + pltpu.roll(from_y, ny - 1, 1)
            )
        rs, ux, uy, temp = physical_variables(energy)
        pmsg[1, comp(0)] = ux
        pmsg[1, comp(1)] = uy
        pmsg[1, comp(2)] = -0.5 / temp
        pmsg[1, comp(3)] = rs / temp * (1.0 / (1.0 + rfull[mid]))
        share(1, full)

        received(START)
        stepped = coarse(assembled(START, 16), band)
        for c in range(4):
            gs[c] = stepped[c]
            delta[c] = energy[c] - stepped[c]

        @pl.when(w == 0)
        def _():
            finish([gs[c] + delta[c] for c in range(4)])

    @pl.loop(0, chunks)
    def _(c):
        vx, vy0, half, _j = chunk_of(first, c)
        shift = ny - 1 - (ny - 2) * half
        ca = fine_ratio * jnp.abs(vx)
        for jj in range(HALF):
            k = c * HALF + jj
            cb = fine_ratio * jnp.abs(vy0 + jj * DVY)
            x = spad[k, main]
            star = (1.0 - ca - cb) * x + ca * spad[k, up] + cb * pltpu.roll(x, shift, 1)
            star2[k] = star * inv_main

    if nw > 1:

        @pl.when(is_owner & (w > 0))
        def _():
            settle(vin, win_recv.at[0])
            settle(vrow_in.at[1], win_recv.at[1])
            settle(vrow_in.at[0], win_recv.at[2])
            u = [
                jnp.concatenate(
                    [
                        vin[comp(c)],
                        jnp.where(row8 == TILE - 1, vrow_in[0, pl.ds(c, 1)], vrow_in[1, pl.ds(c, 1)]),
                    ],
                    axis=0,
                )
                for c in range(4)
            ]
            stepped = coarse(u, band)
            finish([stepped[c] + delta[c] for c in range(4)])

    def shared(n, size):
        rows = pl.ds(0, size)

        @pl.when(is_owner & (h == 1))
        def _():
            settle(pin.at[n, 0, rows], ag_recv.at[n])

        @pl.when(jnp.logical_not(is_owner & (h == 1)))
        def _():
            settle(pin.at[n, :, rows], ag_recv.at[n])

    shared(0, full + TILE)
    for n in range(4):
        for k in range(2):
            phys[n, pl.ds(2 * TILE + k * band, band)] = pin[0, k, comp(n)]
        phys[n, edge] = jnp.broadcast_to(pin[0, 1 - pos, pl.ds(full + n, 1)], (TILE, ny))
    for rows in (main, edge):
        drift, scale = phys[1, rows], phys[2, rows]
        for j in range(NVY):
            d = (-vel_max + (j + 0.5) * DVY) - drift
            e = jnp.exp(d * d * scale)
            yt[j, rows] = e
            if rows is main:
                yr[j] = pltpu.roll(e, ny - 1 if j < HALF else 1, 1)

    @pl.loop(0, chunks)
    def _(c):
        vx, vy0, half, j0 = chunk_of(first, c)
        shift = ny - 1 - (ny - 2) * half
        ca = fine_ratio * jnp.abs(vx)
        for rows in (main, edge):
            d = vx - phys[0, rows]
            xpad[rows] = phys[3, rows] * jnp.exp(d * d * phys[2, rows])
        x = xpad[main]
        here = inv_main * x
        behind = (ca * inv_main) * xpad[up]
        beside = inv_main * pltpu.roll(x, shift, 1)
        for jj in range(HALF):
            k = c * HALF + jj
            cb = fine_ratio * jnp.abs(vy0 + jj * DVY)
            star2[k] = (
                star2[k] + ((1.0 - ca - cb) * here) * yt[j0 + jj, main] + behind * yt[j0 + jj, up]
                + (cb * beside) * yr[j0 + jj]
            )

    shared(1, full)
    for k in range(2):
        rows = pl.ds(k * band, band)
        for n in range(4):
            e_phys[n, rows] = pin[1, k, comp(n)]
    drift, scale = e_phys[1], e_phys[2]
    for j in range(NVY):
        d = (-vel_max + (j + 0.5) * DVY) - drift
        ye[j] = jnp.exp(d * d * scale)
    shared(2, full)
    for k in range(2):
        for n in range(4):
            corr_out[n, pl.ds(k * band, band)] = pin[2, k, comp(n)]

    for field in range(3):
        size = pl.ds(0, sizes[field])
        for k in range(2):
            own = to_owner(s, k)[1]

            @pl.when(jnp.logical_not(own))
            def _():
                settle(msg.at[field, k, size], rs_send.at[field])

    for k in range(2):
        own = to_owner(other, k)[1]

        @pl.when(jnp.logical_not(own))
        def _():
            for part in range(2):
                settle(xmsg.at[k, ACROSS_ROWS[part]], rs_send.at[3 + part])

    @pl.when(is_owner)
    def _():
        for n, size in ((0, full + TILE), (1, full), (2, full)):
            rows = pl.ds(0, size)
            for _ in range(nv - 1):
                settle(pmsg.at[n, rows], ag_send.at[n])

            @pl.when(h == 0)
            def _():
                settle(pmsg.at[n, rows], ag_send.at[n])

        if nw > 1:

            @pl.when(w + 1 < nw)
            def _():
                settle(vmsg, win_send.at[0])
                settle(vrow.at[0], win_send.at[1])
                settle(vrow.at[1], win_send.at[2])


def lift_kernel(parts, star2, ye, e_phys, corr, lifted, corrected, yc, out, save_sem):
    count = star2.shape[0]
    first = lax.axis_index("vel") * count
    corrected[...] = corr[...]
    rs, uc, uy, temp = physical_variables(corr)
    sc = -0.5 / temp
    mc = rs / temp
    for j in range(NVY):
        d = (-vel_max + (j + 0.5) * DVY) - uy
        yc[j] = jnp.exp(d * d * sc)
    chunks = count // HALF
    per = chunks // parts

    def save(n):
        rows = pl.ds(n * per * HALF, per * HALF)
        return pltpu.make_async_copy(out.at[rows], lifted.at[rows], save_sem.at[n])

    for n in range(parts):

        @pl.loop(n * per, (n + 1) * per)
        def _(c):
            vx, _vy, _half, j0 = chunk_of(first, c)
            dc = vx - uc
            xc = mc * jnp.exp(dc * dc * sc)
            de = vx - e_phys[0]
            xe = e_phys[3] * jnp.exp(de * de * e_phys[2])
            for jj in range(HALF):
                k = c * HALF + jj
                out[k] = star2[k] + (xc * yc[j0 + jj] - xe * ye[j0 + jj])

        save(n).start()
    for n in range(parts):
        save(n).wait()


def per_device(nw, nv, f_start, relax_rate):
    field = f_start[0]
    count, nx, ny = field.shape
    band = nx // 2
    frame = band + TILE
    full = 4 * band
    pad = nx + 4 * TILE
    vmem = pltpu.VMEM
    dma = pltpu.SemaphoreType.DMA
    small = jax.ShapeDtypeStruct((4, nx, ny), f32)
    speeds = jax.ShapeDtypeStruct((NVY, nx, ny), f32)
    in_vmem = pl.BlockSpec(memory_space=pltpu.VMEM)
    in_hbm = pl.BlockSpec(memory_space=pltpu.HBM)
    field = pltpu.with_memory_space_constraint(field, pltpu.HBM)
    star2, ye, e_phys, corr = pl.pallas_call(
        functools.partial(advance_kernel, nw, nv),
        out_shape=(jax.ShapeDtypeStruct((count, nx, ny), f32), speeds, small, small),
        in_specs=[in_hbm, in_hbm],
        out_specs=(in_vmem,) * 4,
        scratch_shapes=[
            vmem((count, pad, ny), f32),
            vmem((count, pad, ny), f32),
            vmem((2 * nx, ny), f32),
            vmem((2, len(ORDERS), pad, ny), f32),
            vmem((2, len(ORDERS), pad, ny), f32),
            vmem((2, 4, TILE, ny), f32),
            vmem((3, 2, full + TILE, ny), f32),
            vmem((2, 3 * TILE, ny), f32),
            vmem((3, nv, full + TILE, ny), f32),
            vmem((nv, 3 * TILE, ny), f32),
            vmem((3 * TILE, ny), f32),
            vmem((TILE, ny), f32),
            vmem((4, frame, ny), f32),
            vmem((20, frame, ny), f32),
            vmem((4, band, ny), f32),
            vmem((4, band, ny), f32),
            vmem((4, band, ny), f32),
            vmem((3, full + TILE, ny), f32),
            vmem((3, 2, full + TILE, ny), f32),
            vmem((full, ny), f32),
            vmem((2, TILE, ny), f32),
            vmem((full, ny), f32),
            vmem((2, TILE, ny), f32),
            vmem((4, pad, ny), f32),
            vmem((pad, ny), f32),
            vmem((NVY, pad, ny), f32),
            vmem((NVY, nx, ny), f32),
            dma((1 + nx // TILE,)), dma((2,)), dma((2,)), dma((5,)), dma((5,)), dma((3,)), dma((3,)),
            dma((3,)), dma((3,)),
        ],
        compiler_params=pltpu.CompilerParams(
            collective_id=0, has_side_effects=True, vmem_limit_bytes=40 << 20
        ),
        name="advance",
    )(field, pltpu.with_memory_space_constraint(relax_rate, pltpu.HBM))

    chunks = count // HALF
    parts = next(n for n in (6, 4, 3, 2, 1) if chunks % n == 0)
    lifted, corrected = pl.pallas_call(
        functools.partial(lift_kernel, parts),
        out_shape=(jax.ShapeDtypeStruct((count, nx, ny), f32), small),
        in_specs=[in_vmem] * 4,
        out_specs=(in_hbm, in_vmem),
        scratch_shapes=[
            vmem((NVY, nx, ny), f32), vmem((count, nx, ny), f32), dma((parts,)),
        ],
        compiler_params=pltpu.CompilerParams(vmem_limit_bytes=16 << 20),
        name="lift",
    )(star2, ye, e_phys, corr)
    return corrected[None], lifted[None]


def solution(mesh):
    return jax.shard_map(
        functools.partial(per_device, mesh.shape["win"], mesh.shape["vel"]),
        mesh=mesh,
        in_specs=(P("win", "vel", "sp", None), P("sp", None)),
        out_specs=(P("win", None, "sp", None), P("win", "vel", "sp", None)),
        check_vma=False,
    )
```

```python
import functools
import math

import jax
import jax.numpy as jnp
from jax import lax
from jax.experimental import pallas as pl
from jax.experimental.pallas import tpu as pltpu
from jax.sharding import PartitionSpec as P

NVX = 48
NVY = 32
HALF = NVY // 2
TILE = 8
vel_max = 6.0
fine_ratio = 0.075
coarse_ratio = 0.15
density_floor = 0.3
thermal_lower_bound = 0.3
DVX = 2.0 * vel_max / NVX
DVY = 2.0 * vel_max / NVY
WEIGHT = DVX * DVY / (2.0 * math.pi)
MESH = pl.DeviceIdType.MESH
f32 = jnp.float32
ORDERS = [(p, q) for p in range(5) for q in range(5 - p)]
PLACE = {order: n for n, order in enumerate(ORDERS)}
MAIN = [(0, 0), (0, 1), (1, 0), (0, 2), (2, 0)]
FIRST, START, SECOND = range(3)


def physical_variables(u):
    rs = jnp.maximum(u[0], density_floor)
    ux = u[1] / rs
    uy = u[2] / rs
    temp = jnp.maximum((u[3] - 0.5 * (u[1] * ux + u[2] * uy)) / rs, thermal_lower_bound)
    return rs, ux, uy, temp


def chunk_of(first, c):
    k = first + c * HALF
    i = k // NVY
    j = k % NVY
    vx = -vel_max + (i.astype(f32) + 0.5) * DVX
    vy = -vel_max + (j.astype(f32) + 0.5) * DVY
    return vx, vy, j // HALF, j


def coarse(u, band):
    rows, ny = u[0].shape
    rs, ux, uy, temp = physical_variables(u)
    p = rs * temp
    wave = jnp.sqrt(2.0 * temp)
    fx = [u[1], u[1] * ux + p, u[2] * ux, (u[3] + p) * ux]
    fy = [u[2], u[1] * uy, u[2] * uy + p, (u[3] + p) * uy]
    sx = jnp.abs(ux) + wave
    sy = jnp.abs(uy) + wave
    mx = jnp.maximum(sx, pltpu.roll(sx, rows - 1, 0))
    my = jnp.maximum(sy, pltpu.roll(sy, ny - 1, 1))
    out = []
    for c in range(4):
        face_x = 0.5 * (fx[c] + pltpu.roll(fx[c], rows - 1, 0)) - 0.5 * mx * (
            pltpu.roll(u[c], rows - 1, 0) - u[c]
        )
        face_y = 0.5 * (fy[c] + pltpu.roll(fy[c], ny - 1, 1)) - 0.5 * my * (
            pltpu.roll(u[c], ny - 1, 1) - u[c]
        )
        g = u[c] - coarse_ratio * (
            face_x - pltpu.roll(face_x, 1, 0) + (face_y - pltpu.roll(face_y, 1, 1))
        )
        out.append(g[:band])
    return out


def advance_kernel(
    nw, nv,
    f, r, star2, ye, e_phys, corr_out,
    fpad, spad, rfull, bsum, hsum, gout, msg, xmsg, red, redx, xs, es, fr, flux, energy, delta, gs,
    pmsg, pin, vmsg, vrow, vin, vrow_in, chain, chain_rows, phys, xpad, yt, yr,
    load_sem, halo_send, halo_recv, rs_send, rs_recv, ag_send, ag_recv, win_send, win_recv,
    chain_send, chain_recv, ready,
):
    w, v, s = lax.axis_index("win"), lax.axis_index("vel"), lax.axis_index("sp")
    count, nx, ny = f.shape
    chunks = count // HALF
    first = v * count
    other = 1 - s
    pos = (2 * v) // nv
    band = nx // 2
    frame = band + TILE
    full = 4 * band
    main = pl.ds(2 * TILE, nx)
    end = 2 * TILE + nx
    up = pl.ds(2 * TILE + 1 - 2 * pos, nx)
    hb = pl.multiple_of(end - (end - TILE) * pos, TILE)
    edge = pl.ds(hb, TILE)
    edge_up = pl.ds(hb + 1 - 2 * pos, TILE)
    ho = pl.multiple_of(TILE + (end - TILE) * pos, TILE)
    away = pl.ds(ho, TILE)
    away_up = pl.ds(ho + 1 - 2 * pos, TILE)
    tiles = nx // TILE

    base = nv // 2 - 2
    off = v - base
    is_owner = (s == 1) & (off >= 0) & (off < 4)
    b = off // 2
    h = (off + b) % 2
    g = 2 * h + b

    def owner_at(half, k):
        return base + (half if k == 0 else 3 - half)

    def load_f(t):
        rows = pl.ds(pl.multiple_of(t * TILE, TILE), TILE)
        padded = pl.ds(pl.multiple_of((t + 2) * TILE, TILE), TILE)
        return pltpu.make_async_copy(f.at[:, rows], fpad.at[:, padded], load_sem.at[t])

    for t in range(tiles):
        load_f(t).start()
    mine = pl.ds(pl.multiple_of(s * nx, TILE), nx)
    load_r = pltpu.make_async_copy(r, rfull.at[mine], load_sem.at[tiles])
    load_r.start()

    def signal(device):
        pl.semaphore_signal(barrier, inc=1, device_id=device, device_id_type=MESH)

    barrier = pltpu.get_barrier_semaphore()
    signal((w, v, other))
    for o in range(4):

        @pl.when(jnp.logical_not((v == base + o) & (s == 1)))
        def _():
            signal((w, base + o, 1))

    @pl.when(is_owner)
    def _():
        signal((w, v, 0))
        for d in range(1, nv):
            for half in range(2):
                signal((w, lax.rem(v + d, nv), half))

        @pl.when(w + 1 < nw)
        def _():
            for n in range(nv):
                for half in range(2):
                    signal((w + 1, n, half))

    def remote(src, dst, send, recv, device):
        return pltpu.make_async_remote_copy(
            src_ref=src, dst_ref=dst, send_sem=send, recv_sem=recv,
            device_id=device, device_id_type=MESH,
        )

    def settle(ref, sem):
        pltpu.make_async_copy(ref, ref, sem).wait()

    empty = jnp.zeros((TILE, ny), f32)
    for side in range(2):
        for n in range(len(ORDERS)):
            for at in (TILE, end):
                bsum[side, n, pl.ds(at, TILE)] = empty
                hsum[side, n, pl.ds(at, TILE)] = empty

    parity = (first // HALF) % 2
    rounds = (chunks + 1) // 2

    @pl.loop(0, tiles)
    def _(t):
        load_f(t).wait()
        rows = pl.ds(pl.multiple_of(2 * TILE + t * TILE, TILE), TILE)
        for side in range(2):
            acc = {order: jnp.zeros((TILE, ny), f32) for order in ORDERS}
            for n in range(rounds):
                c = (side + parity) % 2 + 2 * n
                weight = 1.0
                if chunks % 2:
                    weight = jnp.where(c < chunks, 1.0, 0.0).astype(f32)
                    c = jnp.minimum(c, chunks - 1)
                vx = chunk_of(first, c)[0]
                sums = [jnp.zeros((TILE, ny), f32)] * 5
                for jj in range(HALF // 2, HALF):
                    tt = (jj + 0.5) * DVY - 0.5 * vel_max
                    high = fpad[c * HALF + jj, rows]
                    low = fpad[c * HALF + HALF - 1 - jj, rows]
                    even, odd = high + low, high - low
                    sums = [
                        sums[0] + even, sums[1] + tt * odd, sums[2] + tt**2 * even,
                        sums[3] + tt**3 * odd, sums[4] + tt**4 * even,
                    ]
                power = weight
                for q in range(5):
                    for m in range(5 - q):
                        term = sums[m] if q == 0 and chunks % 2 == 0 else sums[m] * power
                        acc[m, q] = acc[m, q] + term
                    power = power * vx
            centre = (side - 0.5) * vel_max
            for p, q in ORDERS:
                total = acc[p, q]
                for m in range(p):
                    total = total + (math.comb(p, m) * centre ** (p - m)) * acc[m, q]
                bsum[side, PLACE[p, q], rows] = total

    def components(get):
        return [
            WEIGHT * get(0, 0), WEIGHT * get(0, 1), WEIGHT * get(1, 0),
            (0.5 * WEIGHT) * (get(0, 2) + get(2, 0)),
        ]

    def fill(field, values):
        for c in range(4):
            for k in range(2):
                msg[field, k, pl.ds(c * band, band)] = values[c][k * band : (k + 1) * band]

    def fill_edges(field):
        for c in range(4):
            for k in range(2):
                if field == FIRST:
                    outer = gout[0, c, pl.ds(TILE - 1 if k == 0 else 0, 1)]
                else:
                    outer = jnp.zeros((1, ny), f32)
                msg[field, k, pl.ds(full + c, 1)] = outer
                inner = c * band if k == 0 else (c + 1) * band - 1
                msg[field, k, pl.ds(full + 4 + c, 1)] = msg[field, 1 - k, pl.ds(inner, 1)]

    def to_owner(half, k):
        target = owner_at(half, k)
        return target, (v == target) & (s == 1)

    sizes = {FIRST: full + TILE, START: full + TILE, SECOND: full}

    def scatter(field):
        size = pl.ds(0, sizes[field])
        for k in range(2):
            target, own = to_owner(s, k)

            @pl.when(own)
            def _():
                red[field, v, size] = msg[field, k, size]

            @pl.when(jnp.logical_not(own))
            def _():
                remote(
                    msg.at[field, k, size], red.at[field, v, size],
                    rs_send.at[field], rs_recv.at[field], (w, target, 1),
                ).start()

    ACROSS_ROWS = (pl.ds(0, TILE), pl.ds(TILE, 2 * TILE))

    def scatter_across(part):
        rows = ACROSS_ROWS[part]
        for k in range(2):
            target, own = to_owner(other, k)

            @pl.when(own)
            def _():
                redx[v, rows] = xmsg[k, rows]

            @pl.when(jnp.logical_not(own))
            def _():
                remote(
                    xmsg.at[k, rows], redx.at[v, rows],
                    rs_send.at[3 + part], rs_recv.at[3 + part], (w, target, 1),
                ).start()

    fill(START, components(lambda p, q: bsum[0, PLACE[p, q], main] + bsum[1, PLACE[p, q], main]))
    fill_edges(START)

    pl.semaphore_wait(barrier, jnp.where(is_owner, 2 * nv + 3, 5) + jnp.where(w > 0, 4, 0))

    @pl.when(w > 0)
    def _():
        for o in range(4):
            pl.semaphore_signal(ready, inc=1, device_id=(w - 1, base + o, 1), device_id_type=MESH)

    load_r.wait()
    source = pl.ds(pl.multiple_of((nx - TILE) * pos, TILE), TILE)
    halo_r = remote(r, rfull.at[mine], halo_send.at[0], halo_recv.at[0], (w, v, other))
    halo_f = remote(f.at[:, source], fpad.at[:, edge], halo_send.at[1], halo_recv.at[1], (w, v, other))
    halo_r.start()
    halo_f.start()

    inv_main = 1.0 / (1.0 + rfull[mine])
    along = fine_ratio * (2 * pos - 1).astype(f32)
    ACROSS = ((-fine_ratio, ny - 1), (fine_ratio, 1))

    def moved(table, side, p, q, rows, rows_up):
        across, shift = ACROSS[side]
        bx = table[side, PLACE[p, q + 1], rows]
        by = table[side, PLACE[p + 1, q], rows]
        return (
            table[side, PLACE[p, q], rows]
            + along * (table[side, PLACE[p, q + 1], rows_up] - bx)
            + across * (pltpu.roll(by, shift, 1) - by)
        )

    star_main, star_away = {}, {}

    def one_step(side, p, q):
        star = moved(bsum, side, p, q, main, up)
        beyond = moved(bsum, side, p, q, away, away_up)
        hsum[side, PLACE[p, q], main] = star * inv_main
        hsum[side, PLACE[p, q], away] = beyond
        return star, beyond

    for order in MAIN:
        parts = [one_step(side, *order) for side in range(2)]
        star_main[order] = parts[0][0] + parts[1][0]
        star_away[order] = parts[0][1] + parts[1][1]
    fill(FIRST, components(lambda p, q: star_main[p, q]))
    for c, value in enumerate(components(lambda p, q: star_away[p, q])):
        gout[0, c] = value
    fill_edges(FIRST)
    for k in range(2):
        last = band - 1 if k == 0 else 0
        for c in range(4):
            xmsg[k, pl.ds(c, 1)] = msg[FIRST, 1 - k, pl.ds(c * band + last, 1)]
            xmsg[k, pl.ds(4 + c, 1)] = gout[0, c, pl.ds(0 if k == 0 else TILE - 1, 1)]
    scatter_across(0)
    scatter(FIRST)
    for p, q in ORDERS:
        if p + q < 4 and (p, q) not in MAIN:
            for side in range(2):
                one_step(side, p, q)
    again = {o: moved(hsum, 0, *o, main, up) + moved(hsum, 1, *o, main, up) for o in MAIN}
    fill(SECOND, components(lambda p, q: again[p, q]))
    scatter(SECOND)

    halo_r.wait()
    theirs = other * nx
    inv_away = 1.0 / (1.0 + rfull[pl.ds(theirs + (nx - 1) * (1 - pos), 1)])
    inv_edge = 1.0 / (1.0 + rfull[pl.ds(pl.multiple_of(theirs + (nx - TILE) * pos, TILE), TILE)])
    for side in range(2):
        for p, q in ORDERS:
            if p + q < 4:
                hsum[side, PLACE[p, q], away] = hsum[side, PLACE[p, q], away] * inv_away
    again = {o: moved(hsum, 0, *o, away, away_up) + moved(hsum, 1, *o, away, away_up) for o in MAIN}
    for c, value in enumerate(components(lambda p, q: again[p, q])):
        gout[1, c] = value
    for k in range(2):
        last = band - 1 if k == 0 else 0
        near, far = (0, 1) if k == 0 else (TILE - 1, TILE - 2)
        for c in range(4):
            xmsg[k, pl.ds(8 + c, 1)] = gout[1, c, pl.ds(near, 1)]
            xmsg[k, pl.ds(12 + c, 1)] = gout[1, c, pl.ds(far, 1)]
            xmsg[k, pl.ds(16 + c, 1)] = msg[START, 1 - k, pl.ds(c * band + last, 1)]
            xmsg[k, pl.ds(20 + c, 1)] = jnp.zeros((1, ny), f32)
    scatter_across(1)
    scatter(START)
    halo_f.wait()

    @pl.loop(0, chunks)
    def _(c):
        vx, vy0, half, _j = chunk_of(first, c)
        shift = ny - 1 - (ny - 2) * half
        ca = fine_ratio * jnp.abs(vx)
        for jj in range(HALF):
            k = c * HALF + jj
            cb = fine_ratio * jnp.abs(vy0 + jj * DVY)
            cc = 1.0 - ca - cb
            x = fpad[k, main]
            spad[k, main] = (cc * x + ca * fpad[k, up] + cb * pltpu.roll(x, shift, 1)) * inv_main
            x = fpad[k, edge]
            spad[k, edge] = (cc * x + ca * fpad[k, edge_up] + cb * pltpu.roll(x, shift, 1)) * inv_edge

    row8 = lax.broadcasted_iota(jnp.int32, (TILE, ny), 0)
    row_band = lax.broadcasted_iota(jnp.int32, (band, ny), 0)
    brow = (band - 1) * b
    brow2 = 1 + (band - 3) * b

    def received(field):
        size = pl.ds(0, sizes[field])

        @pl.when(h == 1)
        def _():
            settle(red.at[field, pl.ds(0, nv - 1), size], rs_recv.at[field])

        @pl.when(h == 0)
        def _():
            settle(red.at[field, :, size], rs_recv.at[field])

    def summed(field, rows):
        total = red[field, 0, rows]
        for n in range(1, nv):
            total = total + red[field, n, rows]
        return total

    def comp(c):
        return pl.ds(c * band, band)

    def framed(value, outer, inner):
        above = jnp.where(b == 0, outer, inner)
        below = jnp.where(b == 0, inner, outer)
        return jnp.concatenate([value, jnp.where(row8 == TILE - 1, above, below)], axis=0)

    def placed(row, at):
        return jnp.where(row_band == at, row, 0.0)

    def share(n, size):
        rows = pl.ds(0, size)

        @pl.when(h == 1)
        def _():
            pin[n, b, rows] = pmsg[n, rows]

        @pl.when(h == 0)
        def _():
            remote(
                pmsg.at[n, rows], pin.at[n, b, rows], ag_send.at[n], ag_recv.at[n], (w, v, 0)
            ).start()

        for d in range(1, nv):
            remote(
                pmsg.at[n, rows], pin.at[n, b, rows], ag_send.at[n], ag_recv.at[n],
                (w, lax.rem(v + d, nv), h),
            ).start()

    def place(n):
        half, k = n // 2, n % 2
        return base + half + k * (3 - 2 * half)

    def along_chain():
        after, before = lax.rem(g + 1, 4), lax.rem(g + 3, 4)
        return [
            remote(vmsg, chain, chain_send.at[0], chain_recv.at[0], (w + 1, v, 1)),
            remote(vrow.at[0], chain_rows.at[1], chain_send.at[1], chain_recv.at[1], (w + 1, place(before), 1)),
            remote(vrow.at[1], chain_rows.at[0], chain_send.at[2], chain_recv.at[2], (w + 1, place(after), 1)),
        ]

    def hand_on(values):
        for c in range(4):
            vmsg[comp(c)] = values[c]
            for row, value in ((0, values[c][:1]), (1, values[c][-1:])):
                vrow[row, pl.ds(c, 1)] = value
                vrow[row, pl.ds(4 + c, 1)] = value
        pl.semaphore_wait(ready, 2 * nv)

        @pl.when(w + 2 < nw)
        def _():
            for copy in along_chain():
                copy.start()

        for d in range(nv):
            to = lax.rem(v + d, nv)
            remote(vrow.at[b], vrow_in.at[b], win_send.at[0], win_recv.at[0], (w + 1, to, 1 - h)).start()
        for d in range(nv):
            to = lax.rem(v + d, nv)
            remote(vmsg, vin.at[b], win_send.at[1], win_recv.at[1], (w + 1, to, h)).start()

    @pl.when(is_owner)
    def _():
        def received_across(part):
            rows = ACROSS_ROWS[part]

            @pl.when(h == 1)
            def _():
                settle(redx.at[:, rows], rs_recv.at[3 + part])

            @pl.when(h == 0)
            def _():
                settle(redx.at[pl.ds(0, nv - 1), rows], rs_recv.at[3 + part])

            across = redx[0, rows]
            for n in range(1, nv):
                across = across + redx[n, rows]
            xs[rows] = across

        received(FIRST)
        received_across(0)

        def x_row(n):
            return xs[pl.ds(n, 1)]

        def assembled(field, at):
            es[...] = summed(field, pl.ds(full, TILE))
            out = []
            for c in range(4):
                value = summed(field, comp(c))
                if field == FIRST:
                    value = value + placed(x_row(4 + c), brow)
                out.append(framed(value, es[pl.ds(c, 1)] + x_row(at + c), es[pl.ds(4 + c, 1)]))
            return out

        rs, ux, uy, temp = physical_variables(assembled(FIRST, 0))
        rows_all = 2 * nx
        mid = pl.ds(pl.multiple_of(g * band, TILE), band)
        above = rfull[pl.ds(lax.rem(g * band + rows_all - 1, rows_all), 1)]
        below = rfull[pl.ds(lax.rem(g * band + band, rows_all), 1)]
        rate = jnp.concatenate([rfull[mid], jnp.where(row8 == TILE - 1, above, below)], axis=0)
        fr[0] = ux
        fr[1] = uy
        fr[2] = -0.5 / temp
        fr[3] = rs / temp * (rate / (1.0 + rate))
        for n in range(4):
            pmsg[0, comp(n)] = fr[n, pl.ds(0, band)]
            outer = fr[n, pl.ds(band + (TILE - 1) * (1 - b), 1)]
            pmsg[0, pl.ds(full + n, 1)] = outer
            pmsg[0, pl.ds(full + 4 + n, 1)] = outer
        share(0, full + TILE)

        @pl.loop(0, frame // TILE)
        def _(t):
            rows = pl.ds(pl.multiple_of(t * TILE, TILE), TILE)
            ux, uy, scale, amp = [fr[n, rows] for n in range(4)]

            def half_sums(speeds, drift):
                weights = []
                for speed in speeds:
                    d = speed - drift
                    weights.append(jnp.exp(d * d * scale))
                sides = []
                half = len(speeds) // 2
                for at, c in ((half, 0.5 * vel_max), (0, -0.5 * vel_max)):
                    m = [empty] * 4
                    for n in range(half // 2, half):
                        t = speeds[at + n] - c
                        high, low = weights[at + n], weights[at + half - 1 - n]
                        even, odd = high + low, high - low
                        m = [m[0] + even, m[1] + t * odd, m[2] + t**2 * even, m[3] + t**3 * odd]
                    sides.append([
                        m[0],
                        m[1] + c * m[0],
                        m[2] + (2 * c) * m[1] + c**2 * m[0],
                        m[3] + (3 * c) * m[2] + (3 * c**2) * m[1] + c**3 * m[0],
                    ])
                return sides

            xp, xm = half_sums([-vel_max + (i + 0.5) * DVX for i in range(NVX)], ux)
            yp, ym = half_sums([-vel_max + (j + 0.5) * DVY for j in range(NVY)], uy)
            xs_ = [x + y for x, y in zip(xp, xm)]
            ys_ = [x + y for x, y in zip(yp, ym)]
            amp = WEIGHT * amp

            def store(n, coef, x, y):
                x = [coef * amp * t for t in x]
                flux[n, rows] = x[0] * y[0]
                flux[n + 1, rows] = x[1] * y[0]
                flux[n + 2, rows] = x[0] * y[1]
                flux[n + 3, rows] = 0.5 * (x[2] * y[0] + x[0] * y[2])

            store(0, 1.0, xs_, ys_)
            store(4, fine_ratio, xp[1:], ys_)
            store(8, -fine_ratio, xm[1:], ys_)
            store(12, fine_ratio, xs_, yp[1:])
            store(16, -fine_ratio, xs_, ym[1:])

        received(SECOND)
        received_across(1)
        inner = pl.ds(0, band)
        for c in range(4):
            to_y, from_y = flux[12 + c, inner], flux[16 + c, inner]
            energy[c] = (
                summed(SECOND, comp(c)) + placed(x_row(8 + c), brow) + placed(x_row(12 + c), brow2)
            ) + (
                flux[c, inner] - flux[4 + c, inner] - flux[8 + c, inner] - to_y - from_y
                + pltpu.roll(flux[4 + c], 1, 0)[:band] + pltpu.roll(flux[8 + c], frame - 1, 0)[:band]
                + pltpu.roll(to_y, 1, 1) + pltpu.roll(from_y, ny - 1, 1)
            )
        rs, ux, uy, temp = physical_variables(energy)
        pmsg[1, comp(0)] = ux
        pmsg[1, comp(1)] = uy
        pmsg[1, comp(2)] = -0.5 / temp
        pmsg[1, comp(3)] = rs / temp * (1.0 / (1.0 + rfull[mid]))
        share(1, full)

        received(START)
        stepped = coarse(assembled(START, 16), band)
        for c in range(4):
            gs[c] = stepped[c]
            delta[c] = energy[c] - stepped[c]

        for c in range(4):
            corrected = gs[c] + delta[c]
            energy[c] = corrected
            pmsg[2, comp(c)] = jnp.where(w == 0, corrected, delta[c])
        share(2, full)
        if nw > 1:

            @pl.when(w == 0)
            def _():
                hand_on([energy[c] for c in range(4)])

    @pl.loop(0, chunks)
    def _(c):
        vx, vy0, half, _j = chunk_of(first, c)
        shift = ny - 1 - (ny - 2) * half
        ca = fine_ratio * jnp.abs(vx)
        for jj in range(HALF):
            k = c * HALF + jj
            cb = fine_ratio * jnp.abs(vy0 + jj * DVY)
            x = spad[k, main]
            star = (1.0 - ca - cb) * x + ca * spad[k, up] + cb * pltpu.roll(x, shift, 1)
            star2[k] = star * inv_main

    if nw > 2:

        @pl.when(is_owner & (w > 0) & (w + 1 < nw))
        def _():
            settle(chain, chain_recv.at[0])
            settle(chain_rows.at[1], chain_recv.at[1])
            settle(chain_rows.at[0], chain_recv.at[2])
            u = [
                jnp.concatenate(
                    [
                        chain[comp(c)],
                        jnp.where(
                            row8 == TILE - 1, chain_rows[0, pl.ds(c, 1)], chain_rows[1, pl.ds(c, 1)]
                        ),
                    ],
                    axis=0,
                )
                for c in range(4)
            ]
            stepped = coarse(u, band)
            hand_on([stepped[c] + delta[c] for c in range(4)])

    def shared(n, size):
        rows = pl.ds(0, size)

        @pl.when(is_owner & (h == 1))
        def _():
            settle(pin.at[n, 0, rows], ag_recv.at[n])

        @pl.when(jnp.logical_not(is_owner & (h == 1)))
        def _():
            settle(pin.at[n, :, rows], ag_recv.at[n])

    shared(0, full + TILE)
    for n in range(4):
        for k in range(2):
            phys[n, pl.ds(2 * TILE + k * band, band)] = pin[0, k, comp(n)]
        phys[n, edge] = jnp.broadcast_to(pin[0, 1 - pos, pl.ds(full + n, 1)], (TILE, ny))
    for rows in (main, edge):
        drift, scale = phys[1, rows], phys[2, rows]
        for j in range(NVY):
            d = (-vel_max + (j + 0.5) * DVY) - drift
            e = jnp.exp(d * d * scale)
            yt[j, rows] = e
            if rows is main:
                yr[j] = pltpu.roll(e, ny - 1 if j < HALF else 1, 1)

    @pl.loop(0, chunks)
    def _(c):
        vx, vy0, half, j0 = chunk_of(first, c)
        shift = ny - 1 - (ny - 2) * half
        ca = fine_ratio * jnp.abs(vx)
        for rows in (main, edge):
            d = vx - phys[0, rows]
            xpad[rows] = phys[3, rows] * jnp.exp(d * d * phys[2, rows])
        x = xpad[main]
        here = inv_main * x
        behind = (ca * inv_main) * xpad[up]
        beside = inv_main * pltpu.roll(x, shift, 1)
        for jj in range(HALF):
            k = c * HALF + jj
            cb = fine_ratio * jnp.abs(vy0 + jj * DVY)
            star2[k] = (
                star2[k] + ((1.0 - ca - cb) * here) * yt[j0 + jj, main] + behind * yt[j0 + jj, up]
                + (cb * beside) * yr[j0 + jj]
            )

    shared(1, full)
    for k in range(2):
        rows = pl.ds(k * band, band)
        for n in range(4):
            e_phys[n, rows] = pin[1, k, comp(n)]
    drift, scale = e_phys[1], e_phys[2]
    for j in range(NVY):
        d = (-vel_max + (j + 0.5) * DVY) - drift
        ye[j] = jnp.exp(d * d * scale)
    shared(2, full)
    for k in range(2):
        for n in range(4):
            corr_out[n, pl.ds(k * band, band)] = pin[2, k, comp(n)]
    if nw > 1:

        @pl.when(w > 0)
        def _():
            settle(vrow_in, win_recv.at[0])
            settle(vin, win_recv.at[1])
            u = [
                jnp.concatenate(
                    [
                        vin[0, comp(c)], vin[1, comp(c)],
                        jnp.where(row8 == TILE - 1, vrow_in[1, pl.ds(c, 1)], vrow_in[0, pl.ds(c, 1)]),
                    ],
                    axis=0,
                )
                for c in range(4)
            ]
            stepped = coarse(u, nx)
            for c in range(4):
                corr_out[c] = stepped[c] + corr_out[c]

    for field in range(3):
        size = pl.ds(0, sizes[field])
        for k in range(2):
            own = to_owner(s, k)[1]

            @pl.when(jnp.logical_not(own))
            def _():
                settle(msg.at[field, k, size], rs_send.at[field])

    for k in range(2):
        own = to_owner(other, k)[1]

        @pl.when(jnp.logical_not(own))
        def _():
            for part in range(2):
                settle(xmsg.at[k, ACROSS_ROWS[part]], rs_send.at[3 + part])

    @pl.when(is_owner)
    def _():
        for n, size in ((0, full + TILE), (1, full), (2, full)):
            rows = pl.ds(0, size)
            for _ in range(nv - 1):
                settle(pmsg.at[n, rows], ag_send.at[n])

            @pl.when(h == 0)
            def _():
                settle(pmsg.at[n, rows], ag_send.at[n])

        if nw > 1:

            @pl.when(w + 1 < nw)
            def _():
                for _ in range(nv):
                    settle(vrow.at[b], win_send.at[0])
                    settle(vmsg, win_send.at[1])

            @pl.when(w + 2 < nw)
            def _():
                settle(vmsg, chain_send.at[0])
                settle(vrow.at[0], chain_send.at[1])
                settle(vrow.at[1], chain_send.at[2])


def lift_kernel(parts, star2, ye, e_phys, corr, lifted, corrected, yc, out, save_sem):
    count = star2.shape[0]
    first = lax.axis_index("vel") * count
    corrected[...] = corr[...]
    rs, uc, uy, temp = physical_variables(corr)
    sc = -0.5 / temp
    mc = rs / temp
    for j in range(NVY):
        d = (-vel_max + (j + 0.5) * DVY) - uy
        yc[j] = jnp.exp(d * d * sc)
    chunks = count // HALF
    per = chunks // parts

    def save(n):
        rows = pl.ds(n * per * HALF, per * HALF)
        return pltpu.make_async_copy(out.at[rows], lifted.at[rows], save_sem.at[n])

    for n in range(parts):

        @pl.loop(n * per, (n + 1) * per)
        def _(c):
            vx, _vy, _half, j0 = chunk_of(first, c)
            dc = vx - uc
            xc = mc * jnp.exp(dc * dc * sc)
            de = vx - e_phys[0]
            xe = e_phys[3] * jnp.exp(de * de * e_phys[2])
            for jj in range(HALF):
                k = c * HALF + jj
                out[k] = star2[k] + (xc * yc[j0 + jj] - xe * ye[j0 + jj])

        save(n).start()
    for n in range(parts):
        save(n).wait()


def per_device(nw, nv, f_start, relax_rate):
    field = f_start[0]
    count, nx, ny = field.shape
    band = nx // 2
    frame = band + TILE
    full = 4 * band
    pad = nx + 4 * TILE
    vmem = pltpu.VMEM
    dma = pltpu.SemaphoreType.DMA
    small = jax.ShapeDtypeStruct((4, nx, ny), f32)
    speeds = jax.ShapeDtypeStruct((NVY, nx, ny), f32)
    in_vmem = pl.BlockSpec(memory_space=pltpu.VMEM)
    in_hbm = pl.BlockSpec(memory_space=pltpu.HBM)
    field = pltpu.with_memory_space_constraint(field, pltpu.HBM)
    star2, ye, e_phys, corr = pl.pallas_call(
        functools.partial(advance_kernel, nw, nv),
        out_shape=(jax.ShapeDtypeStruct((count, nx, ny), f32), speeds, small, small),
        in_specs=[in_hbm, in_hbm],
        out_specs=(in_vmem,) * 4,
        scratch_shapes=[
            vmem((count, pad, ny), f32),
            vmem((count, pad, ny), f32),
            vmem((2 * nx, ny), f32),
            vmem((2, len(ORDERS), pad, ny), f32),
            vmem((2, len(ORDERS), pad, ny), f32),
            vmem((2, 4, TILE, ny), f32),
            vmem((3, 2, full + TILE, ny), f32),
            vmem((2, 3 * TILE, ny), f32),
            vmem((3, nv, full + TILE, ny), f32),
            vmem((nv, 3 * TILE, ny), f32),
            vmem((3 * TILE, ny), f32),
            vmem((TILE, ny), f32),
            vmem((4, frame, ny), f32),
            vmem((20, frame, ny), f32),
            vmem((4, band, ny), f32),
            vmem((4, band, ny), f32),
            vmem((4, band, ny), f32),
            vmem((3, full + TILE, ny), f32),
            vmem((3, 2, full + TILE, ny), f32),
            vmem((full, ny), f32),
            vmem((2, TILE, ny), f32),
            vmem((2, full, ny), f32),
            vmem((2, TILE, ny), f32),
            vmem((full, ny), f32),
            vmem((2, TILE, ny), f32),
            vmem((4, pad, ny), f32),
            vmem((pad, ny), f32),
            vmem((NVY, pad, ny), f32),
            vmem((NVY, nx, ny), f32),
            dma((1 + nx // TILE,)), dma((2,)), dma((2,)), dma((5,)), dma((5,)), dma((3,)), dma((3,)),
            dma((2,)), dma((2,)), dma((3,)), dma((3,)), pltpu.SemaphoreType.REGULAR,
        ],
        compiler_params=pltpu.CompilerParams(
            collective_id=0, has_side_effects=True, vmem_limit_bytes=40 << 20
        ),
        name="advance",
    )(field, pltpu.with_memory_space_constraint(relax_rate, pltpu.HBM))

    chunks = count // HALF
    parts = next(n for n in (6, 4, 3, 2, 1) if chunks % n == 0)
    lifted, corrected = pl.pallas_call(
        functools.partial(lift_kernel, parts),
        out_shape=(jax.ShapeDtypeStruct((count, nx, ny), f32), small),
        in_specs=[in_vmem] * 4,
        out_specs=(in_hbm, in_vmem),
        scratch_shapes=[
            vmem((NVY, nx, ny), f32), vmem((count, nx, ny), f32), dma((parts,)),
        ],
        compiler_params=pltpu.CompilerParams(vmem_limit_bytes=16 << 20),
        name="lift",
    )(star2, ye, e_phys, corr)
    return corrected[None], lifted[None]


def solution(mesh):
    return jax.shard_map(
        functools.partial(per_device, mesh.shape["win"], mesh.shape["vel"]),
        mesh=mesh,
        in_specs=(P("win", "vel", "sp", None), P("sp", None)),
        out_specs=(P("win", None, "sp", None), P("win", "vel", "sp", None)),
        check_vma=False,
    )
```

```python
import functools
import math

import jax
import jax.numpy as jnp
from jax import lax
from jax.experimental import pallas as pl
from jax.experimental.pallas import tpu as pltpu
from jax.sharding import PartitionSpec as P

NVX = 48
NVY = 32
HALF = NVY // 2
TILE = 8
vel_max = 6.0
fine_ratio = 0.075
coarse_ratio = 0.15
density_floor = 0.3
thermal_lower_bound = 0.3
DVX = 2.0 * vel_max / NVX
DVY = 2.0 * vel_max / NVY
WEIGHT = DVX * DVY / (2.0 * math.pi)
MESH = pl.DeviceIdType.MESH
f32 = jnp.float32
ORDERS = [(p, q) for p in range(5) for q in range(5 - p)]
PLACE = {order: n for n, order in enumerate(ORDERS)}
MAIN = [(0, 0), (0, 1), (1, 0), (0, 2), (2, 0)]
FIRST, START, SECOND = range(3)
AHEAD = 1
EARLY = 4


def physical_variables(u):
    rs = jnp.maximum(u[0], density_floor)
    ux = u[1] / rs
    uy = u[2] / rs
    temp = jnp.maximum((u[3] - 0.5 * (u[1] * ux + u[2] * uy)) / rs, thermal_lower_bound)
    return rs, ux, uy, temp


def chunk_of(first, c):
    k = first + c * HALF
    i = k // NVY
    j = k % NVY
    vx = -vel_max + (i.astype(f32) + 0.5) * DVX
    vy = -vel_max + (j.astype(f32) + 0.5) * DVY
    return vx, vy, j // HALF, j


def coarse(u, band):
    rows, ny = u[0].shape
    rs, ux, uy, temp = physical_variables(u)
    p = rs * temp
    wave = jnp.sqrt(2.0 * temp)
    fx = [u[1], u[1] * ux + p, u[2] * ux, (u[3] + p) * ux]
    fy = [u[2], u[1] * uy, u[2] * uy + p, (u[3] + p) * uy]
    sx = jnp.abs(ux) + wave
    sy = jnp.abs(uy) + wave
    mx = jnp.maximum(sx, pltpu.roll(sx, rows - 1, 0))
    my = jnp.maximum(sy, pltpu.roll(sy, ny - 1, 1))
    out = []
    for c in range(4):
        face_x = 0.5 * (fx[c] + pltpu.roll(fx[c], rows - 1, 0)) - 0.5 * mx * (
            pltpu.roll(u[c], rows - 1, 0) - u[c]
        )
        face_y = 0.5 * (fy[c] + pltpu.roll(fy[c], ny - 1, 1)) - 0.5 * my * (
            pltpu.roll(u[c], ny - 1, 1) - u[c]
        )
        g = u[c] - coarse_ratio * (
            face_x - pltpu.roll(face_x, 1, 0) + (face_y - pltpu.roll(face_y, 1, 1))
        )
        out.append(g[:band])
    return out


def advance_kernel(
    nw, nv,
    f, r, star2, ye, e_phys, corr_out,
    fpad, spad, rfull, bsum, hsum, gout, msg, xmsg, red, redx, xs, es, fr, flux, energy, delta, gs,
    pmsg, pin, vmsg, vrow, vin, vrow_in, chain, chain_rows, phys, xpad, yt, yr,
    load_sem, halo_send, halo_recv, rs_send, rs_recv, ag_send, ag_recv, win_send, win_recv,
    chain_send, chain_recv, ready,
):
    w, v, s = lax.axis_index("win"), lax.axis_index("vel"), lax.axis_index("sp")
    count, nx, ny = f.shape
    chunks = count // HALF
    first = v * count
    other = 1 - s
    pos = (2 * v) // nv
    band = nx // 2
    frame = band + TILE
    full = 4 * band
    main = pl.ds(2 * TILE, nx)
    end = 2 * TILE + nx
    up = pl.ds(2 * TILE + 1 - 2 * pos, nx)
    hb = pl.multiple_of(end - (end - TILE) * pos, TILE)
    edge = pl.ds(hb, TILE)
    edge_up = pl.ds(hb + 1 - 2 * pos, TILE)
    ho = pl.multiple_of(TILE + (end - TILE) * pos, TILE)
    away = pl.ds(ho, TILE)
    away_up = pl.ds(ho + 1 - 2 * pos, TILE)
    tiles = nx // TILE

    base = nv // 2 - 2
    off = v - base
    is_owner = (s == 1) & (off >= 0) & (off < 4)
    b = off // 2
    h = (off + b) % 2
    g = 2 * h + b

    def owner_at(half, k):
        return base + (half if k == 0 else 3 - half)

    def load_f(t):
        rows = pl.ds(pl.multiple_of(t * TILE, TILE), TILE)
        padded = pl.ds(pl.multiple_of((t + 2) * TILE, TILE), TILE)
        return pltpu.make_async_copy(f.at[:, rows], fpad.at[:, padded], load_sem.at[t])

    for t in range(tiles):
        load_f(t).start()
    mine = pl.ds(pl.multiple_of(s * nx, TILE), nx)
    load_r = pltpu.make_async_copy(r, rfull.at[mine], load_sem.at[tiles])
    load_r.start()

    def signal(device):
        pl.semaphore_signal(barrier, inc=1, device_id=device, device_id_type=MESH)

    barrier = pltpu.get_barrier_semaphore()
    signal((w, v, other))
    for o in range(4):

        @pl.when(jnp.logical_not((v == base + o) & (s == 1)))
        def _():
            signal((w, base + o, 1))

    @pl.when(is_owner)
    def _():
        signal((w, v, 0))
        for d in range(1, nv):
            for half in range(2):
                signal((w, lax.rem(v + d, nv), half))

        @pl.when(w + 1 < nw)
        def _():
            for n in range(nv):
                for half in range(2):
                    signal((w + 1, n, half))

    def remote(src, dst, send, recv, device):
        return pltpu.make_async_remote_copy(
            src_ref=src, dst_ref=dst, send_sem=send, recv_sem=recv,
            device_id=device, device_id_type=MESH,
        )

    def settle(ref, sem):
        pltpu.make_async_copy(ref, ref, sem).wait()

    empty = jnp.zeros((TILE, ny), f32)
    for side in range(2):
        for n in range(len(ORDERS)):
            for at in (TILE, end):
                bsum[side, n, pl.ds(at, TILE)] = empty
                hsum[side, n, pl.ds(at, TILE)] = empty

    parity = (first // HALF) % 2
    rounds = (chunks + 1) // 2

    @pl.loop(0, tiles)
    def _(t):
        load_f(t).wait()
        rows = pl.ds(pl.multiple_of(2 * TILE + t * TILE, TILE), TILE)
        for side in range(2):
            acc = {order: jnp.zeros((TILE, ny), f32) for order in ORDERS}
            for n in range(rounds):
                c = (side + parity) % 2 + 2 * n
                weight = 1.0
                if chunks % 2:
                    weight = jnp.where(c < chunks, 1.0, 0.0).astype(f32)
                    c = jnp.minimum(c, chunks - 1)
                vx = chunk_of(first, c)[0]
                sums = [jnp.zeros((TILE, ny), f32)] * 5
                for jj in range(HALF // 2, HALF):
                    tt = (jj + 0.5) * DVY - 0.5 * vel_max
                    high = fpad[c * HALF + jj, rows]
                    low = fpad[c * HALF + HALF - 1 - jj, rows]
                    even, odd = high + low, high - low
                    sums = [
                        sums[0] + even, sums[1] + tt * odd, sums[2] + tt**2 * even,
                        sums[3] + tt**3 * odd, sums[4] + tt**4 * even,
                    ]
                power = weight
                for q in range(5):
                    for m in range(5 - q):
                        term = sums[m] if q == 0 and chunks % 2 == 0 else sums[m] * power
                        acc[m, q] = acc[m, q] + term
                    power = power * vx
            centre = (side - 0.5) * vel_max
            for p, q in ORDERS:
                total = acc[p, q]
                for m in range(p):
                    total = total + (math.comb(p, m) * centre ** (p - m)) * acc[m, q]
                bsum[side, PLACE[p, q], rows] = total

    def components(get):
        return [
            WEIGHT * get(0, 0), WEIGHT * get(0, 1), WEIGHT * get(1, 0),
            (0.5 * WEIGHT) * (get(0, 2) + get(2, 0)),
        ]

    def fill(field, values):
        for c in range(4):
            for k in range(2):
                msg[field, k, pl.ds(c * band, band)] = values[c][k * band : (k + 1) * band]

    def fill_edges(field):
        for c in range(4):
            for k in range(2):
                if field == FIRST:
                    outer = gout[0, c, pl.ds(TILE - 1 if k == 0 else 0, 1)]
                else:
                    outer = jnp.zeros((1, ny), f32)
                msg[field, k, pl.ds(full + c, 1)] = outer
                inner = c * band if k == 0 else (c + 1) * band - 1
                msg[field, k, pl.ds(full + 4 + c, 1)] = msg[field, 1 - k, pl.ds(inner, 1)]

    def to_owner(half, k):
        target = owner_at(half, k)
        return target, (v == target) & (s == 1)

    sizes = {FIRST: full + TILE, START: full + TILE, SECOND: full}

    def scatter(field):
        size = pl.ds(0, sizes[field])
        for k in range(2):
            target, own = to_owner(s, k)

            @pl.when(own)
            def _():
                red[field, v, size] = msg[field, k, size]

            @pl.when(jnp.logical_not(own))
            def _():
                remote(
                    msg.at[field, k, size], red.at[field, v, size],
                    rs_send.at[field], rs_recv.at[field], (w, target, 1),
                ).start()

    ACROSS_ROWS = (pl.ds(0, TILE), pl.ds(TILE, 2 * TILE))

    def scatter_across(part):
        rows = ACROSS_ROWS[part]
        for k in range(2):
            target, own = to_owner(other, k)

            @pl.when(own)
            def _():
                redx[v, rows] = xmsg[k, rows]

            @pl.when(jnp.logical_not(own))
            def _():
                remote(
                    xmsg.at[k, rows], redx.at[v, rows],
                    rs_send.at[3 + part], rs_recv.at[3 + part], (w, target, 1),
                ).start()

    fill(START, components(lambda p, q: bsum[0, PLACE[p, q], main] + bsum[1, PLACE[p, q], main]))
    fill_edges(START)

    pl.semaphore_wait(barrier, jnp.where(is_owner, 2 * nv + 3, 5) + jnp.where(w > 0, 4, 0))

    @pl.when(w > 0)
    def _():
        for o in range(4):
            pl.semaphore_signal(ready, inc=1, device_id=(w - 1, base + o, 1), device_id_type=MESH)

    load_r.wait()
    source = pl.ds(pl.multiple_of((nx - TILE) * pos, TILE), TILE)
    halo_r = remote(r, rfull.at[mine], halo_send.at[0], halo_recv.at[0], (w, v, other))
    halo_f = remote(f.at[:, source], fpad.at[:, edge], halo_send.at[1], halo_recv.at[1], (w, v, other))
    halo_r.start()
    halo_f.start()

    inv_main = 1.0 / (1.0 + rfull[mine])
    along = fine_ratio * (2 * pos - 1).astype(f32)
    ACROSS = ((-fine_ratio, ny - 1), (fine_ratio, 1))

    def moved(table, side, p, q, rows, rows_up):
        across, shift = ACROSS[side]
        bx = table[side, PLACE[p, q + 1], rows]
        by = table[side, PLACE[p + 1, q], rows]
        return (
            table[side, PLACE[p, q], rows]
            + along * (table[side, PLACE[p, q + 1], rows_up] - bx)
            + across * (pltpu.roll(by, shift, 1) - by)
        )

    star_main, star_away = {}, {}

    def one_step(side, p, q):
        star = moved(bsum, side, p, q, main, up)
        beyond = moved(bsum, side, p, q, away, away_up)
        hsum[side, PLACE[p, q], main] = star * inv_main
        hsum[side, PLACE[p, q], away] = beyond
        return star, beyond

    for order in MAIN:
        parts = [one_step(side, *order) for side in range(2)]
        star_main[order] = parts[0][0] + parts[1][0]
        star_away[order] = parts[0][1] + parts[1][1]
    fill(FIRST, components(lambda p, q: star_main[p, q]))
    for c, value in enumerate(components(lambda p, q: star_away[p, q])):
        gout[0, c] = value
    fill_edges(FIRST)
    for k in range(2):
        last = band - 1 if k == 0 else 0
        for c in range(4):
            xmsg[k, pl.ds(c, 1)] = msg[FIRST, 1 - k, pl.ds(c * band + last, 1)]
            xmsg[k, pl.ds(4 + c, 1)] = gout[0, c, pl.ds(0 if k == 0 else TILE - 1, 1)]
    scatter_across(0)
    scatter(FIRST)
    for p, q in ORDERS:
        if p + q < 4 and (p, q) not in MAIN:
            for side in range(2):
                one_step(side, p, q)
    again = {o: moved(hsum, 0, *o, main, up) + moved(hsum, 1, *o, main, up) for o in MAIN}
    fill(SECOND, components(lambda p, q: again[p, q]))
    scatter(SECOND)

    halo_r.wait()
    theirs = other * nx
    inv_away = 1.0 / (1.0 + rfull[pl.ds(theirs + (nx - 1) * (1 - pos), 1)])
    inv_edge = 1.0 / (1.0 + rfull[pl.ds(pl.multiple_of(theirs + (nx - TILE) * pos, TILE), TILE)])
    for side in range(2):
        for p, q in ORDERS:
            if p + q < 4:
                hsum[side, PLACE[p, q], away] = hsum[side, PLACE[p, q], away] * inv_away
    again = {o: moved(hsum, 0, *o, away, away_up) + moved(hsum, 1, *o, away, away_up) for o in MAIN}
    for c, value in enumerate(components(lambda p, q: again[p, q])):
        gout[1, c] = value
    for k in range(2):
        last = band - 1 if k == 0 else 0
        near, far = (0, 1) if k == 0 else (TILE - 1, TILE - 2)
        for c in range(4):
            xmsg[k, pl.ds(8 + c, 1)] = gout[1, c, pl.ds(near, 1)]
            xmsg[k, pl.ds(12 + c, 1)] = gout[1, c, pl.ds(far, 1)]
            xmsg[k, pl.ds(16 + c, 1)] = msg[START, 1 - k, pl.ds(c * band + last, 1)]
            xmsg[k, pl.ds(20 + c, 1)] = jnp.zeros((1, ny), f32)
    scatter_across(1)
    scatter(START)
    halo_f.wait()

    @pl.loop(0, chunks)
    def _(c):
        vx, vy0, half, _j = chunk_of(first, c)
        shift = ny - 1 - (ny - 2) * half
        ca = fine_ratio * jnp.abs(vx)
        for jj in range(HALF):
            k = c * HALF + jj
            cb = fine_ratio * jnp.abs(vy0 + jj * DVY)
            cc = 1.0 - ca - cb
            x = fpad[k, main]
            spad[k, main] = (cc * x + ca * fpad[k, up] + cb * pltpu.roll(x, shift, 1)) * inv_main
            x = fpad[k, edge]
            spad[k, edge] = (cc * x + ca * fpad[k, edge_up] + cb * pltpu.roll(x, shift, 1)) * inv_edge

    row8 = lax.broadcasted_iota(jnp.int32, (TILE, ny), 0)
    row_band = lax.broadcasted_iota(jnp.int32, (band, ny), 0)
    brow = (band - 1) * b
    brow2 = 1 + (band - 3) * b

    def received(field):
        size = pl.ds(0, sizes[field])

        @pl.when(h == 1)
        def _():
            settle(red.at[field, pl.ds(0, nv - 1), size], rs_recv.at[field])

        @pl.when(h == 0)
        def _():
            settle(red.at[field, :, size], rs_recv.at[field])

    def summed(field, rows):
        total = red[field, 0, rows]
        for n in range(1, nv):
            total = total + red[field, n, rows]
        return total

    def comp(c):
        return pl.ds(c * band, band)

    def framed(value, outer, inner):
        above = jnp.where(b == 0, outer, inner)
        below = jnp.where(b == 0, inner, outer)
        return jnp.concatenate([value, jnp.where(row8 == TILE - 1, above, below)], axis=0)

    def placed(row, at):
        return jnp.where(row_band == at, row, 0.0)

    def share(n, size, targets):
        rows = pl.ds(0, size)
        for d in targets:

            def send(d=d):
                remote(
                    pmsg.at[n, rows], pin.at[n, b, rows], ag_send.at[n], ag_recv.at[n], (w, d, h)
                ).start()

            if base <= d < base + 4:
                own = (h == 1) & (v == d)
                pl.when(jnp.logical_not(own))(send)

                @pl.when(own)
                def _():
                    pin[n, b, rows] = pmsg[n, rows]
            else:
                send()

    def place(n):
        half, k = n // 2, n % 2
        return base + half + k * (3 - 2 * half)

    def along_chain():
        after, before = lax.rem(g + 1, 4), lax.rem(g + 3, 4)
        return [
            remote(vmsg, chain, chain_send.at[0], chain_recv.at[0], (w + 1, v, 1)),
            remote(vrow.at[0], chain_rows.at[1], chain_send.at[1], chain_recv.at[1], (w + 1, place(before), 1)),
            remote(vrow.at[1], chain_rows.at[0], chain_send.at[2], chain_recv.at[2], (w + 1, place(after), 1)),
        ]

    def hand_to(targets):
        for d in targets:
            remote(vrow.at[b], vrow_in.at[b], win_send.at[0], win_recv.at[0], (w + 1, d, 1 - h)).start()
            remote(vmsg, vin.at[b], win_send.at[1], win_recv.at[1], (w + 1, d, h)).start()

    def hand_on(values, targets):
        for c in range(4):
            vmsg[comp(c)] = values[c]
            for row, value in ((0, values[c][:1]), (1, values[c][-1:])):
                vrow[row, pl.ds(c, 1)] = value
                vrow[row, pl.ds(4 + c, 1)] = value
        pl.semaphore_wait(ready, 2 * nv)

        @pl.when(w + 2 < nw)
        def _():
            for copy in along_chain():
                copy.start()

        hand_to(targets)

    @pl.when(is_owner)
    def _():
        def received_across(part):
            rows = ACROSS_ROWS[part]

            @pl.when(h == 1)
            def _():
                settle(redx.at[:, rows], rs_recv.at[3 + part])

            @pl.when(h == 0)
            def _():
                settle(redx.at[pl.ds(0, nv - 1), rows], rs_recv.at[3 + part])

            across = redx[0, rows]
            for n in range(1, nv):
                across = across + redx[n, rows]
            xs[rows] = across

        received(FIRST)
        received_across(0)

        def x_row(n):
            return xs[pl.ds(n, 1)]

        def assembled(field, at):
            es[...] = summed(field, pl.ds(full, TILE))
            out = []
            for c in range(4):
                value = summed(field, comp(c))
                if field == FIRST:
                    value = value + placed(x_row(4 + c), brow)
                out.append(framed(value, es[pl.ds(c, 1)] + x_row(at + c), es[pl.ds(4 + c, 1)]))
            return out

        rs, ux, uy, temp = physical_variables(assembled(FIRST, 0))
        rows_all = 2 * nx
        mid = pl.ds(pl.multiple_of(g * band, TILE), band)
        above = rfull[pl.ds(lax.rem(g * band + rows_all - 1, rows_all), 1)]
        below = rfull[pl.ds(lax.rem(g * band + band, rows_all), 1)]
        rate = jnp.concatenate([rfull[mid], jnp.where(row8 == TILE - 1, above, below)], axis=0)
        fr[0] = ux
        fr[1] = uy
        fr[2] = -0.5 / temp
        fr[3] = rs / temp * (rate / (1.0 + rate))
        for n in range(4):
            pmsg[0, comp(n)] = fr[n, pl.ds(0, band)]
            outer = fr[n, pl.ds(band + (TILE - 1) * (1 - b), 1)]
            pmsg[0, pl.ds(full + n, 1)] = outer
            pmsg[0, pl.ds(full + 4 + n, 1)] = outer
        share(0, full + TILE, range(nv))

        @pl.loop(0, frame // TILE)
        def _(t):
            rows = pl.ds(pl.multiple_of(t * TILE, TILE), TILE)
            ux, uy, scale, amp = [fr[n, rows] for n in range(4)]

            def half_sums(speeds, drift):
                weights = []
                for speed in speeds:
                    d = speed - drift
                    weights.append(jnp.exp(d * d * scale))
                sides = []
                half = len(speeds) // 2
                for at, c in ((half, 0.5 * vel_max), (0, -0.5 * vel_max)):
                    m = [empty] * 4
                    for n in range(half // 2, half):
                        t = speeds[at + n] - c
                        high, low = weights[at + n], weights[at + half - 1 - n]
                        even, odd = high + low, high - low
                        m = [m[0] + even, m[1] + t * odd, m[2] + t**2 * even, m[3] + t**3 * odd]
                    sides.append([
                        m[0],
                        m[1] + c * m[0],
                        m[2] + (2 * c) * m[1] + c**2 * m[0],
                        m[3] + (3 * c) * m[2] + (3 * c**2) * m[1] + c**3 * m[0],
                    ])
                return sides

            xp, xm = half_sums([-vel_max + (i + 0.5) * DVX for i in range(NVX)], ux)
            yp, ym = half_sums([-vel_max + (j + 0.5) * DVY for j in range(NVY)], uy)
            xs_ = [x + y for x, y in zip(xp, xm)]
            ys_ = [x + y for x, y in zip(yp, ym)]
            amp = WEIGHT * amp

            def store(n, coef, x, y):
                x = [coef * amp * t for t in x]
                flux[n, rows] = x[0] * y[0]
                flux[n + 1, rows] = x[1] * y[0]
                flux[n + 2, rows] = x[0] * y[1]
                flux[n + 3, rows] = 0.5 * (x[2] * y[0] + x[0] * y[2])

            store(0, 1.0, xs_, ys_)
            store(4, fine_ratio, xp[1:], ys_)
            store(8, -fine_ratio, xm[1:], ys_)
            store(12, fine_ratio, xs_, yp[1:])
            store(16, -fine_ratio, xs_, ym[1:])

        received(SECOND)
        received_across(1)
        inner = pl.ds(0, band)
        for c in range(4):
            to_y, from_y = flux[12 + c, inner], flux[16 + c, inner]
            energy[c] = (
                summed(SECOND, comp(c)) + placed(x_row(8 + c), brow) + placed(x_row(12 + c), brow2)
            ) + (
                flux[c, inner] - flux[4 + c, inner] - flux[8 + c, inner] - to_y - from_y
                + pltpu.roll(flux[4 + c], 1, 0)[:band] + pltpu.roll(flux[8 + c], frame - 1, 0)[:band]
                + pltpu.roll(to_y, 1, 1) + pltpu.roll(from_y, ny - 1, 1)
            )
        rs, ux, uy, temp = physical_variables(energy)
        pmsg[1, comp(0)] = ux
        pmsg[1, comp(1)] = uy
        pmsg[1, comp(2)] = -0.5 / temp
        pmsg[1, comp(3)] = rs / temp * (1.0 / (1.0 + rfull[mid]))
        share(1, full, range(nv))

        received(START)
        stepped = coarse(assembled(START, 16), band)
        for c in range(4):
            gs[c] = stepped[c]
            delta[c] = energy[c] - stepped[c]

        for c in range(4):
            corrected = gs[c] + delta[c]
            energy[c] = corrected
            pmsg[2, comp(c)] = jnp.where(w == 0, corrected, delta[c])
        share(2, full, range(AHEAD))
        if nw > 1:

            @pl.when(w == 0)
            def _():
                hand_on([energy[c] for c in range(4)], range(EARLY))

        share(2, full, range(AHEAD, nv))
        if nw > 1:

            @pl.when(w == 0)
            def _():
                hand_to(range(EARLY, nv))


    @pl.loop(0, chunks)
    def _(c):
        vx, vy0, half, _j = chunk_of(first, c)
        shift = ny - 1 - (ny - 2) * half
        ca = fine_ratio * jnp.abs(vx)
        for jj in range(HALF):
            k = c * HALF + jj
            cb = fine_ratio * jnp.abs(vy0 + jj * DVY)
            x = spad[k, main]
            star = (1.0 - ca - cb) * x + ca * spad[k, up] + cb * pltpu.roll(x, shift, 1)
            star2[k] = star * inv_main

    if nw > 2:

        @pl.when(is_owner & (w > 0) & (w + 1 < nw))
        def _():
            settle(chain, chain_recv.at[0])
            settle(chain_rows.at[1], chain_recv.at[1])
            settle(chain_rows.at[0], chain_recv.at[2])
            u = [
                jnp.concatenate(
                    [
                        chain[comp(c)],
                        jnp.where(
                            row8 == TILE - 1, chain_rows[0, pl.ds(c, 1)], chain_rows[1, pl.ds(c, 1)]
                        ),
                    ],
                    axis=0,
                )
                for c in range(4)
            ]
            stepped = coarse(u, band)
            hand_on([stepped[c] + delta[c] for c in range(4)], range(nv))

    def shared(n, size):
        rows = pl.ds(0, size)

        @pl.when(is_owner & (h == 1))
        def _():
            settle(pin.at[n, 0, rows], ag_recv.at[n])

        @pl.when(jnp.logical_not(is_owner & (h == 1)))
        def _():
            settle(pin.at[n, :, rows], ag_recv.at[n])

    shared(0, full + TILE)
    for n in range(4):
        for k in range(2):
            phys[n, pl.ds(2 * TILE + k * band, band)] = pin[0, k, comp(n)]
        phys[n, edge] = jnp.broadcast_to(pin[0, 1 - pos, pl.ds(full + n, 1)], (TILE, ny))
    for rows in (main, edge):
        drift, scale = phys[1, rows], phys[2, rows]
        for j in range(NVY):
            d = (-vel_max + (j + 0.5) * DVY) - drift
            e = jnp.exp(d * d * scale)
            yt[j, rows] = e
            if rows is main:
                yr[j] = pltpu.roll(e, ny - 1 if j < HALF else 1, 1)

    @pl.loop(0, chunks)
    def _(c):
        vx, vy0, half, j0 = chunk_of(first, c)
        shift = ny - 1 - (ny - 2) * half
        ca = fine_ratio * jnp.abs(vx)
        for rows in (main, edge):
            d = vx - phys[0, rows]
            xpad[rows] = phys[3, rows] * jnp.exp(d * d * phys[2, rows])
        x = xpad[main]
        here = inv_main * x
        behind = (ca * inv_main) * xpad[up]
        beside = inv_main * pltpu.roll(x, shift, 1)
        for jj in range(HALF):
            k = c * HALF + jj
            cb = fine_ratio * jnp.abs(vy0 + jj * DVY)
            star2[k] = (
                star2[k] + ((1.0 - ca - cb) * here) * yt[j0 + jj, main] + behind * yt[j0 + jj, up]
                + (cb * beside) * yr[j0 + jj]
            )

    shared(1, full)
    for k in range(2):
        rows = pl.ds(k * band, band)
        for n in range(4):
            e_phys[n, rows] = pin[1, k, comp(n)]
    drift, scale = e_phys[1], e_phys[2]
    for j in range(NVY):
        d = (-vel_max + (j + 0.5) * DVY) - drift
        ye[j] = jnp.exp(d * d * scale)
    shared(2, full)
    for k in range(2):
        for n in range(4):
            corr_out[n, pl.ds(k * band, band)] = pin[2, k, comp(n)]
    if nw > 1:

        @pl.when(w > 0)
        def _():
            settle(vrow_in, win_recv.at[0])
            settle(vin, win_recv.at[1])
            u = [
                jnp.concatenate(
                    [
                        vin[0, comp(c)], vin[1, comp(c)],
                        jnp.where(row8 == TILE - 1, vrow_in[1, pl.ds(c, 1)], vrow_in[0, pl.ds(c, 1)]),
                    ],
                    axis=0,
                )
                for c in range(4)
            ]
            stepped = coarse(u, nx)
            for c in range(4):
                corr_out[c] = stepped[c] + corr_out[c]

    for field in range(3):
        size = pl.ds(0, sizes[field])
        for k in range(2):
            own = to_owner(s, k)[1]

            @pl.when(jnp.logical_not(own))
            def _():
                settle(msg.at[field, k, size], rs_send.at[field])

    for k in range(2):
        own = to_owner(other, k)[1]

        @pl.when(jnp.logical_not(own))
        def _():
            for part in range(2):
                settle(xmsg.at[k, ACROSS_ROWS[part]], rs_send.at[3 + part])

    @pl.when(is_owner)
    def _():
        for n, size in ((0, full + TILE), (1, full), (2, full)):
            rows = pl.ds(0, size)
            for _ in range(nv - 1):
                settle(pmsg.at[n, rows], ag_send.at[n])

            @pl.when(h == 0)
            def _():
                settle(pmsg.at[n, rows], ag_send.at[n])

        if nw > 1:

            @pl.when(w + 1 < nw)
            def _():
                for _ in range(nv):
                    settle(vrow.at[b], win_send.at[0])
                    settle(vmsg, win_send.at[1])

            @pl.when(w + 2 < nw)
            def _():
                settle(vmsg, chain_send.at[0])
                settle(vrow.at[0], chain_send.at[1])
                settle(vrow.at[1], chain_send.at[2])


def lift_kernel(parts, star2, ye, e_phys, corr, lifted, corrected, yc, out, save_sem):
    count = star2.shape[0]
    first = lax.axis_index("vel") * count
    corrected[...] = corr[...]
    rs, uc, uy, temp = physical_variables(corr)
    sc = -0.5 / temp
    mc = rs / temp
    for j in range(NVY):
        d = (-vel_max + (j + 0.5) * DVY) - uy
        yc[j] = jnp.exp(d * d * sc)
    chunks = count // HALF
    per = chunks // parts

    def save(n):
        rows = pl.ds(n * per * HALF, per * HALF)
        return pltpu.make_async_copy(out.at[rows], lifted.at[rows], save_sem.at[n])

    for n in range(parts):

        @pl.loop(n * per, (n + 1) * per)
        def _(c):
            vx, _vy, _half, j0 = chunk_of(first, c)
            dc = vx - uc
            xc = mc * jnp.exp(dc * dc * sc)
            de = vx - e_phys[0]
            xe = e_phys[3] * jnp.exp(de * de * e_phys[2])
            for jj in range(HALF):
                k = c * HALF + jj
                out[k] = star2[k] + (xc * yc[j0 + jj] - xe * ye[j0 + jj])

        save(n).start()
    for n in range(parts):
        save(n).wait()


def per_device(nw, nv, f_start, relax_rate):
    field = f_start[0]
    count, nx, ny = field.shape
    band = nx // 2
    frame = band + TILE
    full = 4 * band
    pad = nx + 4 * TILE
    vmem = pltpu.VMEM
    dma = pltpu.SemaphoreType.DMA
    small = jax.ShapeDtypeStruct((4, nx, ny), f32)
    speeds = jax.ShapeDtypeStruct((NVY, nx, ny), f32)
    in_vmem = pl.BlockSpec(memory_space=pltpu.VMEM)
    in_hbm = pl.BlockSpec(memory_space=pltpu.HBM)
    field = pltpu.with_memory_space_constraint(field, pltpu.HBM)
    star2, ye, e_phys, corr = pl.pallas_call(
        functools.partial(advance_kernel, nw, nv),
        out_shape=(jax.ShapeDtypeStruct((count, nx, ny), f32), speeds, small, small),
        in_specs=[in_hbm, in_hbm],
        out_specs=(in_vmem,) * 4,
        scratch_shapes=[
            vmem((count, pad, ny), f32),
            vmem((count, pad, ny), f32),
            vmem((2 * nx, ny), f32),
            vmem((2, len(ORDERS), pad, ny), f32),
            vmem((2, len(ORDERS), pad, ny), f32),
            vmem((2, 4, TILE, ny), f32),
            vmem((3, 2, full + TILE, ny), f32),
            vmem((2, 3 * TILE, ny), f32),
            vmem((3, nv, full + TILE, ny), f32),
            vmem((nv, 3 * TILE, ny), f32),
            vmem((3 * TILE, ny), f32),
            vmem((TILE, ny), f32),
            vmem((4, frame, ny), f32),
            vmem((20, frame, ny), f32),
            vmem((4, band, ny), f32),
            vmem((4, band, ny), f32),
            vmem((4, band, ny), f32),
            vmem((3, full + TILE, ny), f32),
            vmem((3, 2, full + TILE, ny), f32),
            vmem((full, ny), f32),
            vmem((2, TILE, ny), f32),
            vmem((2, full, ny), f32),
            vmem((2, TILE, ny), f32),
            vmem((full, ny), f32),
            vmem((2, TILE, ny), f32),
            vmem((4, pad, ny), f32),
            vmem((pad, ny), f32),
            vmem((NVY, pad, ny), f32),
            vmem((NVY, nx, ny), f32),
            dma((1 + nx // TILE,)), dma((2,)), dma((2,)), dma((5,)), dma((5,)), dma((3,)), dma((3,)),
            dma((2,)), dma((2,)), dma((3,)), dma((3,)), pltpu.SemaphoreType.REGULAR,
        ],
        compiler_params=pltpu.CompilerParams(
            collective_id=0, has_side_effects=True, vmem_limit_bytes=40 << 20
        ),
        name="advance",
    )(field, pltpu.with_memory_space_constraint(relax_rate, pltpu.HBM))

    chunks = count // HALF
    parts = next(n for n in (6, 4, 3, 2, 1) if chunks % n == 0)
    lifted, corrected = pl.pallas_call(
        functools.partial(lift_kernel, parts),
        out_shape=(jax.ShapeDtypeStruct((count, nx, ny), f32), small),
        in_specs=[in_vmem] * 4,
        out_specs=(in_hbm, in_vmem),
        scratch_shapes=[
            vmem((NVY, nx, ny), f32), vmem((count, nx, ny), f32), dma((parts,)),
        ],
        compiler_params=pltpu.CompilerParams(vmem_limit_bytes=16 << 20),
        name="lift",
    )(star2, ye, e_phys, corr)
    return corrected[None], lifted[None]


def solution(mesh):
    return jax.shard_map(
        functools.partial(per_device, mesh.shape["win"], mesh.shape["vel"]),
        mesh=mesh,
        in_specs=(P("win", "vel", "sp", None), P("sp", None)),
        out_specs=(P("win", None, "sp", None), P("win", "vel", "sp", None)),
        check_vma=False,
    )
```

```python
import functools
import math

import jax
import jax.numpy as jnp
from jax import lax
from jax.experimental import pallas as pl
from jax.experimental.pallas import tpu as pltpu
from jax.sharding import PartitionSpec as P

NVX = 48
NVY = 32
HALF = NVY // 2
TILE = 8
vel_max = 6.0
fine_ratio = 0.075
coarse_ratio = 0.15
density_floor = 0.3
thermal_lower_bound = 0.3
DVX = 2.0 * vel_max / NVX
DVY = 2.0 * vel_max / NVY
WEIGHT = DVX * DVY / (2.0 * math.pi)
MESH = pl.DeviceIdType.MESH
f32 = jnp.float32
ORDERS = [(p, q) for p in range(5) for q in range(5 - p)]
PLACE = {order: n for n, order in enumerate(ORDERS)}
MAIN = [(0, 0), (0, 1), (1, 0), (0, 2), (2, 0)]
FIRST, START, SECOND = range(3)
AHEAD = 1
EARLY = 4


def physical_variables(u):
    rs = jnp.maximum(u[0], density_floor)
    ux = u[1] / rs
    uy = u[2] / rs
    temp = jnp.maximum((u[3] - 0.5 * (u[1] * ux + u[2] * uy)) / rs, thermal_lower_bound)
    return rs, ux, uy, temp


def chunk_of(first, c):
    k = first + c * HALF
    i = k // NVY
    j = k % NVY
    vx = -vel_max + (i.astype(f32) + 0.5) * DVX
    vy = -vel_max + (j.astype(f32) + 0.5) * DVY
    return vx, vy, j // HALF, j


def coarse(u, band):
    rows, ny = u[0].shape
    rs, ux, uy, temp = physical_variables(u)
    p = rs * temp
    wave = jnp.sqrt(2.0 * temp)
    fx = [u[1], u[1] * ux + p, u[2] * ux, (u[3] + p) * ux]
    fy = [u[2], u[1] * uy, u[2] * uy + p, (u[3] + p) * uy]
    sx = jnp.abs(ux) + wave
    sy = jnp.abs(uy) + wave
    mx = jnp.maximum(sx, pltpu.roll(sx, rows - 1, 0))
    my = jnp.maximum(sy, pltpu.roll(sy, ny - 1, 1))
    out = []
    for c in range(4):
        face_x = 0.5 * (fx[c] + pltpu.roll(fx[c], rows - 1, 0)) - 0.5 * mx * (
            pltpu.roll(u[c], rows - 1, 0) - u[c]
        )
        face_y = 0.5 * (fy[c] + pltpu.roll(fy[c], ny - 1, 1)) - 0.5 * my * (
            pltpu.roll(u[c], ny - 1, 1) - u[c]
        )
        g = u[c] - coarse_ratio * (
            face_x - pltpu.roll(face_x, 1, 0) + (face_y - pltpu.roll(face_y, 1, 1))
        )
        out.append(g[:band])
    return out


def advance_kernel(
    nw, nv,
    f, r, star2, ye, e_phys, corr_out,
    fpad, spad, rfull, bsum, hsum, gout, msg, xmsg, red, redx, xs, es, fr, flux, energy, delta, gs,
    pmsg, pin, vmsg, vrow, vin, vrow_in, chain, chain_rows, phys, xpad, yt, yr,
    load_sem, halo_send, halo_recv, rs_send, rs_recv, ag_send, ag_recv, win_send, win_recv,
    chain_send, chain_recv, ready,
):
    w, v, s = lax.axis_index("win"), lax.axis_index("vel"), lax.axis_index("sp")
    count, nx, ny = f.shape
    chunks = count // HALF
    first = v * count
    other = 1 - s
    pos = (2 * v) // nv
    band = nx // 2
    frame = band + TILE
    full = 4 * band
    main = pl.ds(2 * TILE, nx)
    end = 2 * TILE + nx
    up = pl.ds(2 * TILE + 1 - 2 * pos, nx)
    hb = pl.multiple_of(end - (end - TILE) * pos, TILE)
    edge = pl.ds(hb, TILE)
    edge_up = pl.ds(hb + 1 - 2 * pos, TILE)
    ho = pl.multiple_of(TILE + (end - TILE) * pos, TILE)
    away = pl.ds(ho, TILE)
    away_up = pl.ds(ho + 1 - 2 * pos, TILE)
    tiles = nx // TILE

    base = nv // 2 - 2
    off = v - base
    is_owner = (s == 1) & (off >= 0) & (off < 4)
    b = off // 2
    h = (off + b) % 2
    g = 2 * h + b

    def owner_at(half, k):
        return base + (half if k == 0 else 3 - half)

    def load_f(t):
        rows = pl.ds(pl.multiple_of(t * TILE, TILE), TILE)
        padded = pl.ds(pl.multiple_of((t + 2) * TILE, TILE), TILE)
        return pltpu.make_async_copy(f.at[:, rows], fpad.at[:, padded], load_sem.at[t])

    for t in range(tiles):
        load_f(t).start()
    mine = pl.ds(pl.multiple_of(s * nx, TILE), nx)
    load_r = pltpu.make_async_copy(r, rfull.at[mine], load_sem.at[tiles])
    load_r.start()

    def signal(device):
        pl.semaphore_signal(barrier, inc=1, device_id=device, device_id_type=MESH)

    barrier = pltpu.get_barrier_semaphore()
    signal((w, v, other))
    for o in range(4):

        @pl.when(jnp.logical_not((v == base + o) & (s == 1)))
        def _():
            signal((w, base + o, 1))

    @pl.when(is_owner)
    def _():
        signal((w, v, 0))
        for d in range(1, nv):
            for half in range(2):
                signal((w, lax.rem(v + d, nv), half))

        @pl.when(w + 1 < nw)
        def _():
            for n in range(nv):
                for half in range(2):
                    signal((w + 1, n, half))

    def remote(src, dst, send, recv, device):
        return pltpu.make_async_remote_copy(
            src_ref=src, dst_ref=dst, send_sem=send, recv_sem=recv,
            device_id=device, device_id_type=MESH,
        )

    def settle(ref, sem):
        pltpu.make_async_copy(ref, ref, sem).wait()

    empty = jnp.zeros((TILE, ny), f32)
    for side in range(2):
        for n in range(len(ORDERS)):
            for at in (TILE, end):
                bsum[side, n, pl.ds(at, TILE)] = empty
                hsum[side, n, pl.ds(at, TILE)] = empty

    parity = (first // HALF) % 2
    rounds = (chunks + 1) // 2

    @pl.loop(0, tiles)
    def _(t):
        load_f(t).wait()
        rows = pl.ds(pl.multiple_of(2 * TILE + t * TILE, TILE), TILE)
        for side in range(2):
            acc = {order: jnp.zeros((TILE, ny), f32) for order in ORDERS}
            for n in range(rounds):
                c = (side + parity) % 2 + 2 * n
                weight = 1.0
                if chunks % 2:
                    weight = jnp.where(c < chunks, 1.0, 0.0).astype(f32)
                    c = jnp.minimum(c, chunks - 1)
                vx = chunk_of(first, c)[0]
                sums = [jnp.zeros((TILE, ny), f32)] * 5
                for jj in range(HALF // 2, HALF):
                    tt = (jj + 0.5) * DVY - 0.5 * vel_max
                    high = fpad[c * HALF + jj, rows]
                    low = fpad[c * HALF + HALF - 1 - jj, rows]
                    even, odd = high + low, high - low
                    sums = [
                        sums[0] + even, sums[1] + tt * odd, sums[2] + tt**2 * even,
                        sums[3] + tt**3 * odd, sums[4] + tt**4 * even,
                    ]
                power = weight
                for q in range(5):
                    for m in range(5 - q):
                        term = sums[m] if q == 0 and chunks % 2 == 0 else sums[m] * power
                        acc[m, q] = acc[m, q] + term
                    power = power * vx
            centre = (side - 0.5) * vel_max
            for p, q in ORDERS:
                total = acc[p, q]
                for m in range(p):
                    total = total + (math.comb(p, m) * centre ** (p - m)) * acc[m, q]
                bsum[side, PLACE[p, q], rows] = total

    def components(get):
        return [
            WEIGHT * get(0, 0), WEIGHT * get(0, 1), WEIGHT * get(1, 0),
            (0.5 * WEIGHT) * (get(0, 2) + get(2, 0)),
        ]

    def fill(field, values):
        for c in range(4):
            for k in range(2):
                msg[field, k, pl.ds(c * band, band)] = values[c][k * band : (k + 1) * band]

    def fill_edges(field):
        for c in range(4):
            for k in range(2):
                if field == FIRST:
                    outer = gout[0, c, pl.ds(TILE - 1 if k == 0 else 0, 1)]
                else:
                    outer = jnp.zeros((1, ny), f32)
                msg[field, k, pl.ds(full + c, 1)] = outer
                inner = c * band if k == 0 else (c + 1) * band - 1
                msg[field, k, pl.ds(full + 4 + c, 1)] = msg[field, 1 - k, pl.ds(inner, 1)]

    def to_owner(half, k):
        target = owner_at(half, k)
        return target, (v == target) & (s == 1)

    sizes = {FIRST: full + TILE, START: full + TILE, SECOND: full}

    def scatter(field):
        size = pl.ds(0, sizes[field])
        for k in range(2):
            target, own = to_owner(s, k)

            @pl.when(own)
            def _():
                red[field, v, size] = msg[field, k, size]

            @pl.when(jnp.logical_not(own))
            def _():
                remote(
                    msg.at[field, k, size], red.at[field, v, size],
                    rs_send.at[field], rs_recv.at[field], (w, target, 1),
                ).start()

    ACROSS_ROWS = (pl.ds(0, TILE), pl.ds(TILE, 2 * TILE))

    def scatter_across(part):
        rows = ACROSS_ROWS[part]
        for k in range(2):
            target, own = to_owner(other, k)

            @pl.when(own)
            def _():
                redx[v, rows] = xmsg[k, rows]

            @pl.when(jnp.logical_not(own))
            def _():
                remote(
                    xmsg.at[k, rows], redx.at[v, rows],
                    rs_send.at[3 + part], rs_recv.at[3 + part], (w, target, 1),
                ).start()

    fill(START, components(lambda p, q: bsum[0, PLACE[p, q], main] + bsum[1, PLACE[p, q], main]))
    fill_edges(START)

    pl.semaphore_wait(barrier, jnp.where(is_owner, 2 * nv + 3, 5) + jnp.where(w > 0, 4, 0))

    @pl.when(w > 0)
    def _():
        for o in range(4):
            pl.semaphore_signal(ready, inc=1, device_id=(w - 1, base + o, 1), device_id_type=MESH)

    load_r.wait()
    source = pl.ds(pl.multiple_of((nx - TILE) * pos, TILE), TILE)
    halo_r = remote(r, rfull.at[mine], halo_send.at[0], halo_recv.at[0], (w, v, other))
    halo_f = remote(f.at[:, source], fpad.at[:, edge], halo_send.at[1], halo_recv.at[1], (w, v, other))
    halo_r.start()
    halo_f.start()

    inv_main = 1.0 / (1.0 + rfull[mine])
    along = fine_ratio * (2 * pos - 1).astype(f32)
    ACROSS = ((-fine_ratio, ny - 1), (fine_ratio, 1))

    def moved(table, side, p, q, rows, rows_up):
        across, shift = ACROSS[side]
        bx = table[side, PLACE[p, q + 1], rows]
        by = table[side, PLACE[p + 1, q], rows]
        return (
            table[side, PLACE[p, q], rows]
            + along * (table[side, PLACE[p, q + 1], rows_up] - bx)
            + across * (pltpu.roll(by, shift, 1) - by)
        )

    star_main, star_away = {}, {}

    def one_step(side, p, q):
        star = moved(bsum, side, p, q, main, up)
        beyond = moved(bsum, side, p, q, away, away_up)
        hsum[side, PLACE[p, q], main] = star * inv_main
        hsum[side, PLACE[p, q], away] = beyond
        return star, beyond

    for order in MAIN:
        parts = [one_step(side, *order) for side in range(2)]
        star_main[order] = parts[0][0] + parts[1][0]
        star_away[order] = parts[0][1] + parts[1][1]
    fill(FIRST, components(lambda p, q: star_main[p, q]))
    for c, value in enumerate(components(lambda p, q: star_away[p, q])):
        gout[0, c] = value
    fill_edges(FIRST)
    for k in range(2):
        last = band - 1 if k == 0 else 0
        for c in range(4):
            xmsg[k, pl.ds(c, 1)] = msg[FIRST, 1 - k, pl.ds(c * band + last, 1)]
            xmsg[k, pl.ds(4 + c, 1)] = gout[0, c, pl.ds(0 if k == 0 else TILE - 1, 1)]
    scatter_across(0)
    scatter(FIRST)
    for p, q in ORDERS:
        if p + q < 4 and (p, q) not in MAIN:
            for side in range(2):
                one_step(side, p, q)
    again = {o: moved(hsum, 0, *o, main, up) + moved(hsum, 1, *o, main, up) for o in MAIN}
    fill(SECOND, components(lambda p, q: again[p, q]))
    scatter(SECOND)

    halo_r.wait()
    theirs = other * nx
    inv_away = 1.0 / (1.0 + rfull[pl.ds(theirs + (nx - 1) * (1 - pos), 1)])
    inv_edge = 1.0 / (1.0 + rfull[pl.ds(pl.multiple_of(theirs + (nx - TILE) * pos, TILE), TILE)])
    for side in range(2):
        for p, q in ORDERS:
            if p + q < 4:
                hsum[side, PLACE[p, q], away] = hsum[side, PLACE[p, q], away] * inv_away
    again = {o: moved(hsum, 0, *o, away, away_up) + moved(hsum, 1, *o, away, away_up) for o in MAIN}
    for c, value in enumerate(components(lambda p, q: again[p, q])):
        gout[1, c] = value
    for k in range(2):
        last = band - 1 if k == 0 else 0
        near, far = (0, 1) if k == 0 else (TILE - 1, TILE - 2)
        for c in range(4):
            xmsg[k, pl.ds(8 + c, 1)] = gout[1, c, pl.ds(near, 1)]
            xmsg[k, pl.ds(12 + c, 1)] = gout[1, c, pl.ds(far, 1)]
            xmsg[k, pl.ds(16 + c, 1)] = msg[START, 1 - k, pl.ds(c * band + last, 1)]
            xmsg[k, pl.ds(20 + c, 1)] = jnp.zeros((1, ny), f32)
    scatter_across(1)
    halo_f.wait()

    def first_transport(c):
        vx, vy0, half, _j = chunk_of(first, c)
        shift = ny - 1 - (ny - 2) * half
        ca = fine_ratio * jnp.abs(vx)
        for jj in range(HALF):
            k = c * HALF + jj
            cb = fine_ratio * jnp.abs(vy0 + jj * DVY)
            cc = 1.0 - ca - cb
            x = fpad[k, main]
            spad[k, main] = (cc * x + ca * fpad[k, up] + cb * pltpu.roll(x, shift, 1)) * inv_main
            x = fpad[k, edge]
            spad[k, edge] = (cc * x + ca * fpad[k, edge_up] + cb * pltpu.roll(x, shift, 1)) * inv_edge

    pl.loop(0, chunks // 4)(first_transport)
    scatter(START)
    pl.loop(chunks // 4, chunks)(first_transport)

    row8 = lax.broadcasted_iota(jnp.int32, (TILE, ny), 0)
    row_band = lax.broadcasted_iota(jnp.int32, (band, ny), 0)
    brow = (band - 1) * b
    brow2 = 1 + (band - 3) * b

    def received(field):
        size = pl.ds(0, sizes[field])

        @pl.when(h == 1)
        def _():
            settle(red.at[field, pl.ds(0, nv - 1), size], rs_recv.at[field])

        @pl.when(h == 0)
        def _():
            settle(red.at[field, :, size], rs_recv.at[field])

    def summed(field, rows):
        total = red[field, 0, rows]
        for n in range(1, nv):
            total = total + red[field, n, rows]
        return total

    def comp(c):
        return pl.ds(c * band, band)

    def framed(value, outer, inner):
        above = jnp.where(b == 0, outer, inner)
        below = jnp.where(b == 0, inner, outer)
        return jnp.concatenate([value, jnp.where(row8 == TILE - 1, above, below)], axis=0)

    def placed(row, at):
        return jnp.where(row_band == at, row, 0.0)

    def share(n, size, targets):
        rows = pl.ds(0, size)
        for d in targets:

            def send(d=d):
                remote(
                    pmsg.at[n, rows], pin.at[n, b, rows], ag_send.at[n], ag_recv.at[n], (w, d, h)
                ).start()

            if base <= d < base + 4:
                own = (h == 1) & (v == d)
                pl.when(jnp.logical_not(own))(send)

                @pl.when(own)
                def _():
                    pin[n, b, rows] = pmsg[n, rows]
            else:
                send()

    def place(n):
        half, k = n // 2, n % 2
        return base + half + k * (3 - 2 * half)

    def along_chain():
        after, before = lax.rem(g + 1, 4), lax.rem(g + 3, 4)
        return [
            remote(vmsg, chain, chain_send.at[0], chain_recv.at[0], (w + 1, v, 1)),
            remote(vrow.at[0], chain_rows.at[1], chain_send.at[1], chain_recv.at[1], (w + 1, place(before), 1)),
            remote(vrow.at[1], chain_rows.at[0], chain_send.at[2], chain_recv.at[2], (w + 1, place(after), 1)),
        ]

    def hand_to(targets):
        for d in targets:
            remote(vrow.at[b], vrow_in.at[b], win_send.at[0], win_recv.at[0], (w + 1, d, 1 - h)).start()
            remote(vmsg, vin.at[b], win_send.at[1], win_recv.at[1], (w + 1, d, h)).start()

    def hand_on(values, targets):
        for c in range(4):
            vmsg[comp(c)] = values[c]
            for row, value in ((0, values[c][:1]), (1, values[c][-1:])):
                vrow[row, pl.ds(c, 1)] = value
                vrow[row, pl.ds(4 + c, 1)] = value
        pl.semaphore_wait(ready, 2 * nv)

        @pl.when(w + 2 < nw)
        def _():
            for copy in along_chain():
                copy.start()

        hand_to(targets)

    @pl.when(is_owner)
    def _():
        def received_across(part):
            rows = ACROSS_ROWS[part]

            @pl.when(h == 1)
            def _():
                settle(redx.at[:, rows], rs_recv.at[3 + part])

            @pl.when(h == 0)
            def _():
                settle(redx.at[pl.ds(0, nv - 1), rows], rs_recv.at[3 + part])

            across = redx[0, rows]
            for n in range(1, nv):
                across = across + redx[n, rows]
            xs[rows] = across

        received(FIRST)
        received_across(0)

        def x_row(n):
            return xs[pl.ds(n, 1)]

        def assembled(field, at):
            es[...] = summed(field, pl.ds(full, TILE))
            out = []
            for c in range(4):
                value = summed(field, comp(c))
                if field == FIRST:
                    value = value + placed(x_row(4 + c), brow)
                out.append(framed(value, es[pl.ds(c, 1)] + x_row(at + c), es[pl.ds(4 + c, 1)]))
            return out

        rs, ux, uy, temp = physical_variables(assembled(FIRST, 0))
        rows_all = 2 * nx
        mid = pl.ds(pl.multiple_of(g * band, TILE), band)
        above = rfull[pl.ds(lax.rem(g * band + rows_all - 1, rows_all), 1)]
        below = rfull[pl.ds(lax.rem(g * band + band, rows_all), 1)]
        rate = jnp.concatenate([rfull[mid], jnp.where(row8 == TILE - 1, above, below)], axis=0)
        fr[0] = ux
        fr[1] = uy
        fr[2] = -0.5 / temp
        fr[3] = rs / temp * (rate / (1.0 + rate))
        for n in range(4):
            pmsg[0, comp(n)] = fr[n, pl.ds(0, band)]
            outer = fr[n, pl.ds(band + (TILE - 1) * (1 - b), 1)]
            pmsg[0, pl.ds(full + n, 1)] = outer
            pmsg[0, pl.ds(full + 4 + n, 1)] = outer
        share(0, full + TILE, range(nv))

        @pl.loop(0, frame // TILE)
        def _(t):
            rows = pl.ds(pl.multiple_of(t * TILE, TILE), TILE)
            ux, uy, scale, amp = [fr[n, rows] for n in range(4)]

            def half_sums(speeds, drift):
                weights = []
                for speed in speeds:
                    d = speed - drift
                    weights.append(jnp.exp(d * d * scale))
                sides = []
                half = len(speeds) // 2
                for at, c in ((half, 0.5 * vel_max), (0, -0.5 * vel_max)):
                    m = [empty] * 4
                    for n in range(half // 2, half):
                        t = speeds[at + n] - c
                        high, low = weights[at + n], weights[at + half - 1 - n]
                        even, odd = high + low, high - low
                        m = [m[0] + even, m[1] + t * odd, m[2] + t**2 * even, m[3] + t**3 * odd]
                    sides.append([
                        m[0],
                        m[1] + c * m[0],
                        m[2] + (2 * c) * m[1] + c**2 * m[0],
                        m[3] + (3 * c) * m[2] + (3 * c**2) * m[1] + c**3 * m[0],
                    ])
                return sides

            xp, xm = half_sums([-vel_max + (i + 0.5) * DVX for i in range(NVX)], ux)
            yp, ym = half_sums([-vel_max + (j + 0.5) * DVY for j in range(NVY)], uy)
            xs_ = [x + y for x, y in zip(xp, xm)]
            ys_ = [x + y for x, y in zip(yp, ym)]
            amp = WEIGHT * amp

            def store(n, coef, x, y):
                x = [coef * amp * t for t in x]
                flux[n, rows] = x[0] * y[0]
                flux[n + 1, rows] = x[1] * y[0]
                flux[n + 2, rows] = x[0] * y[1]
                flux[n + 3, rows] = 0.5 * (x[2] * y[0] + x[0] * y[2])

            store(0, 1.0, xs_, ys_)
            store(4, fine_ratio, xp[1:], ys_)
            store(8, -fine_ratio, xm[1:], ys_)
            store(12, fine_ratio, xs_, yp[1:])
            store(16, -fine_ratio, xs_, ym[1:])

        received(SECOND)
        received_across(1)
        inner = pl.ds(0, band)
        for c in range(4):
            to_y, from_y = flux[12 + c, inner], flux[16 + c, inner]
            energy[c] = (
                summed(SECOND, comp(c)) + placed(x_row(8 + c), brow) + placed(x_row(12 + c), brow2)
            ) + (
                flux[c, inner] - flux[4 + c, inner] - flux[8 + c, inner] - to_y - from_y
                + pltpu.roll(flux[4 + c], 1, 0)[:band] + pltpu.roll(flux[8 + c], frame - 1, 0)[:band]
                + pltpu.roll(to_y, 1, 1) + pltpu.roll(from_y, ny - 1, 1)
            )
        rs, ux, uy, temp = physical_variables(energy)
        pmsg[1, comp(0)] = ux
        pmsg[1, comp(1)] = uy
        pmsg[1, comp(2)] = -0.5 / temp
        pmsg[1, comp(3)] = rs / temp * (1.0 / (1.0 + rfull[mid]))
        share(1, full, range(nv))

        received(START)
        stepped = coarse(assembled(START, 16), band)
        for c in range(4):
            gs[c] = stepped[c]
            delta[c] = energy[c] - stepped[c]

        for c in range(4):
            corrected = gs[c] + delta[c]
            energy[c] = corrected
            pmsg[2, comp(c)] = jnp.where(w == 0, corrected, delta[c])
        share(2, full, range(AHEAD))
        if nw > 1:

            @pl.when(w == 0)
            def _():
                hand_on([energy[c] for c in range(4)], range(EARLY))

        share(2, full, range(AHEAD, nv))
        if nw > 1:

            @pl.when(w == 0)
            def _():
                hand_to(range(EARLY, nv))


    @pl.loop(0, chunks)
    def _(c):
        vx, vy0, half, _j = chunk_of(first, c)
        shift = ny - 1 - (ny - 2) * half
        ca = fine_ratio * jnp.abs(vx)
        for jj in range(HALF):
            k = c * HALF + jj
            cb = fine_ratio * jnp.abs(vy0 + jj * DVY)
            x = spad[k, main]
            star = (1.0 - ca - cb) * x + ca * spad[k, up] + cb * pltpu.roll(x, shift, 1)
            star2[k] = star * inv_main

    if nw > 2:

        @pl.when(is_owner & (w > 0) & (w + 1 < nw))
        def _():
            settle(chain, chain_recv.at[0])
            settle(chain_rows.at[1], chain_recv.at[1])
            settle(chain_rows.at[0], chain_recv.at[2])
            u = [
                jnp.concatenate(
                    [
                        chain[comp(c)],
                        jnp.where(
                            row8 == TILE - 1, chain_rows[0, pl.ds(c, 1)], chain_rows[1, pl.ds(c, 1)]
                        ),
                    ],
                    axis=0,
                )
                for c in range(4)
            ]
            stepped = coarse(u, band)
            hand_on([stepped[c] + delta[c] for c in range(4)], range(nv))

    def shared(n, size):
        rows = pl.ds(0, size)

        @pl.when(is_owner & (h == 1))
        def _():
            settle(pin.at[n, 0, rows], ag_recv.at[n])

        @pl.when(jnp.logical_not(is_owner & (h == 1)))
        def _():
            settle(pin.at[n, :, rows], ag_recv.at[n])

    shared(0, full + TILE)
    for n in range(4):
        for k in range(2):
            phys[n, pl.ds(2 * TILE + k * band, band)] = pin[0, k, comp(n)]
        phys[n, edge] = jnp.broadcast_to(pin[0, 1 - pos, pl.ds(full + n, 1)], (TILE, ny))
    for rows in (main, edge):
        drift, scale = phys[1, rows], phys[2, rows]
        for j in range(NVY):
            d = (-vel_max + (j + 0.5) * DVY) - drift
            e = jnp.exp(d * d * scale)
            yt[j, rows] = e
            if rows is main:
                yr[j] = pltpu.roll(e, ny - 1 if j < HALF else 1, 1)

    @pl.loop(0, chunks)
    def _(c):
        vx, vy0, half, j0 = chunk_of(first, c)
        shift = ny - 1 - (ny - 2) * half
        ca = fine_ratio * jnp.abs(vx)
        for rows in (main, edge):
            d = vx - phys[0, rows]
            xpad[rows] = phys[3, rows] * jnp.exp(d * d * phys[2, rows])
        x = xpad[main]
        here = inv_main * x
        behind = (ca * inv_main) * xpad[up]
        beside = inv_main * pltpu.roll(x, shift, 1)
        for jj in range(HALF):
            k = c * HALF + jj
            cb = fine_ratio * jnp.abs(vy0 + jj * DVY)
            star2[k] = (
                star2[k] + ((1.0 - ca - cb) * here) * yt[j0 + jj, main] + behind * yt[j0 + jj, up]
                + (cb * beside) * yr[j0 + jj]
            )

    shared(1, full)
    for k in range(2):
        rows = pl.ds(k * band, band)
        for n in range(4):
            e_phys[n, rows] = pin[1, k, comp(n)]
    drift, scale = e_phys[1], e_phys[2]
    for j in range(NVY):
        d = (-vel_max + (j + 0.5) * DVY) - drift
        ye[j] = jnp.exp(d * d * scale)
    shared(2, full)
    for k in range(2):
        for n in range(4):
            corr_out[n, pl.ds(k * band, band)] = pin[2, k, comp(n)]
    if nw > 1:

        @pl.when(w > 0)
        def _():
            settle(vrow_in, win_recv.at[0])
            settle(vin, win_recv.at[1])
            u = [
                jnp.concatenate(
                    [
                        vin[0, comp(c)], vin[1, comp(c)],
                        jnp.where(row8 == TILE - 1, vrow_in[1, pl.ds(c, 1)], vrow_in[0, pl.ds(c, 1)]),
                    ],
                    axis=0,
                )
                for c in range(4)
            ]
            stepped = coarse(u, nx)
            for c in range(4):
                corr_out[c] = stepped[c] + corr_out[c]

    for field in range(3):
        size = pl.ds(0, sizes[field])
        for k in range(2):
            own = to_owner(s, k)[1]

            @pl.when(jnp.logical_not(own))
            def _():
                settle(msg.at[field, k, size], rs_send.at[field])

    for k in range(2):
        own = to_owner(other, k)[1]

        @pl.when(jnp.logical_not(own))
        def _():
            for part in range(2):
                settle(xmsg.at[k, ACROSS_ROWS[part]], rs_send.at[3 + part])

    @pl.when(is_owner)
    def _():
        for n, size in ((0, full + TILE), (1, full), (2, full)):
            rows = pl.ds(0, size)
            for _ in range(nv - 1):
                settle(pmsg.at[n, rows], ag_send.at[n])

            @pl.when(h == 0)
            def _():
                settle(pmsg.at[n, rows], ag_send.at[n])

        if nw > 1:

            @pl.when(w + 1 < nw)
            def _():
                for _ in range(nv):
                    settle(vrow.at[b], win_send.at[0])
                    settle(vmsg, win_send.at[1])

            @pl.when(w + 2 < nw)
            def _():
                settle(vmsg, chain_send.at[0])
                settle(vrow.at[0], chain_send.at[1])
                settle(vrow.at[1], chain_send.at[2])


def lift_kernel(parts, star2, ye, e_phys, corr, lifted, corrected, yc, out, save_sem):
    count = star2.shape[0]
    first = lax.axis_index("vel") * count
    corrected[...] = corr[...]
    rs, uc, uy, temp = physical_variables(corr)
    sc = -0.5 / temp
    mc = rs / temp
    for j in range(NVY):
        d = (-vel_max + (j + 0.5) * DVY) - uy
        yc[j] = jnp.exp(d * d * sc)
    chunks = count // HALF
    per = chunks // parts

    def save(n):
        rows = pl.ds(n * per * HALF, per * HALF)
        return pltpu.make_async_copy(out.at[rows], lifted.at[rows], save_sem.at[n])

    for n in range(parts):

        @pl.loop(n * per, (n + 1) * per)
        def _(c):
            vx, _vy, _half, j0 = chunk_of(first, c)
            dc = vx - uc
            xc = mc * jnp.exp(dc * dc * sc)
            de = vx - e_phys[0]
            xe = e_phys[3] * jnp.exp(de * de * e_phys[2])
            for jj in range(HALF):
                k = c * HALF + jj
                out[k] = star2[k] + (xc * yc[j0 + jj] - xe * ye[j0 + jj])

        save(n).start()
    for n in range(parts):
        save(n).wait()


def per_device(nw, nv, f_start, relax_rate):
    field = f_start[0]
    count, nx, ny = field.shape
    band = nx // 2
    frame = band + TILE
    full = 4 * band
    pad = nx + 4 * TILE
    vmem = pltpu.VMEM
    dma = pltpu.SemaphoreType.DMA
    small = jax.ShapeDtypeStruct((4, nx, ny), f32)
    speeds = jax.ShapeDtypeStruct((NVY, nx, ny), f32)
    in_vmem = pl.BlockSpec(memory_space=pltpu.VMEM)
    in_hbm = pl.BlockSpec(memory_space=pltpu.HBM)
    field = pltpu.with_memory_space_constraint(field, pltpu.HBM)
    star2, ye, e_phys, corr = pl.pallas_call(
        functools.partial(advance_kernel, nw, nv),
        out_shape=(jax.ShapeDtypeStruct((count, nx, ny), f32), speeds, small, small),
        in_specs=[in_hbm, in_hbm],
        out_specs=(in_vmem,) * 4,
        scratch_shapes=[
            vmem((count, pad, ny), f32),
            vmem((count, pad, ny), f32),
            vmem((2 * nx, ny), f32),
            vmem((2, len(ORDERS), pad, ny), f32),
            vmem((2, len(ORDERS), pad, ny), f32),
            vmem((2, 4, TILE, ny), f32),
            vmem((3, 2, full + TILE, ny), f32),
            vmem((2, 3 * TILE, ny), f32),
            vmem((3, nv, full + TILE, ny), f32),
            vmem((nv, 3 * TILE, ny), f32),
            vmem((3 * TILE, ny), f32),
            vmem((TILE, ny), f32),
            vmem((4, frame, ny), f32),
            vmem((20, frame, ny), f32),
            vmem((4, band, ny), f32),
            vmem((4, band, ny), f32),
            vmem((4, band, ny), f32),
            vmem((3, full + TILE, ny), f32),
            vmem((3, 2, full + TILE, ny), f32),
            vmem((full, ny), f32),
            vmem((2, TILE, ny), f32),
            vmem((2, full, ny), f32),
            vmem((2, TILE, ny), f32),
            vmem((full, ny), f32),
            vmem((2, TILE, ny), f32),
            vmem((4, pad, ny), f32),
            vmem((pad, ny), f32),
            vmem((NVY, pad, ny), f32),
            vmem((NVY, nx, ny), f32),
            dma((1 + nx // TILE,)), dma((2,)), dma((2,)), dma((5,)), dma((5,)), dma((3,)), dma((3,)),
            dma((2,)), dma((2,)), dma((3,)), dma((3,)), pltpu.SemaphoreType.REGULAR,
        ],
        compiler_params=pltpu.CompilerParams(
            collective_id=0, has_side_effects=True, vmem_limit_bytes=40 << 20
        ),
        name="advance",
    )(field, pltpu.with_memory_space_constraint(relax_rate, pltpu.HBM))

    chunks = count // HALF
    parts = next(n for n in (6, 4, 3, 2, 1) if chunks % n == 0)
    lifted, corrected = pl.pallas_call(
        functools.partial(lift_kernel, parts),
        out_shape=(jax.ShapeDtypeStruct((count, nx, ny), f32), small),
        in_specs=[in_vmem] * 4,
        out_specs=(in_hbm, in_vmem),
        scratch_shapes=[
            vmem((NVY, nx, ny), f32), vmem((count, nx, ny), f32), dma((parts,)),
        ],
        compiler_params=pltpu.CompilerParams(vmem_limit_bytes=16 << 20),
        name="lift",
    )(star2, ye, e_phys, corr)
    return corrected[None], lifted[None]


def solution(mesh):
    return jax.shard_map(
        functools.partial(per_device, mesh.shape["win"], mesh.shape["vel"]),
        mesh=mesh,
        in_specs=(P("win", "vel", "sp", None), P("sp", None)),
        out_specs=(P("win", None, "sp", None), P("win", "vel", "sp", None)),
        check_vma=False,
    )
```

```python
import functools
import math

import jax
import jax.numpy as jnp
from jax import lax
from jax.experimental import pallas as pl
from jax.experimental.pallas import tpu as pltpu
from jax.sharding import PartitionSpec as P

NVX = 48
NVY = 32
HALF = NVY // 2
TILE = 8
vel_max = 6.0
fine_ratio = 0.075
coarse_ratio = 0.15
density_floor = 0.3
thermal_lower_bound = 0.3
DVX = 2.0 * vel_max / NVX
DVY = 2.0 * vel_max / NVY
WEIGHT = DVX * DVY / (2.0 * math.pi)
MESH = pl.DeviceIdType.MESH
f32 = jnp.float32
ORDERS = [(p, q) for p in range(5) for q in range(5 - p)]
PLACE = {order: n for n, order in enumerate(ORDERS)}
MAIN = [(0, 0), (0, 1), (1, 0), (0, 2), (2, 0)]
FIRST, START, SECOND = range(3)
AHEAD = 1
EARLY = 4


def physical_variables(u):
    rs = jnp.maximum(u[0], density_floor)
    ux = u[1] / rs
    uy = u[2] / rs
    temp = jnp.maximum((u[3] - 0.5 * (u[1] * ux + u[2] * uy)) / rs, thermal_lower_bound)
    return rs, ux, uy, temp


def chunk_of(first, c):
    k = first + c * HALF
    i = k // NVY
    j = k % NVY
    vx = -vel_max + (i.astype(f32) + 0.5) * DVX
    vy = -vel_max + (j.astype(f32) + 0.5) * DVY
    return vx, vy, j // HALF, j


def coarse(u, band):
    rows, ny = u[0].shape
    rs, ux, uy, temp = physical_variables(u)
    p = rs * temp
    wave = jnp.sqrt(2.0 * temp)
    fx = [u[1], u[1] * ux + p, u[2] * ux, (u[3] + p) * ux]
    fy = [u[2], u[1] * uy, u[2] * uy + p, (u[3] + p) * uy]
    sx = jnp.abs(ux) + wave
    sy = jnp.abs(uy) + wave
    mx = jnp.maximum(sx, pltpu.roll(sx, rows - 1, 0))
    my = jnp.maximum(sy, pltpu.roll(sy, ny - 1, 1))
    out = []
    for c in range(4):
        face_x = 0.5 * (fx[c] + pltpu.roll(fx[c], rows - 1, 0)) - 0.5 * mx * (
            pltpu.roll(u[c], rows - 1, 0) - u[c]
        )
        face_y = 0.5 * (fy[c] + pltpu.roll(fy[c], ny - 1, 1)) - 0.5 * my * (
            pltpu.roll(u[c], ny - 1, 1) - u[c]
        )
        g = u[c] - coarse_ratio * (
            face_x - pltpu.roll(face_x, 1, 0) + (face_y - pltpu.roll(face_y, 1, 1))
        )
        out.append(g[:band])
    return out


def advance_kernel(
    nw, nv,
    f, r, star2, ye, e_phys, corr_out,
    fpad, spad, rfull, bsum, hsum, gout, msg, xmsg, red, redx, xs, es, fr, flux, energy, delta, gs,
    pmsg, pin, vmsg, vrow, vin, vrow_in, chain, chain_rows, phys, xpad, yt, yr,
    load_sem, halo_send, halo_recv, rs_send, rs_recv, ag_send, ag_recv, win_send, win_recv,
    chain_send, chain_recv, ready,
):
    w, v, s = lax.axis_index("win"), lax.axis_index("vel"), lax.axis_index("sp")
    count, nx, ny = f.shape
    chunks = count // HALF
    first = v * count
    other = 1 - s
    pos = (2 * v) // nv
    band = nx // 2
    frame = band + TILE
    full = 4 * band
    main = pl.ds(2 * TILE, nx)
    end = 2 * TILE + nx
    up = pl.ds(2 * TILE + 1 - 2 * pos, nx)
    hb = pl.multiple_of(end - (end - TILE) * pos, TILE)
    edge = pl.ds(hb, TILE)
    edge_up = pl.ds(hb + 1 - 2 * pos, TILE)
    ho = pl.multiple_of(TILE + (end - TILE) * pos, TILE)
    away = pl.ds(ho, TILE)
    away_up = pl.ds(ho + 1 - 2 * pos, TILE)
    tiles = nx // TILE

    base = nv // 2 - 2
    off = v - base
    is_owner = (s == 1) & (off >= 0) & (off < 4)
    b = off // 2
    h = (off + b) % 2
    g = 2 * h + b

    def owner_at(half, k):
        return base + (half if k == 0 else 3 - half)

    def load_f(t):
        rows = pl.ds(pl.multiple_of(t * TILE, TILE), TILE)
        padded = pl.ds(pl.multiple_of((t + 2) * TILE, TILE), TILE)
        return pltpu.make_async_copy(f.at[:, rows], fpad.at[:, padded], load_sem.at[t])

    for t in range(tiles):
        load_f(t).start()
    mine = pl.ds(pl.multiple_of(s * nx, TILE), nx)
    load_r = pltpu.make_async_copy(r, rfull.at[mine], load_sem.at[tiles])
    load_r.start()

    def signal(device):
        pl.semaphore_signal(barrier, inc=1, device_id=device, device_id_type=MESH)

    barrier = pltpu.get_barrier_semaphore()
    signal((w, v, other))
    for o in range(4):

        @pl.when(jnp.logical_not((v == base + o) & (s == 1)))
        def _():
            signal((w, base + o, 1))

    @pl.when(is_owner)
    def _():
        signal((w, v, 0))
        for d in range(1, nv):
            for half in range(2):
                signal((w, lax.rem(v + d, nv), half))

        @pl.when(w + 1 < nw)
        def _():
            for n in range(nv):
                for half in range(2):
                    signal((w + 1, n, half))

    def remote(src, dst, send, recv, device):
        return pltpu.make_async_remote_copy(
            src_ref=src, dst_ref=dst, send_sem=send, recv_sem=recv,
            device_id=device, device_id_type=MESH,
        )

    def settle(ref, sem):
        pltpu.make_async_copy(ref, ref, sem).wait()

    empty = jnp.zeros((TILE, ny), f32)
    for side in range(2):
        for n in range(len(ORDERS)):
            for at in (TILE, end):
                bsum[side, n, pl.ds(at, TILE)] = empty
                hsum[side, n, pl.ds(at, TILE)] = empty

    parity = (first // HALF) % 2
    rounds = (chunks + 1) // 2

    @pl.loop(0, tiles)
    def _(t):
        load_f(t).wait()
        rows = pl.ds(pl.multiple_of(2 * TILE + t * TILE, TILE), TILE)
        for side in range(2):
            acc = {order: jnp.zeros((TILE, ny), f32) for order in ORDERS}
            for n in range(rounds):
                c = (side + parity) % 2 + 2 * n
                weight = 1.0
                if chunks % 2:
                    weight = jnp.where(c < chunks, 1.0, 0.0).astype(f32)
                    c = jnp.minimum(c, chunks - 1)
                vx = chunk_of(first, c)[0]
                sums = [jnp.zeros((TILE, ny), f32)] * 5
                for jj in range(HALF // 2, HALF):
                    tt = (jj + 0.5) * DVY - 0.5 * vel_max
                    high = fpad[c * HALF + jj, rows]
                    low = fpad[c * HALF + HALF - 1 - jj, rows]
                    even, odd = high + low, high - low
                    sums = [
                        sums[0] + even, sums[1] + tt * odd, sums[2] + tt**2 * even,
                        sums[3] + tt**3 * odd, sums[4] + tt**4 * even,
                    ]
                power = weight
                for q in range(5):
                    for m in range(5 - q):
                        term = sums[m] if q == 0 and chunks % 2 == 0 else sums[m] * power
                        acc[m, q] = acc[m, q] + term
                    power = power * vx
            centre = (side - 0.5) * vel_max
            for p, q in ORDERS:
                total = acc[p, q]
                for m in range(p):
                    total = total + (math.comb(p, m) * centre ** (p - m)) * acc[m, q]
                bsum[side, PLACE[p, q], rows] = total

    def components(get):
        return [
            WEIGHT * get(0, 0), WEIGHT * get(0, 1), WEIGHT * get(1, 0),
            (0.5 * WEIGHT) * (get(0, 2) + get(2, 0)),
        ]

    def fill(field, values):
        for c in range(4):
            for k in range(2):
                msg[field, k, pl.ds(c * band, band)] = values[c][k * band : (k + 1) * band]

    def fill_edges(field):
        for c in range(4):
            for k in range(2):
                if field == FIRST:
                    outer = gout[0, c, pl.ds(TILE - 1 if k == 0 else 0, 1)]
                else:
                    outer = jnp.zeros((1, ny), f32)
                msg[field, k, pl.ds(full + c, 1)] = outer
                inner = c * band if k == 0 else (c + 1) * band - 1
                msg[field, k, pl.ds(full + 4 + c, 1)] = msg[field, 1 - k, pl.ds(inner, 1)]

    def to_owner(half, k):
        target = owner_at(half, k)
        return target, (v == target) & (s == 1)

    sizes = {FIRST: full + TILE, START: full + TILE, SECOND: full}

    def scatter(field):
        size = pl.ds(0, sizes[field])
        for k in range(2):
            target, own = to_owner(s, k)

            @pl.when(own)
            def _():
                red[field, v, size] = msg[field, k, size]

            @pl.when(jnp.logical_not(own))
            def _():
                remote(
                    msg.at[field, k, size], red.at[field, v, size],
                    rs_send.at[field], rs_recv.at[field], (w, target, 1),
                ).start()

    ACROSS_ROWS = (pl.ds(0, TILE), pl.ds(TILE, 2 * TILE))

    def scatter_across(part):
        rows = ACROSS_ROWS[part]
        for k in range(2):
            target, own = to_owner(other, k)

            @pl.when(own)
            def _():
                redx[v, rows] = xmsg[k, rows]

            @pl.when(jnp.logical_not(own))
            def _():
                remote(
                    xmsg.at[k, rows], redx.at[v, rows],
                    rs_send.at[3 + part], rs_recv.at[3 + part], (w, target, 1),
                ).start()

    fill(START, components(lambda p, q: bsum[0, PLACE[p, q], main] + bsum[1, PLACE[p, q], main]))
    fill_edges(START)

    pl.semaphore_wait(barrier, jnp.where(is_owner, 2 * nv + 3, 5) + jnp.where(w > 0, 4, 0))

    @pl.when(w > 0)
    def _():
        for o in range(4):
            pl.semaphore_signal(ready, inc=1, device_id=(w - 1, base + o, 1), device_id_type=MESH)

    load_r.wait()
    source = pl.ds(pl.multiple_of((nx - TILE) * pos, TILE), TILE)
    halo_r = remote(r, rfull.at[mine], halo_send.at[0], halo_recv.at[0], (w, v, other))
    halo_f = remote(f.at[:, source], fpad.at[:, edge], halo_send.at[1], halo_recv.at[1], (w, v, other))
    halo_r.start()
    halo_f.start()

    inv_main = 1.0 / (1.0 + rfull[mine])
    along = fine_ratio * (2 * pos - 1).astype(f32)
    ACROSS = ((-fine_ratio, ny - 1), (fine_ratio, 1))

    def moved(table, side, p, q, rows, rows_up):
        across, shift = ACROSS[side]
        bx = table[side, PLACE[p, q + 1], rows]
        by = table[side, PLACE[p + 1, q], rows]
        return (
            table[side, PLACE[p, q], rows]
            + along * (table[side, PLACE[p, q + 1], rows_up] - bx)
            + across * (pltpu.roll(by, shift, 1) - by)
        )

    star_main, star_away = {}, {}

    def one_step(side, p, q):
        star = moved(bsum, side, p, q, main, up)
        beyond = moved(bsum, side, p, q, away, away_up)
        hsum[side, PLACE[p, q], main] = star * inv_main
        hsum[side, PLACE[p, q], away] = beyond
        return star, beyond

    for order in MAIN:
        parts = [one_step(side, *order) for side in range(2)]
        star_main[order] = parts[0][0] + parts[1][0]
        star_away[order] = parts[0][1] + parts[1][1]
    fill(FIRST, components(lambda p, q: star_main[p, q]))
    for c, value in enumerate(components(lambda p, q: star_away[p, q])):
        gout[0, c] = value
    fill_edges(FIRST)
    for k in range(2):
        last = band - 1 if k == 0 else 0
        for c in range(4):
            xmsg[k, pl.ds(c, 1)] = msg[FIRST, 1 - k, pl.ds(c * band + last, 1)]
            xmsg[k, pl.ds(4 + c, 1)] = gout[0, c, pl.ds(0 if k == 0 else TILE - 1, 1)]
    scatter_across(0)
    scatter(FIRST)
    for p, q in ORDERS:
        if p + q < 4 and (p, q) not in MAIN:
            for side in range(2):
                one_step(side, p, q)
    again = {o: moved(hsum, 0, *o, main, up) + moved(hsum, 1, *o, main, up) for o in MAIN}
    fill(SECOND, components(lambda p, q: again[p, q]))
    scatter(SECOND)

    halo_r.wait()
    theirs = other * nx
    inv_away = 1.0 / (1.0 + rfull[pl.ds(theirs + (nx - 1) * (1 - pos), 1)])
    inv_edge = 1.0 / (1.0 + rfull[pl.ds(pl.multiple_of(theirs + (nx - TILE) * pos, TILE), TILE)])
    for side in range(2):
        for p, q in ORDERS:
            if p + q < 4:
                hsum[side, PLACE[p, q], away] = hsum[side, PLACE[p, q], away] * inv_away
    again = {o: moved(hsum, 0, *o, away, away_up) + moved(hsum, 1, *o, away, away_up) for o in MAIN}
    for c, value in enumerate(components(lambda p, q: again[p, q])):
        gout[1, c] = value
    for k in range(2):
        last = band - 1 if k == 0 else 0
        near, far = (0, 1) if k == 0 else (TILE - 1, TILE - 2)
        for c in range(4):
            xmsg[k, pl.ds(8 + c, 1)] = gout[1, c, pl.ds(near, 1)]
            xmsg[k, pl.ds(12 + c, 1)] = gout[1, c, pl.ds(far, 1)]
            xmsg[k, pl.ds(16 + c, 1)] = msg[START, 1 - k, pl.ds(c * band + last, 1)]
            xmsg[k, pl.ds(20 + c, 1)] = jnp.zeros((1, ny), f32)
    scatter_across(1)
    halo_f.wait()

    def first_transport(c):
        vx, vy0, half, _j = chunk_of(first, c)
        shift = ny - 1 - (ny - 2) * half
        ca = fine_ratio * jnp.abs(vx)
        for jj in range(HALF):
            k = c * HALF + jj
            cb = fine_ratio * jnp.abs(vy0 + jj * DVY)
            cc = 1.0 - ca - cb
            x = fpad[k, main]
            spad[k, main] = (cc * x + ca * fpad[k, up] + cb * pltpu.roll(x, shift, 1)) * inv_main
            x = fpad[k, edge]
            spad[k, edge] = (cc * x + ca * fpad[k, edge_up] + cb * pltpu.roll(x, shift, 1)) * inv_edge

    pl.loop(0, chunks // 4)(first_transport)
    scatter(START)
    pl.loop(chunks // 4, chunks)(first_transport)

    row8 = lax.broadcasted_iota(jnp.int32, (TILE, ny), 0)
    row_band = lax.broadcasted_iota(jnp.int32, (band, ny), 0)
    brow = (band - 1) * b
    brow2 = 1 + (band - 3) * b

    def received(field):
        size = pl.ds(0, sizes[field])

        @pl.when(h == 1)
        def _():
            settle(red.at[field, pl.ds(0, nv - 1), size], rs_recv.at[field])

        @pl.when(h == 0)
        def _():
            settle(red.at[field, :, size], rs_recv.at[field])

    def summed(field, rows):
        total = red[field, 0, rows]
        for n in range(1, nv):
            total = total + red[field, n, rows]
        return total

    def comp(c):
        return pl.ds(c * band, band)

    def framed(value, outer, inner):
        above = jnp.where(b == 0, outer, inner)
        below = jnp.where(b == 0, inner, outer)
        return jnp.concatenate([value, jnp.where(row8 == TILE - 1, above, below)], axis=0)

    def placed(row, at):
        return jnp.where(row_band == at, row, 0.0)

    def share(n, size, targets):
        rows = pl.ds(0, size)
        for d in targets:

            def send(d=d):
                remote(
                    pmsg.at[n, rows], pin.at[n, b, rows], ag_send.at[n], ag_recv.at[n], (w, d, h)
                ).start()

            if base <= d < base + 4:
                own = (h == 1) & (v == d)
                pl.when(jnp.logical_not(own))(send)

                @pl.when(own)
                def _():
                    pin[n, b, rows] = pmsg[n, rows]
            else:
                send()

    def place(n):
        half, k = n // 2, n % 2
        return base + half + k * (3 - 2 * half)

    def along_chain():
        after, before = lax.rem(g + 1, 4), lax.rem(g + 3, 4)
        return [
            remote(vmsg, chain, chain_send.at[0], chain_recv.at[0], (w + 1, v, 1)),
            remote(vrow.at[0], chain_rows.at[1], chain_send.at[1], chain_recv.at[1], (w + 1, place(before), 1)),
            remote(vrow.at[1], chain_rows.at[0], chain_send.at[2], chain_recv.at[2], (w + 1, place(after), 1)),
        ]

    def hand_to(targets):
        for d in targets:
            remote(vrow.at[b], vrow_in.at[b], win_send.at[0], win_recv.at[0], (w + 1, d, 1 - h)).start()
            remote(vmsg, vin.at[b], win_send.at[1], win_recv.at[1], (w + 1, d, h)).start()

    def hand_on(values, targets):
        for c in range(4):
            vmsg[comp(c)] = values[c]
            for row, value in ((0, values[c][:1]), (1, values[c][-1:])):
                vrow[row, pl.ds(c, 1)] = value
                vrow[row, pl.ds(4 + c, 1)] = value
        pl.semaphore_wait(ready, 2 * nv)

        @pl.when(w + 2 < nw)
        def _():
            for copy in along_chain():
                copy.start()

        hand_to(targets)

    @pl.when(is_owner)
    def _():
        def received_across(part):
            rows = ACROSS_ROWS[part]

            @pl.when(h == 1)
            def _():
                settle(redx.at[:, rows], rs_recv.at[3 + part])

            @pl.when(h == 0)
            def _():
                settle(redx.at[pl.ds(0, nv - 1), rows], rs_recv.at[3 + part])

            across = redx[0, rows]
            for n in range(1, nv):
                across = across + redx[n, rows]
            xs[rows] = across

        received(FIRST)
        received_across(0)

        def x_row(n):
            return xs[pl.ds(n, 1)]

        def assembled(field, at):
            es[...] = summed(field, pl.ds(full, TILE))
            out = []
            for c in range(4):
                value = summed(field, comp(c))
                if field == FIRST:
                    value = value + placed(x_row(4 + c), brow)
                out.append(framed(value, es[pl.ds(c, 1)] + x_row(at + c), es[pl.ds(4 + c, 1)]))
            return out

        rs, ux, uy, temp = physical_variables(assembled(FIRST, 0))
        rows_all = 2 * nx
        mid = pl.ds(pl.multiple_of(g * band, TILE), band)
        above = rfull[pl.ds(lax.rem(g * band + rows_all - 1, rows_all), 1)]
        below = rfull[pl.ds(lax.rem(g * band + band, rows_all), 1)]
        rate = jnp.concatenate([rfull[mid], jnp.where(row8 == TILE - 1, above, below)], axis=0)
        fr[0] = ux
        fr[1] = uy
        fr[2] = -0.5 / temp
        fr[3] = rs / temp * (rate / (1.0 + rate))
        for n in range(4):
            pmsg[0, comp(n)] = fr[n, pl.ds(0, band)]
            outer = fr[n, pl.ds(band + (TILE - 1) * (1 - b), 1)]
            pmsg[0, pl.ds(full + n, 1)] = outer
            pmsg[0, pl.ds(full + 4 + n, 1)] = outer
        share(0, full + TILE, range(nv))

        @pl.loop(0, frame // TILE)
        def _(t):
            rows = pl.ds(pl.multiple_of(t * TILE, TILE), TILE)
            ux, uy, scale, amp = [fr[n, rows] for n in range(4)]

            def half_sums(speeds, drift):
                weights = []
                for speed in speeds:
                    d = speed - drift
                    weights.append(jnp.exp(d * d * scale))
                sides = []
                half = len(speeds) // 2
                for at, c in ((half, 0.5 * vel_max), (0, -0.5 * vel_max)):
                    m = [empty] * 4
                    for n in range(half // 2, half):
                        t = speeds[at + n] - c
                        high, low = weights[at + n], weights[at + half - 1 - n]
                        even, odd = high + low, high - low
                        m = [m[0] + even, m[1] + t * odd, m[2] + t**2 * even, m[3] + t**3 * odd]
                    sides.append([
                        m[0],
                        m[1] + c * m[0],
                        m[2] + (2 * c) * m[1] + c**2 * m[0],
                        m[3] + (3 * c) * m[2] + (3 * c**2) * m[1] + c**3 * m[0],
                    ])
                return sides

            xp, xm = half_sums([-vel_max + (i + 0.5) * DVX for i in range(NVX)], ux)
            yp, ym = half_sums([-vel_max + (j + 0.5) * DVY for j in range(NVY)], uy)
            xs_ = [x + y for x, y in zip(xp, xm)]
            ys_ = [x + y for x, y in zip(yp, ym)]
            amp = WEIGHT * amp

            def store(n, coef, x, y):
                x = [coef * amp * t for t in x]
                flux[n, rows] = x[0] * y[0]
                flux[n + 1, rows] = x[1] * y[0]
                flux[n + 2, rows] = x[0] * y[1]
                flux[n + 3, rows] = 0.5 * (x[2] * y[0] + x[0] * y[2])

            store(0, 1.0, xs_, ys_)
            store(4, fine_ratio, xp[1:], ys_)
            store(8, -fine_ratio, xm[1:], ys_)
            store(12, fine_ratio, xs_, yp[1:])
            store(16, -fine_ratio, xs_, ym[1:])

        received(SECOND)
        received_across(1)
        inner = pl.ds(0, band)
        for c in range(4):
            to_y, from_y = flux[12 + c, inner], flux[16 + c, inner]
            energy[c] = (
                summed(SECOND, comp(c)) + placed(x_row(8 + c), brow) + placed(x_row(12 + c), brow2)
            ) + (
                flux[c, inner] - flux[4 + c, inner] - flux[8 + c, inner] - to_y - from_y
                + pltpu.roll(flux[4 + c], 1, 0)[:band] + pltpu.roll(flux[8 + c], frame - 1, 0)[:band]
                + pltpu.roll(to_y, 1, 1) + pltpu.roll(from_y, ny - 1, 1)
            )
        rs, ux, uy, temp = physical_variables(energy)
        pmsg[1, comp(0)] = ux
        pmsg[1, comp(1)] = uy
        pmsg[1, comp(2)] = -0.5 / temp
        pmsg[1, comp(3)] = rs / temp * (1.0 / (1.0 + rfull[mid]))
        share(1, full, range(nv))

        received(START)
        stepped = coarse(assembled(START, 16), band)
        for c in range(4):
            gs[c] = stepped[c]
            delta[c] = energy[c] - stepped[c]

        for c in range(4):
            corrected = gs[c] + delta[c]
            energy[c] = corrected
            pmsg[2, comp(c)] = jnp.where(w == 0, corrected, delta[c])
        share(2, full, range(AHEAD))
        if nw > 1:

            @pl.when(w == 0)
            def _():
                hand_on([energy[c] for c in range(4)], range(EARLY))

        share(2, full, range(AHEAD, nv))
        if nw > 1:

            @pl.when(w == 0)
            def _():
                hand_to(range(EARLY, nv))


    @pl.loop(0, chunks)
    def _(c):
        vx, vy0, half, _j = chunk_of(first, c)
        shift = ny - 1 - (ny - 2) * half
        ca = fine_ratio * jnp.abs(vx)
        for jj in range(HALF):
            k = c * HALF + jj
            cb = fine_ratio * jnp.abs(vy0 + jj * DVY)
            x = spad[k, main]
            star = (1.0 - ca - cb) * x + ca * spad[k, up] + cb * pltpu.roll(x, shift, 1)
            star2[k] = star * inv_main

    if nw > 2:

        @pl.when(is_owner & (w > 0) & (w + 1 < nw))
        def _():
            settle(chain, chain_recv.at[0])
            settle(chain_rows.at[1], chain_recv.at[1])
            settle(chain_rows.at[0], chain_recv.at[2])
            u = [
                jnp.concatenate(
                    [
                        chain[comp(c)],
                        jnp.where(
                            row8 == TILE - 1, chain_rows[0, pl.ds(c, 1)], chain_rows[1, pl.ds(c, 1)]
                        ),
                    ],
                    axis=0,
                )
                for c in range(4)
            ]
            stepped = coarse(u, band)
            hand_on([stepped[c] + delta[c] for c in range(4)], range(nv))

    def shared(n, size):
        rows = pl.ds(0, size)

        @pl.when(is_owner & (h == 1))
        def _():
            settle(pin.at[n, 0, rows], ag_recv.at[n])

        @pl.when(jnp.logical_not(is_owner & (h == 1)))
        def _():
            settle(pin.at[n, :, rows], ag_recv.at[n])

    shared(0, full + TILE)
    for n in range(4):
        for k in range(2):
            phys[n, pl.ds(2 * TILE + k * band, band)] = pin[0, k, comp(n)]
        phys[n, edge] = jnp.broadcast_to(pin[0, 1 - pos, pl.ds(full + n, 1)], (TILE, ny))
    for rows in (main, edge):
        drift, scale = phys[1, rows], phys[2, rows]
        for j in range(NVY):
            d = (-vel_max + (j + 0.5) * DVY) - drift
            e = jnp.exp(d * d * scale)
            yt[j, rows] = e
            if rows is main:
                yr[j] = pltpu.roll(e, ny - 1 if j < HALF else 1, 1)

    @pl.loop(0, chunks)
    def _(c):
        vx, vy0, half, j0 = chunk_of(first, c)
        shift = ny - 1 - (ny - 2) * half
        ca = fine_ratio * jnp.abs(vx)
        for rows in (main, edge):
            d = vx - phys[0, rows]
            xpad[rows] = phys[3, rows] * jnp.exp(d * d * phys[2, rows])
        x = xpad[main]
        here = inv_main * x
        behind = (ca * inv_main) * xpad[up]
        beside = inv_main * pltpu.roll(x, shift, 1)
        for jj in range(HALF):
            k = c * HALF + jj
            cb = fine_ratio * jnp.abs(vy0 + jj * DVY)
            star2[k] = (
                star2[k] + ((1.0 - ca - cb) * here) * yt[j0 + jj, main] + behind * yt[j0 + jj, up]
                + (cb * beside) * yr[j0 + jj]
            )

    shared(1, full)
    for k in range(2):
        rows = pl.ds(k * band, band)
        for n in range(4):
            e_phys[n, rows] = pin[1, k, comp(n)]
    drift, scale = e_phys[1], e_phys[2]
    for j in range(NVY):
        d = (-vel_max + (j + 0.5) * DVY) - drift
        ye[j] = jnp.exp(d * d * scale)
    shared(2, full)
    for k in range(2):
        for n in range(4):
            corr_out[n, pl.ds(k * band, band)] = pin[2, k, comp(n)]
    if nw > 1:

        @pl.when(w > 0)
        def _():
            settle(vrow_in, win_recv.at[0])
            settle(vin, win_recv.at[1])
            u = [
                jnp.concatenate(
                    [
                        vin[0, comp(c)], vin[1, comp(c)],
                        jnp.where(row8 == TILE - 1, vrow_in[1, pl.ds(c, 1)], vrow_in[0, pl.ds(c, 1)]),
                    ],
                    axis=0,
                )
                for c in range(4)
            ]
            stepped = coarse(u, nx)
            for c in range(4):
                corr_out[c] = stepped[c] + corr_out[c]

    for field in range(3):
        size = pl.ds(0, sizes[field])
        for k in range(2):
            own = to_owner(s, k)[1]

            @pl.when(jnp.logical_not(own))
            def _():
                settle(msg.at[field, k, size], rs_send.at[field])

    for k in range(2):
        own = to_owner(other, k)[1]

        @pl.when(jnp.logical_not(own))
        def _():
            for part in range(2):
                settle(xmsg.at[k, ACROSS_ROWS[part]], rs_send.at[3 + part])

    @pl.when(is_owner)
    def _():
        for n, size in ((0, full + TILE), (1, full), (2, full)):
            rows = pl.ds(0, size)
            for _ in range(nv - 1):
                settle(pmsg.at[n, rows], ag_send.at[n])

            @pl.when(h == 0)
            def _():
                settle(pmsg.at[n, rows], ag_send.at[n])

        if nw > 1:

            @pl.when(w + 1 < nw)
            def _():
                for _ in range(nv):
                    settle(vrow.at[b], win_send.at[0])
                    settle(vmsg, win_send.at[1])

            @pl.when(w + 2 < nw)
            def _():
                settle(vmsg, chain_send.at[0])
                settle(vrow.at[0], chain_send.at[1])
                settle(vrow.at[1], chain_send.at[2])


def lift_kernel(parts, star2, ye, e_phys, corr, lifted, corrected, yc, out, save_sem):
    count = star2.shape[0]
    first = lax.axis_index("vel") * count
    corrected[...] = corr[...]
    rs, uc, uy, temp = physical_variables(corr)
    sc = -0.5 / temp
    mc = rs / temp
    for j in range(NVY):
        d = (-vel_max + (j + 0.5) * DVY) - uy
        yc[j] = jnp.exp(d * d * sc)
    chunks = count // HALF
    per = chunks // parts

    def save(n):
        rows = pl.ds(n * per * HALF, per * HALF)
        return pltpu.make_async_copy(out.at[rows], lifted.at[rows], save_sem.at[n])

    for n in range(parts):

        @pl.loop(n * per, (n + 1) * per)
        def _(c):
            vx, _vy, _half, j0 = chunk_of(first, c)
            dc = vx - uc
            xc = mc * jnp.exp(dc * dc * sc)
            de = vx - e_phys[0]
            xe = e_phys[3] * jnp.exp(de * de * e_phys[2])
            for jj in range(HALF):
                k = c * HALF + jj
                out[k] = star2[k] + (xc * yc[j0 + jj] - xe * ye[j0 + jj])

        save(n).start()
    for n in range(parts):
        save(n).wait()


def per_device(nw, nv, f_start, relax_rate):
    field = f_start[0]
    count, nx, ny = field.shape
    band = nx // 2
    frame = band + TILE
    full = 4 * band
    pad = nx + 4 * TILE
    vmem = pltpu.VMEM
    dma = pltpu.SemaphoreType.DMA
    small = jax.ShapeDtypeStruct((4, nx, ny), f32)
    speeds = jax.ShapeDtypeStruct((NVY, nx, ny), f32)
    in_vmem = pl.BlockSpec(memory_space=pltpu.VMEM)
    in_hbm = pl.BlockSpec(memory_space=pltpu.HBM)
    field = pltpu.with_memory_space_constraint(field, pltpu.HBM)
    star2, ye, e_phys, corr = pl.pallas_call(
        functools.partial(advance_kernel, nw, nv),
        out_shape=(jax.ShapeDtypeStruct((count, nx, ny), f32), speeds, small, small),
        in_specs=[in_hbm, in_hbm],
        out_specs=(in_vmem,) * 4,
        scratch_shapes=[
            vmem((count, pad, ny), f32),
            vmem((count, pad, ny), f32),
            vmem((2 * nx, ny), f32),
            vmem((2, len(ORDERS), pad, ny), f32),
            vmem((2, len(ORDERS), pad, ny), f32),
            vmem((2, 4, TILE, ny), f32),
            vmem((3, 2, full + TILE, ny), f32),
            vmem((2, 3 * TILE, ny), f32),
            vmem((3, nv, full + TILE, ny), f32),
            vmem((nv, 3 * TILE, ny), f32),
            vmem((3 * TILE, ny), f32),
            vmem((TILE, ny), f32),
            vmem((4, frame, ny), f32),
            vmem((20, frame, ny), f32),
            vmem((4, band, ny), f32),
            vmem((4, band, ny), f32),
            vmem((4, band, ny), f32),
            vmem((3, full + TILE, ny), f32),
            vmem((3, 2, full + TILE, ny), f32),
            vmem((full, ny), f32),
            vmem((2, TILE, ny), f32),
            vmem((2, full, ny), f32),
            vmem((2, TILE, ny), f32),
            vmem((full, ny), f32),
            vmem((2, TILE, ny), f32),
            vmem((4, pad, ny), f32),
            vmem((pad, ny), f32),
            vmem((NVY, pad, ny), f32),
            vmem((NVY, nx, ny), f32),
            dma((1 + nx // TILE,)), dma((2,)), dma((2,)), dma((5,)), dma((5,)), dma((3,)), dma((3,)),
            dma((2,)), dma((2,)), dma((3,)), dma((3,)), pltpu.SemaphoreType.REGULAR,
        ],
        compiler_params=pltpu.CompilerParams(
            collective_id=0, has_side_effects=True, vmem_limit_bytes=40 << 20
        ),
        name="advance",
    )(field, pltpu.with_memory_space_constraint(relax_rate, pltpu.HBM))

    chunks = count // HALF
    parts = next(n for n in (12, 6, 4, 3, 2, 1) if chunks % n == 0)
    lifted, corrected = pl.pallas_call(
        functools.partial(lift_kernel, parts),
        out_shape=(jax.ShapeDtypeStruct((count, nx, ny), f32), small),
        in_specs=[in_vmem] * 4,
        out_specs=(in_hbm, in_vmem),
        scratch_shapes=[
            vmem((NVY, nx, ny), f32), vmem((count, nx, ny), f32), dma((parts,)),
        ],
        compiler_params=pltpu.CompilerParams(vmem_limit_bytes=16 << 20),
        name="lift",
    )(star2, ye, e_phys, corr)
    return corrected[None], lifted[None]


def solution(mesh):
    return jax.shard_map(
        functools.partial(per_device, mesh.shape["win"], mesh.shape["vel"]),
        mesh=mesh,
        in_specs=(P("win", "vel", "sp", None), P("sp", None)),
        out_specs=(P("win", None, "sp", None), P("win", "vel", "sp", None)),
        check_vma=False,
    )
```

```python
import functools
import math

import jax
import jax.numpy as jnp
from jax import lax
from jax.experimental import pallas as pl
from jax.experimental.pallas import tpu as pltpu
from jax.sharding import PartitionSpec as P

NVX = 48
NVY = 32
HALF = NVY // 2
TILE = 8
vel_max = 6.0
fine_ratio = 0.075
coarse_ratio = 0.15
density_floor = 0.3
thermal_lower_bound = 0.3
DVX = 2.0 * vel_max / NVX
DVY = 2.0 * vel_max / NVY
WEIGHT = DVX * DVY / (2.0 * math.pi)
MESH = pl.DeviceIdType.MESH
f32 = jnp.float32
ORDERS = [(p, q) for p in range(5) for q in range(5 - p)]
PLACE = {order: n for n, order in enumerate(ORDERS)}
MAIN = [(0, 0), (0, 1), (1, 0), (0, 2), (2, 0)]
FIRST, START, SECOND = range(3)
AHEAD = 1
EARLY = 4


def physical_variables(u):
    rs = jnp.maximum(u[0], density_floor)
    ux = u[1] / rs
    uy = u[2] / rs
    temp = jnp.maximum((u[3] - 0.5 * (u[1] * ux + u[2] * uy)) / rs, thermal_lower_bound)
    return rs, ux, uy, temp


def chunk_of(first, c):
    k = first + c * HALF
    i = k // NVY
    j = k % NVY
    vx = -vel_max + (i.astype(f32) + 0.5) * DVX
    vy = -vel_max + (j.astype(f32) + 0.5) * DVY
    return vx, vy, j // HALF, j


def coarse(u, band):
    rows, ny = u[0].shape
    rs, ux, uy, temp = physical_variables(u)
    p = rs * temp
    wave = jnp.sqrt(2.0 * temp)
    fx = [u[1], u[1] * ux + p, u[2] * ux, (u[3] + p) * ux]
    fy = [u[2], u[1] * uy, u[2] * uy + p, (u[3] + p) * uy]
    sx = jnp.abs(ux) + wave
    sy = jnp.abs(uy) + wave
    mx = jnp.maximum(sx, pltpu.roll(sx, rows - 1, 0))
    my = jnp.maximum(sy, pltpu.roll(sy, ny - 1, 1))
    out = []
    for c in range(4):
        face_x = 0.5 * (fx[c] + pltpu.roll(fx[c], rows - 1, 0)) - 0.5 * mx * (
            pltpu.roll(u[c], rows - 1, 0) - u[c]
        )
        face_y = 0.5 * (fy[c] + pltpu.roll(fy[c], ny - 1, 1)) - 0.5 * my * (
            pltpu.roll(u[c], ny - 1, 1) - u[c]
        )
        g = u[c] - coarse_ratio * (
            face_x - pltpu.roll(face_x, 1, 0) + (face_y - pltpu.roll(face_y, 1, 1))
        )
        out.append(g[:band])
    return out


def advance_kernel(
    nw, nv,
    f, r, star2, ye, e_phys, corr_out,
    fpad, spad, rfull, bsum, hsum, gout, msg, xmsg, red, redx, xs, es, fr, flux, energy, delta, gs,
    pmsg, pin, vmsg, vrow, vin, vrow_in, chain, chain_rows, phys, xpad, yt, yr,
    load_sem, halo_send, halo_recv, rs_send, rs_recv, ag_send, ag_recv, win_send, win_recv,
    chain_send, chain_recv, ready,
):
    w, v, s = lax.axis_index("win"), lax.axis_index("vel"), lax.axis_index("sp")
    count, nx, ny = f.shape
    chunks = count // HALF
    first = v * count
    other = 1 - s
    pos = (2 * v) // nv
    band = nx // 2
    frame = band + TILE
    full = 4 * band
    main = pl.ds(2 * TILE, nx)
    end = 2 * TILE + nx
    up = pl.ds(2 * TILE + 1 - 2 * pos, nx)
    hb = pl.multiple_of(end - (end - TILE) * pos, TILE)
    edge = pl.ds(hb, TILE)
    edge_up = pl.ds(hb + 1 - 2 * pos, TILE)
    ho = pl.multiple_of(TILE + (end - TILE) * pos, TILE)
    away = pl.ds(ho, TILE)
    away_up = pl.ds(ho + 1 - 2 * pos, TILE)
    tiles = nx // TILE

    base = nv // 2 - 2
    off = v - base
    is_owner = (s == 1) & (off >= 0) & (off < 4)
    b = off // 2
    h = (off + b) % 2
    g = 2 * h + b

    def owner_at(half, k):
        return base + (half if k == 0 else 3 - half)

    def load_f(t):
        rows = pl.ds(pl.multiple_of(t * TILE, TILE), TILE)
        padded = pl.ds(pl.multiple_of((t + 2) * TILE, TILE), TILE)
        return pltpu.make_async_copy(f.at[:, rows], fpad.at[:, padded], load_sem.at[t])

    for t in range(tiles):
        load_f(t).start()
    mine = pl.ds(pl.multiple_of(s * nx, TILE), nx)
    load_r = pltpu.make_async_copy(r, rfull.at[mine], load_sem.at[tiles])
    load_r.start()

    def signal(device):
        pl.semaphore_signal(barrier, inc=1, device_id=device, device_id_type=MESH)

    barrier = pltpu.get_barrier_semaphore()
    signal((w, v, other))
    for o in range(4):

        @pl.when(jnp.logical_not((v == base + o) & (s == 1)))
        def _():
            signal((w, base + o, 1))

    @pl.when(is_owner)
    def _():
        signal((w, v, 0))
        for d in range(1, nv):
            for half in range(2):
                signal((w, lax.rem(v + d, nv), half))

        @pl.when(w + 1 < nw)
        def _():
            for n in range(nv):
                for half in range(2):
                    signal((w + 1, n, half))

    def remote(src, dst, send, recv, device):
        return pltpu.make_async_remote_copy(
            src_ref=src, dst_ref=dst, send_sem=send, recv_sem=recv,
            device_id=device, device_id_type=MESH,
        )

    def settle(ref, sem):
        pltpu.make_async_copy(ref, ref, sem).wait()

    empty = jnp.zeros((TILE, ny), f32)
    for side in range(2):
        for n in range(len(ORDERS)):
            for at in (TILE, end):
                bsum[side, n, pl.ds(at, TILE)] = empty
                hsum[side, n, pl.ds(at, TILE)] = empty

    parity = (first // HALF) % 2
    rounds = (chunks + 1) // 2

    @pl.loop(0, tiles)
    def _(t):
        load_f(t).wait()
        rows = pl.ds(pl.multiple_of(2 * TILE + t * TILE, TILE), TILE)
        for side in range(2):
            acc = {order: jnp.zeros((TILE, ny), f32) for order in ORDERS}
            for n in range(rounds):
                c = (side + parity) % 2 + 2 * n
                weight = 1.0
                if chunks % 2:
                    weight = jnp.where(c < chunks, 1.0, 0.0).astype(f32)
                    c = jnp.minimum(c, chunks - 1)
                vx = chunk_of(first, c)[0]
                sums = [jnp.zeros((TILE, ny), f32)] * 5
                for jj in range(HALF // 2, HALF):
                    tt = (jj + 0.5) * DVY - 0.5 * vel_max
                    high = fpad[c * HALF + jj, rows]
                    low = fpad[c * HALF + HALF - 1 - jj, rows]
                    even, odd = high + low, high - low
                    sums = [
                        sums[0] + even, sums[1] + tt * odd, sums[2] + tt**2 * even,
                        sums[3] + tt**3 * odd, sums[4] + tt**4 * even,
                    ]
                power = weight
                for q in range(5):
                    for m in range(5 - q):
                        term = sums[m] if q == 0 and chunks % 2 == 0 else sums[m] * power
                        acc[m, q] = acc[m, q] + term
                    power = power * vx
            centre = (side - 0.5) * vel_max
            for p, q in ORDERS:
                total = acc[p, q]
                for m in range(p):
                    total = total + (math.comb(p, m) * centre ** (p - m)) * acc[m, q]
                bsum[side, PLACE[p, q], rows] = total

    def components(get):
        return [
            WEIGHT * get(0, 0), WEIGHT * get(0, 1), WEIGHT * get(1, 0),
            (0.5 * WEIGHT) * (get(0, 2) + get(2, 0)),
        ]

    def fill(field, values):
        for c in range(4):
            for k in range(2):
                msg[field, k, pl.ds(c * band, band)] = values[c][k * band : (k + 1) * band]

    def fill_edges(field):
        for c in range(4):
            for k in range(2):
                if field == FIRST:
                    outer = gout[0, c, pl.ds(TILE - 1 if k == 0 else 0, 1)]
                else:
                    outer = jnp.zeros((1, ny), f32)
                msg[field, k, pl.ds(full + c, 1)] = outer
                inner = c * band if k == 0 else (c + 1) * band - 1
                msg[field, k, pl.ds(full + 4 + c, 1)] = msg[field, 1 - k, pl.ds(inner, 1)]

    def to_owner(half, k):
        target = owner_at(half, k)
        return target, (v == target) & (s == 1)

    sizes = {FIRST: full + TILE, START: full + TILE, SECOND: full}

    def scatter(field):
        size = pl.ds(0, sizes[field])
        for k in range(2):
            target, own = to_owner(s, k)

            @pl.when(own)
            def _():
                red[field, v, size] = msg[field, k, size]

            @pl.when(jnp.logical_not(own))
            def _():
                remote(
                    msg.at[field, k, size], red.at[field, v, size],
                    rs_send.at[field], rs_recv.at[field], (w, target, 1),
                ).start()

    ACROSS_ROWS = (pl.ds(0, TILE), pl.ds(TILE, 2 * TILE))

    def scatter_across(part):
        rows = ACROSS_ROWS[part]
        for k in range(2):
            target, own = to_owner(other, k)

            @pl.when(own)
            def _():
                redx[v, rows] = xmsg[k, rows]

            @pl.when(jnp.logical_not(own))
            def _():
                remote(
                    xmsg.at[k, rows], redx.at[v, rows],
                    rs_send.at[3 + part], rs_recv.at[3 + part], (w, target, 1),
                ).start()


    pl.semaphore_wait(barrier, jnp.where(is_owner, 2 * nv + 3, 5) + jnp.where(w > 0, 4, 0))

    @pl.when(w > 0)
    def _():
        for o in range(4):
            pl.semaphore_signal(ready, inc=1, device_id=(w - 1, base + o, 1), device_id_type=MESH)

    load_r.wait()
    source = pl.ds(pl.multiple_of((nx - TILE) * pos, TILE), TILE)
    halo_r = remote(r, rfull.at[mine], halo_send.at[0], halo_recv.at[0], (w, v, other))
    halo_f = remote(f.at[:, source], fpad.at[:, edge], halo_send.at[1], halo_recv.at[1], (w, v, other))
    halo_r.start()
    halo_f.start()

    inv_main = 1.0 / (1.0 + rfull[mine])
    along = fine_ratio * (2 * pos - 1).astype(f32)
    ACROSS = ((-fine_ratio, ny - 1), (fine_ratio, 1))

    def moved(table, side, p, q, rows, rows_up):
        across, shift = ACROSS[side]
        bx = table[side, PLACE[p, q + 1], rows]
        by = table[side, PLACE[p + 1, q], rows]
        return (
            table[side, PLACE[p, q], rows]
            + along * (table[side, PLACE[p, q + 1], rows_up] - bx)
            + across * (pltpu.roll(by, shift, 1) - by)
        )

    star_main, star_away = {}, {}

    def one_step(side, p, q):
        star = moved(bsum, side, p, q, main, up)
        beyond = moved(bsum, side, p, q, away, away_up)
        hsum[side, PLACE[p, q], main] = star * inv_main
        hsum[side, PLACE[p, q], away] = beyond
        return star, beyond

    for order in MAIN:
        parts = [one_step(side, *order) for side in range(2)]
        star_main[order] = parts[0][0] + parts[1][0]
        star_away[order] = parts[0][1] + parts[1][1]
    fill(FIRST, components(lambda p, q: star_main[p, q]))
    for c, value in enumerate(components(lambda p, q: star_away[p, q])):
        gout[0, c] = value
    fill_edges(FIRST)
    for k in range(2):
        last = band - 1 if k == 0 else 0
        for c in range(4):
            xmsg[k, pl.ds(c, 1)] = msg[FIRST, 1 - k, pl.ds(c * band + last, 1)]
            xmsg[k, pl.ds(4 + c, 1)] = gout[0, c, pl.ds(0 if k == 0 else TILE - 1, 1)]
    scatter_across(0)
    scatter(FIRST)
    for p, q in ORDERS:
        if p + q < 4 and (p, q) not in MAIN:
            for side in range(2):
                one_step(side, p, q)
    again = {o: moved(hsum, 0, *o, main, up) + moved(hsum, 1, *o, main, up) for o in MAIN}
    fill(SECOND, components(lambda p, q: again[p, q]))
    scatter(SECOND)

    fill(START, components(lambda p, q: bsum[0, PLACE[p, q], main] + bsum[1, PLACE[p, q], main]))
    fill_edges(START)
    halo_r.wait()
    theirs = other * nx
    inv_away = 1.0 / (1.0 + rfull[pl.ds(theirs + (nx - 1) * (1 - pos), 1)])
    inv_edge = 1.0 / (1.0 + rfull[pl.ds(pl.multiple_of(theirs + (nx - TILE) * pos, TILE), TILE)])
    for side in range(2):
        for p, q in ORDERS:
            if p + q < 4:
                hsum[side, PLACE[p, q], away] = hsum[side, PLACE[p, q], away] * inv_away
    again = {o: moved(hsum, 0, *o, away, away_up) + moved(hsum, 1, *o, away, away_up) for o in MAIN}
    for c, value in enumerate(components(lambda p, q: again[p, q])):
        gout[1, c] = value
    for k in range(2):
        last = band - 1 if k == 0 else 0
        near, far = (0, 1) if k == 0 else (TILE - 1, TILE - 2)
        for c in range(4):
            xmsg[k, pl.ds(8 + c, 1)] = gout[1, c, pl.ds(near, 1)]
            xmsg[k, pl.ds(12 + c, 1)] = gout[1, c, pl.ds(far, 1)]
            xmsg[k, pl.ds(16 + c, 1)] = msg[START, 1 - k, pl.ds(c * band + last, 1)]
            xmsg[k, pl.ds(20 + c, 1)] = jnp.zeros((1, ny), f32)
    scatter_across(1)
    halo_f.wait()

    def first_transport(c):
        vx, vy0, half, _j = chunk_of(first, c)
        shift = ny - 1 - (ny - 2) * half
        ca = fine_ratio * jnp.abs(vx)
        for jj in range(HALF):
            k = c * HALF + jj
            cb = fine_ratio * jnp.abs(vy0 + jj * DVY)
            cc = 1.0 - ca - cb
            x = fpad[k, main]
            spad[k, main] = (cc * x + ca * fpad[k, up] + cb * pltpu.roll(x, shift, 1)) * inv_main
            x = fpad[k, edge]
            spad[k, edge] = (cc * x + ca * fpad[k, edge_up] + cb * pltpu.roll(x, shift, 1)) * inv_edge

    pl.loop(0, chunks // 4)(first_transport)
    scatter(START)
    pl.loop(chunks // 4, chunks)(first_transport)

    row8 = lax.broadcasted_iota(jnp.int32, (TILE, ny), 0)
    row_band = lax.broadcasted_iota(jnp.int32, (band, ny), 0)
    brow = (band - 1) * b
    brow2 = 1 + (band - 3) * b

    def received(field):
        size = pl.ds(0, sizes[field])

        @pl.when(h == 1)
        def _():
            settle(red.at[field, pl.ds(0, nv - 1), size], rs_recv.at[field])

        @pl.when(h == 0)
        def _():
            settle(red.at[field, :, size], rs_recv.at[field])

    def summed(field, rows):
        total = red[field, 0, rows]
        for n in range(1, nv):
            total = total + red[field, n, rows]
        return total

    def comp(c):
        return pl.ds(c * band, band)

    def framed(value, outer, inner):
        above = jnp.where(b == 0, outer, inner)
        below = jnp.where(b == 0, inner, outer)
        return jnp.concatenate([value, jnp.where(row8 == TILE - 1, above, below)], axis=0)

    def placed(row, at):
        return jnp.where(row_band == at, row, 0.0)

    def share(n, size, targets):
        rows = pl.ds(0, size)
        for d in targets:

            def send(d=d):
                remote(
                    pmsg.at[n, rows], pin.at[n, b, rows], ag_send.at[n], ag_recv.at[n], (w, d, h)
                ).start()

            if base <= d < base + 4:
                own = (h == 1) & (v == d)
                pl.when(jnp.logical_not(own))(send)

                @pl.when(own)
                def _():
                    pin[n, b, rows] = pmsg[n, rows]
            else:
                send()

    def place(n):
        half, k = n // 2, n % 2
        return base + half + k * (3 - 2 * half)

    def along_chain():
        after, before = lax.rem(g + 1, 4), lax.rem(g + 3, 4)
        return [
            remote(vmsg, chain, chain_send.at[0], chain_recv.at[0], (w + 1, v, 1)),
            remote(vrow.at[0], chain_rows.at[1], chain_send.at[1], chain_recv.at[1], (w + 1, place(before), 1)),
            remote(vrow.at[1], chain_rows.at[0], chain_send.at[2], chain_recv.at[2], (w + 1, place(after), 1)),
        ]

    def hand_to(targets):
        for d in targets:
            remote(vrow.at[b], vrow_in.at[b], win_send.at[0], win_recv.at[0], (w + 1, d, 1 - h)).start()
            remote(vmsg, vin.at[b], win_send.at[1], win_recv.at[1], (w + 1, d, h)).start()

    def hand_on(values, targets):
        for c in range(4):
            vmsg[comp(c)] = values[c]
            for row, value in ((0, values[c][:1]), (1, values[c][-1:])):
                vrow[row, pl.ds(c, 1)] = value
                vrow[row, pl.ds(4 + c, 1)] = value
        pl.semaphore_wait(ready, 2 * nv)

        @pl.when(w + 2 < nw)
        def _():
            for copy in along_chain():
                copy.start()

        hand_to(targets)

    @pl.when(is_owner)
    def _():
        def received_across(part):
            rows = ACROSS_ROWS[part]

            @pl.when(h == 1)
            def _():
                settle(redx.at[:, rows], rs_recv.at[3 + part])

            @pl.when(h == 0)
            def _():
                settle(redx.at[pl.ds(0, nv - 1), rows], rs_recv.at[3 + part])

            across = redx[0, rows]
            for n in range(1, nv):
                across = across + redx[n, rows]
            xs[rows] = across

        received(FIRST)
        received_across(0)

        def x_row(n):
            return xs[pl.ds(n, 1)]

        def assembled(field, at):
            es[...] = summed(field, pl.ds(full, TILE))
            out = []
            for c in range(4):
                value = summed(field, comp(c))
                if field == FIRST:
                    value = value + placed(x_row(4 + c), brow)
                out.append(framed(value, es[pl.ds(c, 1)] + x_row(at + c), es[pl.ds(4 + c, 1)]))
            return out

        rs, ux, uy, temp = physical_variables(assembled(FIRST, 0))
        rows_all = 2 * nx
        mid = pl.ds(pl.multiple_of(g * band, TILE), band)
        above = rfull[pl.ds(lax.rem(g * band + rows_all - 1, rows_all), 1)]
        below = rfull[pl.ds(lax.rem(g * band + band, rows_all), 1)]
        rate = jnp.concatenate([rfull[mid], jnp.where(row8 == TILE - 1, above, below)], axis=0)
        fr[0] = ux
        fr[1] = uy
        fr[2] = -0.5 / temp
        fr[3] = rs / temp * (rate / (1.0 + rate))
        for n in range(4):
            pmsg[0, comp(n)] = fr[n, pl.ds(0, band)]
            outer = fr[n, pl.ds(band + (TILE - 1) * (1 - b), 1)]
            pmsg[0, pl.ds(full + n, 1)] = outer
            pmsg[0, pl.ds(full + 4 + n, 1)] = outer
        share(0, full + TILE, range(nv))

        @pl.loop(0, frame // TILE)
        def _(t):
            rows = pl.ds(pl.multiple_of(t * TILE, TILE), TILE)
            ux, uy, scale, amp = [fr[n, rows] for n in range(4)]

            def half_sums(speeds, drift):
                weights = []
                for speed in speeds:
                    d = speed - drift
                    weights.append(jnp.exp(d * d * scale))
                sides = []
                half = len(speeds) // 2
                for at, c in ((half, 0.5 * vel_max), (0, -0.5 * vel_max)):
                    m = [empty] * 4
                    for n in range(half // 2, half):
                        t = speeds[at + n] - c
                        high, low = weights[at + n], weights[at + half - 1 - n]
                        even, odd = high + low, high - low
                        m = [m[0] + even, m[1] + t * odd, m[2] + t**2 * even, m[3] + t**3 * odd]
                    sides.append([
                        m[0],
                        m[1] + c * m[0],
                        m[2] + (2 * c) * m[1] + c**2 * m[0],
                        m[3] + (3 * c) * m[2] + (3 * c**2) * m[1] + c**3 * m[0],
                    ])
                return sides

            xp, xm = half_sums([-vel_max + (i + 0.5) * DVX for i in range(NVX)], ux)
            yp, ym = half_sums([-vel_max + (j + 0.5) * DVY for j in range(NVY)], uy)
            xs_ = [x + y for x, y in zip(xp, xm)]
            ys_ = [x + y for x, y in zip(yp, ym)]
            amp = WEIGHT * amp

            def store(n, coef, x, y):
                x = [coef * amp * t for t in x]
                flux[n, rows] = x[0] * y[0]
                flux[n + 1, rows] = x[1] * y[0]
                flux[n + 2, rows] = x[0] * y[1]
                flux[n + 3, rows] = 0.5 * (x[2] * y[0] + x[0] * y[2])

            store(0, 1.0, xs_, ys_)
            store(4, fine_ratio, xp[1:], ys_)
            store(8, -fine_ratio, xm[1:], ys_)
            store(12, fine_ratio, xs_, yp[1:])
            store(16, -fine_ratio, xs_, ym[1:])

        received(SECOND)
        received_across(1)
        inner = pl.ds(0, band)
        for c in range(4):
            to_y, from_y = flux[12 + c, inner], flux[16 + c, inner]
            energy[c] = (
                summed(SECOND, comp(c)) + placed(x_row(8 + c), brow) + placed(x_row(12 + c), brow2)
            ) + (
                flux[c, inner] - flux[4 + c, inner] - flux[8 + c, inner] - to_y - from_y
                + pltpu.roll(flux[4 + c], 1, 0)[:band] + pltpu.roll(flux[8 + c], frame - 1, 0)[:band]
                + pltpu.roll(to_y, 1, 1) + pltpu.roll(from_y, ny - 1, 1)
            )
        rs, ux, uy, temp = physical_variables(energy)
        pmsg[1, comp(0)] = ux
        pmsg[1, comp(1)] = uy
        pmsg[1, comp(2)] = -0.5 / temp
        pmsg[1, comp(3)] = rs / temp * (1.0 / (1.0 + rfull[mid]))
        share(1, full, range(nv))

        received(START)
        stepped = coarse(assembled(START, 16), band)
        for c in range(4):
            gs[c] = stepped[c]
            delta[c] = energy[c] - stepped[c]

        for c in range(4):
            corrected = gs[c] + delta[c]
            energy[c] = corrected
            pmsg[2, comp(c)] = jnp.where(w == 0, corrected, delta[c])
        share(2, full, range(AHEAD))
        if nw > 1:

            @pl.when(w == 0)
            def _():
                hand_on([energy[c] for c in range(4)], range(EARLY))

        share(2, full, range(AHEAD, nv))
        if nw > 1:

            @pl.when(w == 0)
            def _():
                hand_to(range(EARLY, nv))


    @pl.loop(0, chunks)
    def _(c):
        vx, vy0, half, _j = chunk_of(first, c)
        shift = ny - 1 - (ny - 2) * half
        ca = fine_ratio * jnp.abs(vx)
        for jj in range(HALF):
            k = c * HALF + jj
            cb = fine_ratio * jnp.abs(vy0 + jj * DVY)
            x = spad[k, main]
            star = (1.0 - ca - cb) * x + ca * spad[k, up] + cb * pltpu.roll(x, shift, 1)
            star2[k] = star * inv_main

    if nw > 2:

        @pl.when(is_owner & (w > 0) & (w + 1 < nw))
        def _():
            settle(chain, chain_recv.at[0])
            settle(chain_rows.at[1], chain_recv.at[1])
            settle(chain_rows.at[0], chain_recv.at[2])
            u = [
                jnp.concatenate(
                    [
                        chain[comp(c)],
                        jnp.where(
                            row8 == TILE - 1, chain_rows[0, pl.ds(c, 1)], chain_rows[1, pl.ds(c, 1)]
                        ),
                    ],
                    axis=0,
                )
                for c in range(4)
            ]
            stepped = coarse(u, band)
            hand_on([stepped[c] + delta[c] for c in range(4)], range(nv))

    def shared(n, size):
        rows = pl.ds(0, size)

        @pl.when(is_owner & (h == 1))
        def _():
            settle(pin.at[n, 0, rows], ag_recv.at[n])

        @pl.when(jnp.logical_not(is_owner & (h == 1)))
        def _():
            settle(pin.at[n, :, rows], ag_recv.at[n])

    shared(0, full + TILE)
    for n in range(4):
        for k in range(2):
            phys[n, pl.ds(2 * TILE + k * band, band)] = pin[0, k, comp(n)]
        phys[n, edge] = jnp.broadcast_to(pin[0, 1 - pos, pl.ds(full + n, 1)], (TILE, ny))
    for rows in (main, edge):
        drift, scale = phys[1, rows], phys[2, rows]
        for j in range(NVY):
            d = (-vel_max + (j + 0.5) * DVY) - drift
            e = jnp.exp(d * d * scale)
            yt[j, rows] = e
            if rows is main:
                yr[j] = pltpu.roll(e, ny - 1 if j < HALF else 1, 1)

    @pl.loop(0, chunks)
    def _(c):
        vx, vy0, half, j0 = chunk_of(first, c)
        shift = ny - 1 - (ny - 2) * half
        ca = fine_ratio * jnp.abs(vx)
        for rows in (main, edge):
            d = vx - phys[0, rows]
            xpad[rows] = phys[3, rows] * jnp.exp(d * d * phys[2, rows])
        x = xpad[main]
        here = inv_main * x
        behind = (ca * inv_main) * xpad[up]
        beside = inv_main * pltpu.roll(x, shift, 1)
        for jj in range(HALF):
            k = c * HALF + jj
            cb = fine_ratio * jnp.abs(vy0 + jj * DVY)
            star2[k] = (
                star2[k] + ((1.0 - ca - cb) * here) * yt[j0 + jj, main] + behind * yt[j0 + jj, up]
                + (cb * beside) * yr[j0 + jj]
            )

    shared(1, full)
    for k in range(2):
        rows = pl.ds(k * band, band)
        for n in range(4):
            e_phys[n, rows] = pin[1, k, comp(n)]
    drift, scale = e_phys[1], e_phys[2]
    for j in range(NVY):
        d = (-vel_max + (j + 0.5) * DVY) - drift
        ye[j] = jnp.exp(d * d * scale)
    shared(2, full)
    for k in range(2):
        for n in range(4):
            corr_out[n, pl.ds(k * band, band)] = pin[2, k, comp(n)]
    if nw > 1:

        @pl.when(w > 0)
        def _():
            settle(vrow_in, win_recv.at[0])
            settle(vin, win_recv.at[1])
            u = [
                jnp.concatenate(
                    [
                        vin[0, comp(c)], vin[1, comp(c)],
                        jnp.where(row8 == TILE - 1, vrow_in[1, pl.ds(c, 1)], vrow_in[0, pl.ds(c, 1)]),
                    ],
                    axis=0,
                )
                for c in range(4)
            ]
            stepped = coarse(u, nx)
            for c in range(4):
                corr_out[c] = stepped[c] + corr_out[c]

    for field in range(3):
        size = pl.ds(0, sizes[field])
        for k in range(2):
            own = to_owner(s, k)[1]

            @pl.when(jnp.logical_not(own))
            def _():
                settle(msg.at[field, k, size], rs_send.at[field])

    for k in range(2):
        own = to_owner(other, k)[1]

        @pl.when(jnp.logical_not(own))
        def _():
            for part in range(2):
                settle(xmsg.at[k, ACROSS_ROWS[part]], rs_send.at[3 + part])

    @pl.when(is_owner)
    def _():
        for n, size in ((0, full + TILE), (1, full), (2, full)):
            rows = pl.ds(0, size)
            for _ in range(nv - 1):
                settle(pmsg.at[n, rows], ag_send.at[n])

            @pl.when(h == 0)
            def _():
                settle(pmsg.at[n, rows], ag_send.at[n])

        if nw > 1:

            @pl.when(w + 1 < nw)
            def _():
                for _ in range(nv):
                    settle(vrow.at[b], win_send.at[0])
                    settle(vmsg, win_send.at[1])

            @pl.when(w + 2 < nw)
            def _():
                settle(vmsg, chain_send.at[0])
                settle(vrow.at[0], chain_send.at[1])
                settle(vrow.at[1], chain_send.at[2])


def lift_kernel(parts, star2, ye, e_phys, corr, lifted, corrected, yc, out, save_sem):
    count = star2.shape[0]
    first = lax.axis_index("vel") * count
    corrected[...] = corr[...]
    rs, uc, uy, temp = physical_variables(corr)
    sc = -0.5 / temp
    mc = rs / temp
    for j in range(NVY):
        d = (-vel_max + (j + 0.5) * DVY) - uy
        yc[j] = jnp.exp(d * d * sc)
    chunks = count // HALF
    per = chunks // parts

    def save(n):
        rows = pl.ds(n * per * HALF, per * HALF)
        return pltpu.make_async_copy(out.at[rows], lifted.at[rows], save_sem.at[n])

    for n in range(parts):

        @pl.loop(n * per, (n + 1) * per)
        def _(c):
            vx, _vy, _half, j0 = chunk_of(first, c)
            dc = vx - uc
            xc = mc * jnp.exp(dc * dc * sc)
            de = vx - e_phys[0]
            xe = e_phys[3] * jnp.exp(de * de * e_phys[2])
            for jj in range(HALF):
                k = c * HALF + jj
                out[k] = star2[k] + (xc * yc[j0 + jj] - xe * ye[j0 + jj])

        save(n).start()
    for n in range(parts):
        save(n).wait()


def per_device(nw, nv, f_start, relax_rate):
    field = f_start[0]
    count, nx, ny = field.shape
    band = nx // 2
    frame = band + TILE
    full = 4 * band
    pad = nx + 4 * TILE
    vmem = pltpu.VMEM
    dma = pltpu.SemaphoreType.DMA
    small = jax.ShapeDtypeStruct((4, nx, ny), f32)
    speeds = jax.ShapeDtypeStruct((NVY, nx, ny), f32)
    in_vmem = pl.BlockSpec(memory_space=pltpu.VMEM)
    in_hbm = pl.BlockSpec(memory_space=pltpu.HBM)
    field = pltpu.with_memory_space_constraint(field, pltpu.HBM)
    star2, ye, e_phys, corr = pl.pallas_call(
        functools.partial(advance_kernel, nw, nv),
        out_shape=(jax.ShapeDtypeStruct((count, nx, ny), f32), speeds, small, small),
        in_specs=[in_hbm, in_hbm],
        out_specs=(in_vmem,) * 4,
        scratch_shapes=[
            vmem((count, pad, ny), f32),
            vmem((count, pad, ny), f32),
            vmem((2 * nx, ny), f32),
            vmem((2, len(ORDERS), pad, ny), f32),
            vmem((2, len(ORDERS), pad, ny), f32),
            vmem((2, 4, TILE, ny), f32),
            vmem((3, 2, full + TILE, ny), f32),
            vmem((2, 3 * TILE, ny), f32),
            vmem((3, nv, full + TILE, ny), f32),
            vmem((nv, 3 * TILE, ny), f32),
            vmem((3 * TILE, ny), f32),
            vmem((TILE, ny), f32),
            vmem((4, frame, ny), f32),
            vmem((20, frame, ny), f32),
            vmem((4, band, ny), f32),
            vmem((4, band, ny), f32),
            vmem((4, band, ny), f32),
            vmem((3, full + TILE, ny), f32),
            vmem((3, 2, full + TILE, ny), f32),
            vmem((full, ny), f32),
            vmem((2, TILE, ny), f32),
            vmem((2, full, ny), f32),
            vmem((2, TILE, ny), f32),
            vmem((full, ny), f32),
            vmem((2, TILE, ny), f32),
            vmem((4, pad, ny), f32),
            vmem((pad, ny), f32),
            vmem((NVY, pad, ny), f32),
            vmem((NVY, nx, ny), f32),
            dma((1 + nx // TILE,)), dma((2,)), dma((2,)), dma((5,)), dma((5,)), dma((3,)), dma((3,)),
            dma((2,)), dma((2,)), dma((3,)), dma((3,)), pltpu.SemaphoreType.REGULAR,
        ],
        compiler_params=pltpu.CompilerParams(
            collective_id=0, has_side_effects=True, vmem_limit_bytes=40 << 20
        ),
        name="advance",
    )(field, pltpu.with_memory_space_constraint(relax_rate, pltpu.HBM))

    chunks = count // HALF
    parts = next(n for n in (12, 6, 4, 3, 2, 1) if chunks % n == 0)
    lifted, corrected = pl.pallas_call(
        functools.partial(lift_kernel, parts),
        out_shape=(jax.ShapeDtypeStruct((count, nx, ny), f32), small),
        in_specs=[in_vmem] * 4,
        out_specs=(in_hbm, in_vmem),
        scratch_shapes=[
            vmem((NVY, nx, ny), f32), vmem((count, nx, ny), f32), dma((parts,)),
        ],
        compiler_params=pltpu.CompilerParams(vmem_limit_bytes=16 << 20),
        name="lift",
    )(star2, ye, e_phys, corr)
    return corrected[None], lifted[None]


def solution(mesh):
    return jax.shard_map(
        functools.partial(per_device, mesh.shape["win"], mesh.shape["vel"]),
        mesh=mesh,
        in_specs=(P("win", "vel", "sp", None), P("sp", None)),
        out_specs=(P("win", None, "sp", None), P("win", "vel", "sp", None)),
        check_vma=False,
    )
```
